32 devices in a mesh: lat: 16 (over z, y, x), lev: 2 (over core).
Axes of the slice: x: 2, y: 2, z: 4, core: 2. Of those that a mesh axis runs over, the one named last changes fastest.
Arguments:
- grid: bfloat16 [96, 2, 48, 400], P('lat', None, 'lev'), may hold values from -6 to 6
- point_counts: int32 [96], P('lat'), may hold values from 16 to 400, as said below
- waves: int32 [96], replicated, may hold values from 0 to 95, each once
- legendre: bfloat16 [96, 96, 96], P('lat'), may hold values from -0.625 to 0.625
- weights: float32 [96], P('lat'), may hold values from 0.5 to 2
- stiffness: float32 [48], replicated, may hold values from 1e-06 to 0.0001
Outputs:
- grid_out: bfloat16 [96, 2, 48, 400], P('lat', None, 'lev')
The draws below stay inside these ranges and needn't reach their ends.
Inputs may be any that keep to these rules, and one draw needn't show every extreme that they name: point_counts[j] is 4 j + 16 or 4 j + 20 (j counted from 0 at the pole), and the last pair has exactly 400 points. `waves`: each wavenumber from 0 to 95 appears once.
All inputs are finite; a program needn't handle non-finite values.
Results may differ from the reference program's by a relative error of at most 0.015.
Values may be sent and summed in bfloat16 or wider, within the bound.
No kernel may reach another device: no remote copies, remote signals or barrier semaphores. Data moves between devices by JAX's collectives and lax.ppermute only.
A program may use at most 128 MiB of HBM per device.

```python
import math
import jax
import jax.numpy as jnp
from jax import lax

M = 96
H = 96
NLON_MAX = 400
F = 48


def draw_point_counts(key, part):
    latitude = jnp.arange(H, dtype=jnp.int32)
    extra = jax.random.randint(key, (H,), 0, 2).astype(jnp.int32)
    counts = 4 * latitude + 16 + 4 * extra
    return jnp.where(latitude == H - 1, 4 * H + 16, counts).astype(jnp.int32)


def level_of(rng, shape, shards, low, largest):
    gain, own = 1.0, jax.random.fold_in(rng, 6)
    for axis_at, blocks in shards:
        draws = jnp.exp(jax.random.uniform(jax.random.fold_in(own, axis_at), (blocks,), jnp.float32, low / len(shards), largest / len(shards)))
        gain = gain * jnp.repeat(draws, shape[axis_at] // blocks).reshape([-1 if axis == axis_at else 1 for axis in range(len(shape))])
    return gain


def scatter_about(stream_key, shape, deviation, limit, cuts=(), kind=jnp.bfloat16):
    gain = level_of(stream_key, shape, cuts, -0.22, 0.18) if cuts else 1.0
    result = jax.random.normal(stream_key, shape, jnp.float32) * deviation * gain
    return jnp.minimum(jnp.maximum(result, -limit), limit).astype(kind)


def setup_inputs(seed: int = 0) -> dict:
    splits = jax.random.split(jax.random.key(seed), 7)
    grid = scatter_about(splits[0], (H, 2, F, NLON_MAX), 1.0, 6.0, ((0, 16), (2, 2)))
    point_counts = draw_point_counts(jax.random.fold_in(splits[6], 71), 0)
    waves = jax.random.permutation(splits[2], M).astype(jnp.int32)
    legendre = scatter_about(splits[3], (M, H, M), H ** -0.5, 0.625, ((0, 16),))
    weights = jnp.clip(jnp.exp(math.log(2.0) - 1.3862944 * jax.random.uniform(splits[4], (H,), jnp.float32) ** level_of(splits[4], (H,), ((0, 16),), -0.2, 0.2)), 0.5, 2.0)
    stiffness = jnp.clip(jnp.exp(jax.random.uniform(splits[5], (F,), jnp.float32, math.log(9.999999974752427e-07), math.log(0.0001))), 9.999999974752427e-07, 0.0001)
    return {"grid": grid, "point_counts": point_counts, "waves": waves, "legendre": legendre, "weights": weights, "stiffness": stiffness}


TWO_PI = 2.0 * math.pi
EXACT = lax.Precision.HIGHEST


def reference(grid, point_counts, waves, legendre, weights, stiffness):
    positions = jnp.arange(NLON_MAX, dtype=jnp.int32)
    degree_shift = jnp.arange(M, dtype=jnp.int32)
    parity = (1 - 2 * (degree_shift % 2)).astype(jnp.float32)

    def harmonics(count):
        phase = (positions[:, None] * waves[None, :]) % count
        angle = phase.astype(jnp.float32) * (TWO_PI / count.astype(jnp.float32))
        inside = (positions < count)[:, None]
        return jnp.where(inside, jnp.cos(angle), 0.0), jnp.where(inside, jnp.sin(angle), 0.0)

    def analyse(pieces):
        latitude, count, weight = pieces
        cosine, sine = harmonics(count)
        values = latitude.astype(jnp.float32)
        real = jnp.einsum("hfk,km->hfm", values, cosine, precision=EXACT)
        imag = -jnp.einsum("hfk,km->hfm", values, sine, precision=EXACT)
        factor = jnp.where(2 * waves < count, weight / count.astype(jnp.float32), 0.0)
        return jnp.stack([real * factor, imag * factor], axis=2).astype(jnp.bfloat16)

    coefficients = lax.map(analyse, (grid, point_counts, weights))
    by_slot = jnp.moveaxis(coefficients, 4, 0)

    def transform(pieces):
        block_data, basis, wavenumber = pieces
        basis_wide = basis.astype(jnp.float32)
        spectra = jnp.einsum("jhfr,jl->hfrl", block_data.astype(jnp.float32), basis_wide, precision=EXACT)
        combined = spectra[0] + parity * spectra[1]
        degrees = (wavenumber + degree_shift).astype(jnp.float32)
        inside_band = degree_shift < M - wavenumber
        factor = 1.0 / (1.0 + stiffness[:, None] * degrees[None, :] * (degrees[None, :] + 1.0))
        damping = jnp.where(inside_band[None, :], factor, 0.0)
        rounded = lax.optimization_barrier((combined * damping[:, None, :]).astype(jnp.bfloat16))
        scaled = rounded.astype(jnp.float32)
        operand = jnp.stack([scaled, scaled * parity], axis=0)
        returned = jnp.einsum("hfrl,jl->jhfr", operand, basis_wide, precision=EXACT)
        return returned.astype(jnp.bfloat16)

    synthesised = lax.map(transform, (by_slot, legendre, waves))
    fourier = jnp.moveaxis(synthesised, 0, 4)

    def synthesise(pieces):
        block_data, count = pieces
        cosine, sine = harmonics(count)
        factor = jnp.where(2 * waves < count, jnp.where(waves == 0, 1.0, 2.0), 0.0)
        real = block_data[:, :, 0, :].astype(jnp.float32) * factor
        imag = block_data[:, :, 1, :].astype(jnp.float32) * factor
        values = jnp.einsum("hfm,km->hfk", real, cosine, precision=EXACT) - jnp.einsum("hfm,km->hfk", imag, sine, precision=EXACT)
        return values.astype(jnp.bfloat16)

    return lax.map(synthesise, (fourier, point_counts))
```

```python
import functools
import math

import jax
import jax.numpy as jnp
from jax import lax
from jax.experimental import pallas as pl
from jax.experimental.pallas import tpu as pltpu
from jax.sharding import PartitionSpec as P

TWO_PI = 2.0 * math.pi
FINE_STEPS = 32
LANES = 128
ROWS = 8
TABLE_BUDGET = 16 << 20

COS_TURN = (
    0.9999999998781397, -19.739208740145937, 64.9393888386778, -85.45665201444898,
    60.24205245141228, -26.404165331517056, 7.79855301354287, -1.4511773940976733,
)
SIN_TURN = (
    6.2831853022485955, -41.341700317335295, 81.60512671223316, -76.70292598092092,
    42.02516399730493, -14.896874459689428, 3.233831551278599,
)


def polynomial(coefficients, u):
    total = coefficients[-1] * u + coefficients[-2]
    for value in coefficients[-3::-1]:
        total = total * u + value
    return total


def cos_minus_sin(steps, count, inverse):
    reduced = steps - jnp.floor(steps * inverse + 0.5) * count
    turn = reduced * inverse
    square = turn * turn
    return polynomial(COS_TURN, square), -turn * polynomial(SIN_TURN, square)


def wave_column(waves_ref, held, slots):
    width = waves_ref.shape[1]
    row = lax.broadcasted_iota(jnp.int32, (slots, width), 0)
    lane = lax.broadcasted_iota(jnp.int32, (slots, width), 1)
    place = row & (ROWS - 1)
    chosen = ((row >> 3) * held + place == lane) & (place < held)
    waves = jnp.broadcast_to(waves_ref[...].astype(jnp.float32), (slots, width))
    column = jnp.sum(jnp.where(chosen, waves, 0.0), axis=1, keepdims=True)
    filled = (lax.broadcasted_iota(jnp.int32, (slots, 1), 0) & (ROWS - 1)) < held
    return column, filled


def analysis_kernel(held, counts, weights, waves_ref, grid_hbm, coef_ref, table_ref, values, arrived):
    owners, pairs, _, _ = coef_ref.shape
    slots = owners * ROWS
    points = grid_hbm.shape[1]
    rows = grid_hbm.shape[0] // pairs
    fetch = pltpu.make_async_copy(grid_hbm, values, arrived)
    fetch.start()
    wave, filled = wave_column(waves_ref, held, slots)
    lane = lax.broadcasted_iota(jnp.int32, (1, LANES), 1)
    lane_count = jnp.ones((1, LANES), jnp.float32)
    for j in range(pairs):
        lane_count = jnp.where(lane == j, counts[j].astype(jnp.float32), lane_count)
    lane_inverse = 1.0 / lane_count
    turn_cos, turn_sin = cos_minus_sin(
        jnp.broadcast_to(wave * float(LANES), (slots, LANES)), lane_count, lane_inverse
    )
    steps = wave * lane.astype(jnp.float32)
    blocks = table_ref.shape[2] // LANES
    for j in range(pairs):
        count = jnp.full((1, LANES), counts[j].astype(jnp.float32))
        inverse = 1.0 / count
        cosine, sine = cos_minus_sin(steps, count, inverse)
        kept = filled & (2.0 * wave < count[:, :1])
        cosine = jnp.where(kept, cosine, 0.0)
        sine = jnp.where(kept, sine, 0.0)
        block_cos = turn_cos[:, j : j + 1]
        block_sin = turn_sin[:, j : j + 1]
        for block in range(blocks):
            if block > 0:
                cosine, sine = (
                    cosine * block_cos - sine * block_sin,
                    sine * block_cos + cosine * block_sin,
                )
            at = pl.ds(block * LANES, LANES)
            table_ref[j, :slots, at] = cosine.astype(jnp.bfloat16)
            table_ref[j, slots:, at] = sine.astype(jnp.bfloat16)
    fetch.wait()
    position = lax.broadcasted_iota(jnp.int32, (1, points), 1)
    for j in range(pairs):
        inside = jnp.where(position < counts[j], 1.0, 0.0).astype(jnp.bfloat16)
        latitude = values[j * rows : (j + 1) * rows, :] * inside
        product = lax.dot_general(
            table_ref[j, :, :points],
            latitude,
            (((1,), (1,)), ((), ())),
            preferred_element_type=jnp.float32,
        )
        scale = jnp.full((1, 1), weights[j]) / jnp.full((1, 1), counts[j].astype(jnp.float32))
        product = product * scale
        packed = jnp.concatenate(
            [
                product[:slots],
                product[slots:],
                jnp.zeros((slots, LANES - 2 * rows), jnp.float32),
            ],
            axis=1,
        )
        coef_ref[:, j] = packed.reshape(owners, ROWS, LANES).astype(jnp.bfloat16)


def legendre_kernel(held, fields, waves, stiffness_ref, basis_ref, recv_ref, send_ref, fan_in, fan_out):
    owners, pairs, _, _ = recv_ref.shape
    latitudes = owners * pairs
    width = basis_ref.shape[2]
    first = lax.axis_index("lat") * held
    fan_in[...] = recv_ref[...].astype(jnp.float32).reshape(latitudes * ROWS, LANES)
    lane = lax.broadcasted_iota(jnp.int32, (1, LANES), 1)
    own = pltpu.roll(stiffness_ref[...], (LANES - lax.axis_index("lev") * fields) % LANES, 1)
    own = jnp.where(lane < fields, own, 0.0)
    stiffness = own
    for copy in range(1, 4):
        stiffness = stiffness + pltpu.roll(own, copy * fields, 1)
    south = ((lane >= fields) & (lane < 2 * fields)) | (lane >= 3 * fields)
    offset = lax.broadcasted_iota(jnp.int32, (width, 1), 0)
    parity = jnp.where((offset & 1) == 0, 1.0, -1.0)
    for c in range(held):
        wave = waves[first + c]
        degree = (offset + wave).astype(jnp.float32)
        factor = 1.0 / (1.0 + stiffness * degree * (degree + 1.0))
        damping = jnp.where(offset < width - wave, factor, 0.0)
        block = fan_in[pl.ds(c, latitudes, stride=ROWS), :].astype(jnp.bfloat16)
        basis = basis_ref[c]
        spectra = lax.dot_general(
            basis, block, (((0,), (0,)), ((), ())), preferred_element_type=jnp.float32
        )
        other = jnp.where(
            south, pltpu.roll(spectra, fields, 1), pltpu.roll(spectra, LANES - fields, 1)
        )
        scaled = ((spectra + parity * other) * damping).astype(jnp.bfloat16)
        returned = jnp.dot(basis, scaled, preferred_element_type=jnp.float32)
        returned = returned * jnp.where(wave == 0, 1.0, 2.0)
        fan_out[pl.ds(c, latitudes, stride=ROWS), :] = returned
    for c in range(held, ROWS):
        fan_out[pl.ds(c, latitudes, stride=ROWS), :] = jnp.zeros((latitudes, LANES), jnp.float32)
    send_ref[...] = fan_out[...].reshape(owners, pairs, ROWS, LANES).astype(jnp.bfloat16)


def synthesis_kernel(counts, recv_ref, table_ref, grid_hbm, values, left):
    owners, pairs, _, _ = recv_ref.shape
    slots = owners * ROWS
    points = grid_hbm.shape[1]
    rows = grid_hbm.shape[0] // pairs
    position = lax.broadcasted_iota(jnp.int32, (1, points), 1)
    copies = []
    for j in range(pairs):
        block = recv_ref[:, j].astype(jnp.float32).reshape(slots, LANES)
        operand = jnp.concatenate([block[:, :rows], block[:, rows : 2 * rows]], axis=0)
        product = lax.dot_general(
            operand.astype(jnp.bfloat16),
            table_ref[j],
            (((0,), (0,)), ((), ())),
            preferred_element_type=jnp.float32,
        )
        kept = jnp.where(position < counts[j], product[:, :points], 0.0)
        at = pl.ds(j * rows, rows)
        values[at, :] = kept.astype(jnp.bfloat16)
        copies.append(pltpu.make_async_copy(values.at[at, :], grid_hbm.at[at, :], left.at[j]))
        copies[-1].start()
    for copy in copies:
        copy.wait()


def on_device(grid, point_counts, waves, legendre, weights, stiffness):
    pairs, _, fields, points = grid.shape
    held = legendre.shape[0]
    width = waves.shape[0]
    owners = width // held
    slots = owners * ROWS
    rows = 2 * fields
    padded = -(-points // LANES) * LANES
    smem = pl.BlockSpec(memory_space=pltpu.SMEM)
    vmem = pl.BlockSpec(memory_space=pltpu.VMEM)
    anywhere = pl.BlockSpec(memory_space=pl.ANY)
    exchanged = jax.ShapeDtypeStruct((owners, pairs, ROWS, LANES), jnp.bfloat16)
    coefficients, tables = pl.pallas_call(
        functools.partial(analysis_kernel, held),
        out_shape=(exchanged, jax.ShapeDtypeStruct((pairs, 2 * slots, padded), jnp.bfloat16)),
        in_specs=[smem, smem, vmem, anywhere],
        out_specs=(vmem, vmem),
        scratch_shapes=[
            pltpu.VMEM((pairs * rows, points), jnp.bfloat16),
            pltpu.SemaphoreType.DMA,
        ],
        name="analysis",
    )(point_counts, weights, waves.reshape(1, width), grid.reshape(pairs * rows, points))
    received = lax.all_to_all(coefficients, "lat", split_axis=0, concat_axis=0, tiled=True)
    lane_stiffness = jnp.pad(stiffness, (0, LANES - stiffness.shape[0])).reshape(1, LANES)
    synthesised = pl.pallas_call(
        functools.partial(legendre_kernel, held, fields),
        out_shape=exchanged,
        in_specs=[smem, vmem, vmem, vmem],
        out_specs=vmem,
        scratch_shapes=[
            pltpu.VMEM((owners * pairs * ROWS, LANES), jnp.float32),
            pltpu.VMEM((owners * pairs * ROWS, LANES), jnp.float32),
        ],
        name="legendre",
    )(waves, lane_stiffness, legendre, received)
    returned = lax.all_to_all(synthesised, "lat", split_axis=0, concat_axis=0, tiled=True)
    result = pl.pallas_call(
        synthesis_kernel,
        out_shape=jax.ShapeDtypeStruct((pairs * rows, points), jnp.bfloat16),
        in_specs=[smem, vmem, vmem],
        out_specs=anywhere,
        scratch_shapes=[
            pltpu.VMEM((pairs * rows, points), jnp.bfloat16),
            pltpu.SemaphoreType.DMA((pairs,)),
        ],
        name="synthesis",
    )(point_counts, returned, tables)
    return result.reshape(grid.shape)


def fourier_tables(count, wavenumbers, quarter_max):
    quarter = count // 4
    step_angle = TWO_PI / quarter.astype(jnp.float32)
    coarse_count = (quarter_max + FINE_STEPS - 1) // FINE_STEPS
    coarse_pos = FINE_STEPS * jnp.arange(coarse_count, dtype=jnp.int32)
    fine_pos = jnp.arange(FINE_STEPS, dtype=jnp.int32)
    coarse_angle = (coarse_pos[:, None] * wavenumbers[None, :] % quarter).astype(
        jnp.float32
    ) * step_angle
    fine_angle = (fine_pos[:, None] * wavenumbers[None, :] % quarter).astype(
        jnp.float32
    ) * step_angle
    coarse_cos = jnp.cos(coarse_angle)[:, None, :]
    coarse_sin = jnp.sin(coarse_angle)[:, None, :]
    fine_cos = jnp.cos(fine_angle)[None, :, :]
    fine_sin = jnp.sin(fine_angle)[None, :, :]
    full_cos = (coarse_cos * fine_cos - coarse_sin * fine_sin).reshape(
        coarse_count * FINE_STEPS, -1
    )[:quarter_max]
    full_sin = (coarse_sin * fine_cos + coarse_cos * fine_sin).reshape(
        coarse_count * FINE_STEPS, -1
    )[:quarter_max]
    positions = jnp.arange(quarter_max, dtype=jnp.int32)
    inside = (positions < quarter)[:, None]
    cosine = jnp.where(inside, full_cos, 0.0)
    sine = jnp.where(inside, full_sin, 0.0)
    matrix = jnp.concatenate([cosine, sine], axis=1).astype(jnp.bfloat16)
    offsets = jnp.arange(4, dtype=jnp.int32)
    twist = offsets[:, None] * wavenumbers[None, :] % count
    theta = twist.astype(jnp.float32) * (TWO_PI / count.astype(jnp.float32))
    return (matrix, jnp.cos(theta), jnp.sin(theta))


def helmholtz(spectra, wavenumbers, offsets, stiffness_local, width):
    full_shape = spectra.shape
    quartered = spectra.reshape(full_shape[:-2] + (full_shape[-2] // 4, 2, 2, full_shape[-1]))
    parity = (1 - 2 * (offsets % 2)).astype(jnp.float32)
    combined = quartered[..., 0, :] + parity * quartered[..., 1, :]
    degrees = (wavenumbers + offsets).astype(jnp.float32)
    inside_band = offsets < width - wavenumbers
    factor = 1.0 / (
        1.0 + stiffness_local[:, None] * degrees[..., None, :] * (degrees[..., None, :] + 1.0)
    )
    damping = jnp.where(inside_band[..., None, :], factor, 0.0)
    scaled = (combined * damping[..., :, None, :]).astype(jnp.bfloat16)
    flipped = scaled * parity.astype(jnp.bfloat16)
    return jnp.stack([scaled, flipped], axis=-2).reshape(full_shape)


def spectral(received, wavenumbers, basis, stiffness_local):
    width = basis.shape[2]
    spectra = jnp.einsum("jcr,cjl->crl", received, basis, preferred_element_type=jnp.float32)
    offsets = jnp.arange(width, dtype=jnp.int32)
    operand = helmholtz(spectra, wavenumbers[:, None], offsets, stiffness_local, width)
    returned = jnp.einsum("crl,cjl->jcr", operand, basis, preferred_element_type=jnp.float32)
    return returned.astype(jnp.bfloat16)


def on_device_blocked(grid, point_counts, waves, legendre, weights, stiffness):
    pairs, _, fields, points = grid.shape
    quarter_max = points // 4
    width = waves.shape[0]
    held_slots = legendre.shape[0]
    lat_index = lax.axis_index("lat")
    lev_index = lax.axis_index("lev")

    def analyse(pieces):
        latitude, count, weight = pieces
        matrix, twist_cos, twist_sin = fourier_tables(count, waves, quarter_max)
        values = latitude.reshape(2, fields, quarter_max, 4)
        partial_value = jnp.einsum(
            "hfab,at->hfbt", values, matrix, preferred_element_type=jnp.float32
        )
        cos_part = partial_value[..., :width]
        sin_part = partial_value[..., width:]
        real = jnp.sum(twist_cos * cos_part - twist_sin * sin_part, axis=2)
        imag = -jnp.sum(twist_sin * cos_part + twist_cos * sin_part, axis=2)
        factor = jnp.where(2 * waves < count, weight / count.astype(jnp.float32), 0.0)
        stacked = jnp.stack([real * factor, imag * factor], axis=0)
        packed = jnp.transpose(stacked, (3, 2, 0, 1)).reshape(width, 4 * fields)
        return (packed.astype(jnp.bfloat16), matrix, twist_cos, twist_sin)

    coefficients, matrices, twist_cos, twist_sin = lax.map(analyse, (grid, point_counts, weights))
    received = lax.all_to_all(coefficients, "lat", split_axis=1, concat_axis=0, tiled=True)
    owned = lax.dynamic_slice_in_dim(waves, lat_index * held_slots, held_slots)
    own_stiffness = lax.dynamic_slice_in_dim(stiffness, lev_index * fields, fields)
    synthesised = spectral(received, owned, legendre, own_stiffness)
    returned = lax.all_to_all(synthesised, "lat", split_axis=0, concat_axis=1, tiled=True)

    def synthesise(pieces):
        packed, matrix, turn_cos, turn_sin, count = pieces
        values = packed.astype(jnp.float32).reshape(width, fields, 2, 2)
        real = values[:, :, 0, :]
        imag = values[:, :, 1, :]
        factor = jnp.where(2 * waves < count, jnp.where(waves == 0, 1.0, 2.0), 0.0)[:, None, None]
        cosines = turn_cos[:, :, None, None]
        sines = turn_sin[:, :, None, None]
        turned_real = factor * (real * cosines - imag * sines)
        turned_imag = factor * (real * sines + imag * cosines)
        operand = jnp.concatenate([turned_real, -turned_imag], axis=1)
        upper = operand.astype(jnp.bfloat16)
        lower = (operand - upper.astype(jnp.float32)).astype(jnp.bfloat16)
        result = jnp.einsum("bmfh,am->hfab", upper, matrix, preferred_element_type=jnp.float32)
        result = result + jnp.einsum(
            "bmfh,am->hfab", lower, matrix, preferred_element_type=jnp.float32
        )
        return result.reshape(2, fields, points).astype(jnp.bfloat16)

    return lax.map(synthesise, (returned, matrices, twist_cos, twist_sin, point_counts))


def fits_on_chip(mesh, grid, legendre, stiffness):
    owners, levels = mesh.shape["lat"], mesh.shape["lev"]
    pairs, fields = grid.shape[0] // owners, grid.shape[2] // levels
    held = legendre.shape[0] // owners
    table_bytes = 4 * pairs * owners * ROWS * grid.shape[3]
    return (
        table_bytes <= TABLE_BUDGET
        and held <= ROWS
        and 4 * fields <= LANES
        and fields % ROWS == 0
        and stiffness.shape[0] <= LANES
    )


def solution(mesh):
    in_specs = (P("lat", None, "lev", None), P("lat"), P(), P("lat", None, None), P("lat"), P())
    out_specs = P("lat", None, "lev", None)

    def program(grid, point_counts, waves, legendre, weights, stiffness):
        body = on_device if fits_on_chip(mesh, grid, legendre, stiffness) else on_device_blocked
        return jax.shard_map(
            body, mesh=mesh, in_specs=in_specs, out_specs=out_specs, check_vma=False
        )(grid, point_counts, waves, legendre, weights, stiffness)

    return program
```

```python
import functools
import math

import jax
import jax.numpy as jnp
from jax import lax
from jax.experimental import pallas as pl
from jax.experimental.pallas import tpu as pltpu
from jax.sharding import PartitionSpec as P

TWO_PI = 2.0 * math.pi
FINE_STEPS = 32
LANES = 128
ROWS = 8
TABLE_BUDGET = 4 << 20
KERNEL_BYTES = 8 << 20

COS_TURN = (
    0.9999999998781397, -19.739208740145937, 64.9393888386778, -85.45665201444898,
    60.24205245141228, -26.404165331517056, 7.79855301354287, -1.4511773940976733,
)
SIN_TURN = (
    6.2831853022485955, -41.341700317335295, 81.60512671223316, -76.70292598092092,
    42.02516399730493, -14.896874459689428, 3.233831551278599,
)


def polynomial(coefficients, u):
    total = coefficients[-1] * u + coefficients[-2]
    for value in coefficients[-3::-1]:
        total = total * u + value
    return total


def cos_minus_sin(steps, count, inverse):
    reduced = steps - jnp.floor(steps * inverse + 0.5) * count
    turn = reduced * inverse
    square = turn * turn
    return polynomial(COS_TURN, square), -turn * polynomial(SIN_TURN, square)


def wave_column(waves_ref, held, slots):
    width = waves_ref.shape[1]
    row = lax.broadcasted_iota(jnp.int32, (slots, width), 0)
    lane = lax.broadcasted_iota(jnp.int32, (slots, width), 1)
    place = row & (ROWS - 1)
    chosen = ((row >> 3) * held + place == lane) & (place < held)
    waves = jnp.broadcast_to(waves_ref[...].astype(jnp.float32), (slots, width))
    column = jnp.sum(jnp.where(chosen, waves, 0.0), axis=1, keepdims=True)
    filled = (lax.broadcasted_iota(jnp.int32, (slots, 1), 0) & (ROWS - 1)) < held
    return column, filled


def analysis_kernel(
    held, fields,
    counts_hbm, weights_hbm, waves_hbm, stiffness_hbm, basis_hbm, grid_hbm,
    coef_ref, table_ref, basis_ref, wave_ref, stiffness_ref, limit_ref,
    counts, weights, waves, levels, values, arrived,
):
    owners, pairs, _, _ = coef_ref.shape
    slots = owners * ROWS
    points = grid_hbm.shape[1]
    rows = grid_hbm.shape[0] // pairs
    needed = [
        pltpu.make_async_copy(source, target, arrived.at[k])
        for k, (source, target) in enumerate(
            [(counts_hbm, counts), (waves_hbm, waves), (weights_hbm, weights),
             (stiffness_hbm, levels), (grid_hbm, values), (basis_hbm, basis_ref)]
        )
    ]
    for copy in needed:
        copy.start()
    for copy in needed[:5]:
        copy.wait()
    wave, filled = wave_column(waves, held, slots)
    wave_ref[...] = jnp.broadcast_to(wave, (slots, LANES))
    lane = lax.broadcasted_iota(jnp.int32, (1, LANES), 1)
    all_levels = levels.shape[1]
    own = jnp.concatenate([levels[...], jnp.zeros((1, LANES - all_levels), jnp.float32)], axis=1)
    own = pltpu.roll(own, (LANES - lax.axis_index("lev") * fields) % LANES, 1)
    own = jnp.where(lane < fields, own, 0.0)
    stiffness = own
    for copy in range(1, 4):
        stiffness = stiffness + pltpu.roll(own, copy * fields, 1)
    stiffness_ref[...] = stiffness
    lane_count = jnp.ones((1, LANES), jnp.float32)
    for j in range(pairs):
        lane_count = jnp.where(lane == j, counts[j].astype(jnp.float32), lane_count)
    lane_inverse = 1.0 / lane_count
    turn_cos, turn_sin = cos_minus_sin(
        jnp.broadcast_to(wave * float(LANES), (slots, LANES)), lane_count, lane_inverse
    )
    steps = wave * lane.astype(jnp.float32)
    blocks = table_ref.shape[2] // LANES
    position = lax.broadcasted_iota(jnp.int32, (1, points), 1)
    for j in range(pairs):
        count = jnp.full((1, LANES), counts[j].astype(jnp.float32))
        limit_ref[j : j + 1, :] = count
        inverse = 1.0 / count
        cosine, sine = cos_minus_sin(steps, count, inverse)
        kept = filled & (2.0 * wave < count[:, :1])
        cosine = jnp.where(kept, cosine, 0.0)
        sine = jnp.where(kept, sine, 0.0)
        block_cos = turn_cos[:, j : j + 1]
        block_sin = turn_sin[:, j : j + 1]
        for block in range(blocks):
            if block > 0:
                cosine, sine = (
                    cosine * block_cos - sine * block_sin,
                    sine * block_cos + cosine * block_sin,
                )
            at = pl.ds(block * LANES, LANES)
            table_ref[j, :slots, at] = cosine.astype(jnp.bfloat16)
            table_ref[j, slots:, at] = sine.astype(jnp.bfloat16)
        inside = jnp.where(position < counts[j], 1.0, 0.0).astype(jnp.bfloat16)
        latitude = values[j * rows : (j + 1) * rows, :] * inside
        product = lax.dot_general(
            table_ref[j, :, :points],
            latitude,
            (((1,), (1,)), ((), ())),
            preferred_element_type=jnp.float32,
        )
        product = product * (jnp.full((1, 1), weights[j]) * inverse[:, :1])
        packed = jnp.concatenate(
            [
                product[:slots],
                product[slots:],
                jnp.zeros((slots, LANES - 2 * rows), jnp.float32),
            ],
            axis=1,
        )
        coef_ref[:, j] = packed.reshape(owners, ROWS, LANES).astype(jnp.bfloat16)
    needed[5].wait()


def legendre_kernel(held, fields, wave_ref, stiffness_ref, basis_ref, recv_ref, send_ref, fan_in, fan_out):
    owners, pairs, _, _ = recv_ref.shape
    latitudes = owners * pairs
    width = basis_ref.shape[2]
    first = lax.axis_index("lat") * ROWS
    fan_in[...] = recv_ref[...].astype(jnp.float32).reshape(latitudes * ROWS, LANES)
    stiffness = stiffness_ref[...]
    lane = lax.broadcasted_iota(jnp.int32, (1, LANES), 1)
    south = ((lane >= fields) & (lane < 2 * fields)) | (lane >= 3 * fields)
    offset = lax.broadcasted_iota(jnp.int32, (width, 1), 0)
    parity = jnp.where((offset & 1) == 0, 1.0, -1.0)
    offset = offset.astype(jnp.float32)
    for c in range(held):
        wave = wave_ref[pl.ds(first + c, 1), :]
        degree = offset + wave
        factor = 1.0 / (1.0 + stiffness * degree * (degree + 1.0))
        damping = jnp.where(degree < float(width), factor, 0.0)
        block = fan_in[pl.ds(c, latitudes, stride=ROWS), :].astype(jnp.bfloat16)
        basis = basis_ref[c]
        spectra = lax.dot_general(
            basis, block, (((0,), (0,)), ((), ())), preferred_element_type=jnp.float32
        )
        other = jnp.where(
            south, pltpu.roll(spectra, fields, 1), pltpu.roll(spectra, LANES - fields, 1)
        )
        scaled = ((spectra + parity * other) * damping).astype(jnp.bfloat16)
        returned = jnp.dot(basis, scaled, preferred_element_type=jnp.float32)
        returned = returned * jnp.where(wave == 0.0, 1.0, 2.0)
        fan_out[pl.ds(c, latitudes, stride=ROWS), :] = returned
    for c in range(held, ROWS):
        fan_out[pl.ds(c, latitudes, stride=ROWS), :] = jnp.zeros((latitudes, LANES), jnp.float32)
    send_ref[...] = fan_out[...].reshape(owners, pairs, ROWS, LANES).astype(jnp.bfloat16)


def synthesis_kernel(limit_ref, recv_ref, table_ref, grid_hbm, values, left):
    owners, pairs, _, _ = recv_ref.shape
    slots = owners * ROWS
    points = grid_hbm.shape[1]
    rows = grid_hbm.shape[0] // pairs
    position = lax.broadcasted_iota(jnp.int32, (1, points), 1).astype(jnp.float32)
    copies = []
    for j in range(pairs):
        block = recv_ref[:, j].astype(jnp.float32).reshape(slots, LANES)
        operand = jnp.concatenate([block[:, :rows], block[:, rows : 2 * rows]], axis=0)
        product = lax.dot_general(
            operand.astype(jnp.bfloat16),
            table_ref[j],
            (((0,), (0,)), ((), ())),
            preferred_element_type=jnp.float32,
        )
        kept = jnp.where(position < limit_ref[j : j + 1, :1], product[:, :points], 0.0)
        at = pl.ds(j * rows, rows)
        values[at, :] = kept.astype(jnp.bfloat16)
        copies.append(pltpu.make_async_copy(values.at[at, :], grid_hbm.at[at, :], left.at[j]))
        copies[-1].start()
    for copy in copies:
        copy.wait()


def on_device(grid, point_counts, waves, legendre, weights, stiffness):
    pairs, _, fields, points = grid.shape
    held = legendre.shape[0]
    width = waves.shape[0]
    owners = width // held
    slots = owners * ROWS
    rows = 2 * fields
    padded = -(-points // LANES) * LANES
    vmem = pl.BlockSpec(memory_space=pltpu.VMEM)
    hbm = pl.BlockSpec(memory_space=pltpu.HBM)
    limits = pltpu.CompilerParams(vmem_limit_bytes=KERNEL_BYTES)
    exchanged = jax.ShapeDtypeStruct((owners, pairs, ROWS, LANES), jnp.bfloat16)
    coefficients, tables, basis, wave_rows, levels, ends = pl.pallas_call(
        functools.partial(analysis_kernel, held, fields),
        out_shape=(
            exchanged,
            jax.ShapeDtypeStruct((pairs, 2 * slots, padded), jnp.bfloat16),
            jax.ShapeDtypeStruct(legendre.shape, legendre.dtype),
            jax.ShapeDtypeStruct((slots, LANES), jnp.float32),
            jax.ShapeDtypeStruct((1, LANES), jnp.float32),
            jax.ShapeDtypeStruct((pairs, LANES), jnp.float32),
        ),
        in_specs=[hbm] * 6,
        out_specs=(vmem,) * 6,
        scratch_shapes=[
            pltpu.SMEM((pairs,), jnp.int32),
            pltpu.SMEM((pairs,), jnp.float32),
            pltpu.VMEM((1, width), jnp.int32),
            pltpu.VMEM((1, stiffness.shape[0]), jnp.float32),
            pltpu.VMEM((pairs * rows, points), jnp.bfloat16),
            pltpu.SemaphoreType.DMA((6,)),
        ],
        compiler_params=limits,
        name="analysis",
    )(
        *(
            pltpu.with_memory_space_constraint(array, pltpu.HBM)
            for array in (
                point_counts, weights, waves.reshape(1, width), stiffness.reshape(1, -1), legendre,
                grid.reshape(pairs * rows, points),
            )
        )
    )
    received = lax.all_to_all(coefficients, "lat", split_axis=0, concat_axis=0, tiled=True)
    synthesised = pl.pallas_call(
        functools.partial(legendre_kernel, held, fields),
        out_shape=exchanged,
        in_specs=[vmem] * 4,
        out_specs=vmem,
        scratch_shapes=[
            pltpu.VMEM((owners * pairs * ROWS, LANES), jnp.float32),
            pltpu.VMEM((owners * pairs * ROWS, LANES), jnp.float32),
        ],
        compiler_params=limits,
        name="legendre",
    )(wave_rows, levels, basis, received)
    returned = lax.all_to_all(synthesised, "lat", split_axis=0, concat_axis=0, tiled=True)
    result = pl.pallas_call(
        synthesis_kernel,
        out_shape=jax.ShapeDtypeStruct((pairs * rows, points), jnp.bfloat16),
        in_specs=[vmem] * 3,
        out_specs=hbm,
        scratch_shapes=[
            pltpu.VMEM((pairs * rows, points), jnp.bfloat16),
            pltpu.SemaphoreType.DMA((pairs,)),
        ],
        compiler_params=limits,
        name="synthesis",
    )(ends, returned, tables)
    return result.reshape(grid.shape)


def fourier_tables(count, wavenumbers, quarter_max):
    quarter = count // 4
    step_angle = TWO_PI / quarter.astype(jnp.float32)
    coarse_count = (quarter_max + FINE_STEPS - 1) // FINE_STEPS
    coarse_pos = FINE_STEPS * jnp.arange(coarse_count, dtype=jnp.int32)
    fine_pos = jnp.arange(FINE_STEPS, dtype=jnp.int32)
    coarse_angle = (coarse_pos[:, None] * wavenumbers[None, :] % quarter).astype(
        jnp.float32
    ) * step_angle
    fine_angle = (fine_pos[:, None] * wavenumbers[None, :] % quarter).astype(
        jnp.float32
    ) * step_angle
    coarse_cos = jnp.cos(coarse_angle)[:, None, :]
    coarse_sin = jnp.sin(coarse_angle)[:, None, :]
    fine_cos = jnp.cos(fine_angle)[None, :, :]
    fine_sin = jnp.sin(fine_angle)[None, :, :]
    full_cos = (coarse_cos * fine_cos - coarse_sin * fine_sin).reshape(
        coarse_count * FINE_STEPS, -1
    )[:quarter_max]
    full_sin = (coarse_sin * fine_cos + coarse_cos * fine_sin).reshape(
        coarse_count * FINE_STEPS, -1
    )[:quarter_max]
    positions = jnp.arange(quarter_max, dtype=jnp.int32)
    inside = (positions < quarter)[:, None]
    cosine = jnp.where(inside, full_cos, 0.0)
    sine = jnp.where(inside, full_sin, 0.0)
    matrix = jnp.concatenate([cosine, sine], axis=1).astype(jnp.bfloat16)
    offsets = jnp.arange(4, dtype=jnp.int32)
    twist = offsets[:, None] * wavenumbers[None, :] % count
    theta = twist.astype(jnp.float32) * (TWO_PI / count.astype(jnp.float32))
    return (matrix, jnp.cos(theta), jnp.sin(theta))


def helmholtz(spectra, wavenumbers, offsets, stiffness_local, width):
    full_shape = spectra.shape
    quartered = spectra.reshape(full_shape[:-2] + (full_shape[-2] // 4, 2, 2, full_shape[-1]))
    parity = (1 - 2 * (offsets % 2)).astype(jnp.float32)
    combined = quartered[..., 0, :] + parity * quartered[..., 1, :]
    degrees = (wavenumbers + offsets).astype(jnp.float32)
    inside_band = offsets < width - wavenumbers
    factor = 1.0 / (
        1.0 + stiffness_local[:, None] * degrees[..., None, :] * (degrees[..., None, :] + 1.0)
    )
    damping = jnp.where(inside_band[..., None, :], factor, 0.0)
    scaled = (combined * damping[..., :, None, :]).astype(jnp.bfloat16)
    flipped = scaled * parity.astype(jnp.bfloat16)
    return jnp.stack([scaled, flipped], axis=-2).reshape(full_shape)


def spectral(received, wavenumbers, basis, stiffness_local):
    width = basis.shape[2]
    spectra = jnp.einsum("jcr,cjl->crl", received, basis, preferred_element_type=jnp.float32)
    offsets = jnp.arange(width, dtype=jnp.int32)
    operand = helmholtz(spectra, wavenumbers[:, None], offsets, stiffness_local, width)
    returned = jnp.einsum("crl,cjl->jcr", operand, basis, preferred_element_type=jnp.float32)
    return returned.astype(jnp.bfloat16)


def on_device_blocked(grid, point_counts, waves, legendre, weights, stiffness):
    pairs, _, fields, points = grid.shape
    quarter_max = points // 4
    width = waves.shape[0]
    held_slots = legendre.shape[0]
    lat_index = lax.axis_index("lat")
    lev_index = lax.axis_index("lev")

    def analyse(pieces):
        latitude, count, weight = pieces
        matrix, twist_cos, twist_sin = fourier_tables(count, waves, quarter_max)
        values = latitude.reshape(2, fields, quarter_max, 4)
        partial_value = jnp.einsum(
            "hfab,at->hfbt", values, matrix, preferred_element_type=jnp.float32
        )
        cos_part = partial_value[..., :width]
        sin_part = partial_value[..., width:]
        real = jnp.sum(twist_cos * cos_part - twist_sin * sin_part, axis=2)
        imag = -jnp.sum(twist_sin * cos_part + twist_cos * sin_part, axis=2)
        factor = jnp.where(2 * waves < count, weight / count.astype(jnp.float32), 0.0)
        stacked = jnp.stack([real * factor, imag * factor], axis=0)
        packed = jnp.transpose(stacked, (3, 2, 0, 1)).reshape(width, 4 * fields)
        return (packed.astype(jnp.bfloat16), matrix, twist_cos, twist_sin)

    coefficients, matrices, twist_cos, twist_sin = lax.map(analyse, (grid, point_counts, weights))
    received = lax.all_to_all(coefficients, "lat", split_axis=1, concat_axis=0, tiled=True)
    owned = lax.dynamic_slice_in_dim(waves, lat_index * held_slots, held_slots)
    own_stiffness = lax.dynamic_slice_in_dim(stiffness, lev_index * fields, fields)
    synthesised = spectral(received, owned, legendre, own_stiffness)
    returned = lax.all_to_all(synthesised, "lat", split_axis=0, concat_axis=1, tiled=True)

    def synthesise(pieces):
        packed, matrix, turn_cos, turn_sin, count = pieces
        values = packed.astype(jnp.float32).reshape(width, fields, 2, 2)
        real = values[:, :, 0, :]
        imag = values[:, :, 1, :]
        factor = jnp.where(2 * waves < count, jnp.where(waves == 0, 1.0, 2.0), 0.0)[:, None, None]
        cosines = turn_cos[:, :, None, None]
        sines = turn_sin[:, :, None, None]
        turned_real = factor * (real * cosines - imag * sines)
        turned_imag = factor * (real * sines + imag * cosines)
        operand = jnp.concatenate([turned_real, -turned_imag], axis=1)
        upper = operand.astype(jnp.bfloat16)
        lower = (operand - upper.astype(jnp.float32)).astype(jnp.bfloat16)
        result = jnp.einsum("bmfh,am->hfab", upper, matrix, preferred_element_type=jnp.float32)
        result = result + jnp.einsum(
            "bmfh,am->hfab", lower, matrix, preferred_element_type=jnp.float32
        )
        return result.reshape(2, fields, points).astype(jnp.bfloat16)

    return lax.map(synthesise, (returned, matrices, twist_cos, twist_sin, point_counts))


def fits_on_chip(mesh, grid, legendre, stiffness):
    owners, levels = mesh.shape["lat"], mesh.shape["lev"]
    pairs, fields = grid.shape[0] // owners, grid.shape[2] // levels
    held = legendre.shape[0] // owners
    table_bytes = 4 * pairs * owners * ROWS * grid.shape[3]
    return (
        table_bytes <= TABLE_BUDGET
        and held <= ROWS
        and 4 * fields <= LANES
        and fields % ROWS == 0
        and stiffness.shape[0] <= LANES
    )


def solution(mesh):
    in_specs = (P("lat", None, "lev", None), P("lat"), P(), P("lat", None, None), P("lat"), P())
    out_specs = P("lat", None, "lev", None)

    def program(grid, point_counts, waves, legendre, weights, stiffness):
        body = on_device if fits_on_chip(mesh, grid, legendre, stiffness) else on_device_blocked
        return jax.shard_map(
            body, mesh=mesh, in_specs=in_specs, out_specs=out_specs, check_vma=False
        )(grid, point_counts, waves, legendre, weights, stiffness)

    return program
```

```python
import functools
import math

import jax
import jax.numpy as jnp
from jax import lax
from jax.experimental import pallas as pl
from jax.experimental.pallas import tpu as pltpu
from jax.sharding import PartitionSpec as P

TWO_PI = 2.0 * math.pi
FINE_STEPS = 32
LANES = 128
ROWS = 8
HALF = 4
TABLE_BUDGET = 4 << 20
KERNEL_BYTES = 8 << 20

COS_TURN = (
    0.9999999998781397, -19.739208740145937, 64.9393888386778, -85.45665201444898,
    60.24205245141228, -26.404165331517056, 7.79855301354287, -1.4511773940976733,
)
SIN_TURN = (
    6.2831853022485955, -41.341700317335295, 81.60512671223316, -76.70292598092092,
    42.02516399730493, -14.896874459689428, 3.233831551278599,
)


def polynomial(coefficients, u):
    total = coefficients[-1] * u + coefficients[-2]
    for value in coefficients[-3::-1]:
        total = total * u + value
    return total


def cos_minus_sin(steps, count, inverse):
    reduced = steps - jnp.floor(steps * inverse + 0.5) * count
    turn = reduced * inverse
    square = turn * turn
    return polynomial(COS_TURN, square), -turn * polynomial(SIN_TURN, square)


def wave_column(waves_ref, held, slots):
    width = waves_ref.shape[1]
    row = lax.broadcasted_iota(jnp.int32, (slots, width), 0)
    lane = lax.broadcasted_iota(jnp.int32, (slots, width), 1)
    place = row & (HALF - 1)
    chosen = ((row >> 2) * held + place == lane) & (place < held)
    waves = jnp.broadcast_to(waves_ref[...].astype(jnp.float32), (slots, width))
    column = jnp.sum(jnp.where(chosen, waves, 0.0), axis=1, keepdims=True)
    filled = (lax.broadcasted_iota(jnp.int32, (slots, 1), 0) & (HALF - 1)) < held
    return column, filled


def segments(start, length):
    done = 0
    while done < length:
        block, lane = divmod(start + done, LANES)
        size = min(length - done, LANES - lane)
        yield block, lane, done, size
        done += size


def turn(x, shift, axis):
    shift %= x.shape[axis]
    return pltpu.roll(x, shift, axis) if shift else x


def fold_rest(whole, part, held, rest):
    sublane = lax.broadcasted_iota(jnp.int32, (1, ROWS, LANES), 1) & (HALF - 1)
    lane = lax.broadcasted_iota(jnp.int32, (1, ROWS, LANES), 2)
    for c in range(held):
        moved = turn(turn(part, HALF - 1 - c, 1), c * rest, 2)
        here = (sublane == HALF - 1) & (lane >= c * rest) & (lane < (c + 1) * rest)
        whole = jnp.where(here, moved, whole)
    return whole


def unfold_rest(whole, held, rest):
    sublane = lax.broadcasted_iota(jnp.int32, (1, ROWS, LANES), 1) & (HALF - 1)
    part = whole
    for c in range(held):
        part = jnp.where(sublane == c, turn(turn(whole, c + 1 - HALF, 1), -c * rest, 2), part)
    return part


def analysis_kernel(
    held, fields,
    counts_hbm, weights_hbm, waves_hbm, stiffness_hbm, basis_hbm, grid_hbm,
    coef_ref, table_ref, basis_ref, wave_ref, stiffness_ref, limit_ref,
    counts, weights, waves, levels, values, given, widened, arrived,
):
    owners, blocks, _, _ = coef_ref.shape
    pairs = table_ref.shape[0]
    slots = owners * HALF
    points = grid_hbm.shape[1]
    rows = grid_hbm.shape[0] // pairs
    rest = pairs * rows - blocks * LANES
    groups = slots // ROWS
    own_basis = basis_hbm.at[pl.ds(lax.axis_index("lev") * held, held)]
    needed = [
        pltpu.make_async_copy(source, target, arrived.at[k])
        for k, (source, target) in enumerate(
            [(counts_hbm, counts), (waves_hbm, waves), (weights_hbm, weights),
             (stiffness_hbm, levels), (grid_hbm, values), (own_basis, given)]
        )
    ]
    for copy in needed:
        copy.start()
    for copy in needed:
        copy.wait()
    wave, filled = wave_column(waves, held, slots)
    wave_ref[...] = jnp.broadcast_to(wave, (slots, LANES))
    latitudes = basis_ref.shape[1]
    shards = latitudes // pairs
    widened[...] = given[...].astype(jnp.float32)
    for c in range(held):
        for j in range(pairs):
            basis_ref[c, j * shards : (j + 1) * shards, :] = widened[
                c, pl.ds(j, shards, stride=pairs), :
            ].astype(jnp.bfloat16)
    lane = lax.broadcasted_iota(jnp.int32, (1, LANES), 1)
    all_levels = levels.shape[1]
    padded = jnp.concatenate([levels[...], jnp.zeros((1, LANES - all_levels), jnp.float32)], axis=1)
    for shard in range(all_levels // fields):
        own = jnp.where(lane < fields, turn(padded, -shard * fields, 1), 0.0)
        stiffness = own
        for copy in range(1, 4):
            stiffness = stiffness + turn(own, copy * fields, 1)
        stiffness_ref[shard : shard + 1, :] = stiffness
    lane_count = jnp.ones((1, LANES), jnp.float32)
    for j in range(pairs):
        lane_count = jnp.where(lane == j, counts[j].astype(jnp.float32), lane_count)
    lane_inverse = 1.0 / lane_count
    turn_cos, turn_sin = cos_minus_sin(
        jnp.broadcast_to(wave * float(LANES), (slots, LANES)), lane_count, lane_inverse
    )
    steps = wave * lane.astype(jnp.float32)
    position = lax.broadcasted_iota(jnp.int32, (1, points), 1)
    real, imaginary = [], []
    for j in range(pairs):
        count = jnp.full((1, LANES), counts[j].astype(jnp.float32))
        limit_ref[j : j + 1, :] = count
        inverse = 1.0 / count
        cosine, sine = cos_minus_sin(steps, count, inverse)
        kept = filled & (2.0 * wave < count[:, :1])
        cosine = jnp.where(kept, cosine, 0.0)
        sine = jnp.where(kept, sine, 0.0)
        block_cos = turn_cos[:, j : j + 1]
        block_sin = turn_sin[:, j : j + 1]
        for block in range(table_ref.shape[2] // LANES):
            if block > 0:
                cosine, sine = (
                    cosine * block_cos - sine * block_sin,
                    sine * block_cos + cosine * block_sin,
                )
            at = pl.ds(block * LANES, LANES)
            table_ref[j, :slots, at] = cosine.astype(jnp.bfloat16)
            table_ref[j, slots:, at] = sine.astype(jnp.bfloat16)
        inside = jnp.where(position < counts[j], 1.0, 0.0).astype(jnp.bfloat16)
        latitude = values[j * rows : (j + 1) * rows, :] * inside
        product = lax.dot_general(
            table_ref[j, :, :points],
            latitude,
            (((1,), (1,)), ((), ())),
            preferred_element_type=jnp.float32,
        )
        product = product * (jnp.full((1, 1), weights[j]) * inverse[:, :1])
        real.append(product[:slots])
        imaginary.append(product[slots:])
    tail = [jnp.zeros((slots, LANES - rest), jnp.float32)] if rest else []
    parts = []
    for pieces in (real, imaginary):
        whole = jnp.concatenate(pieces + tail, axis=1)
        cut = [
            whole[:, block * LANES : (block + 1) * LANES].reshape(groups, ROWS, LANES)
            for block in range(whole.shape[1] // LANES)
        ]
        if rest:
            cut[-2] = fold_rest(cut[-2], cut[-1], held, rest)
        parts.append(cut)
    low = lax.broadcasted_iota(jnp.int32, (1, ROWS, LANES), 1) < HALF
    for block in range(blocks):
        first, second = parts[0][block], parts[1][block]
        even = jnp.where(low, first, turn(second, HALF, 1))
        odd = jnp.where(low, turn(first, HALF, 1), second)
        both = jnp.stack([even, odd], axis=1).reshape(owners, ROWS, LANES)
        coef_ref[:, block] = both.astype(jnp.bfloat16)


def legendre_kernel(
    held, fields, wave_ref, stiffness_ref, basis_ref, recv_ref, send_ref, fan_in, fan_out
):
    owners, blocks, _, _ = recv_ref.shape
    latitudes, width = basis_ref.shape[1:]
    shards = stiffness_ref.shape[0]
    senders = owners // shards
    pairs = latitudes // senders
    rows = 2 * fields
    rest = pairs * rows - blocks * LANES
    first = (lax.axis_index("lat") * shards + lax.axis_index("lev")) * HALF
    fan_in[...] = recv_ref[...].astype(jnp.float32).reshape(owners * blocks * ROWS, LANES)

    def chunk_rows(shard, block, row):
        return pl.ds((shard * blocks + block) * ROWS + row, senders, stride=shards * blocks * ROWS)

    def home(part, c, block, lane):
        if block == blocks:
            return part * HALF + HALF - 1, block - 1, c * rest + lane
        return part * HALF + c, block, lane

    lane_at = lax.broadcasted_iota(jnp.int32, (1, LANES), 1)
    south = ((lane_at >= fields) & (lane_at < 2 * fields)) | (lane_at >= 3 * fields)
    offset = lax.broadcasted_iota(jnp.int32, (width, 1), 0)
    parity = jnp.where((offset & 1) == 0, 1.0, -1.0)
    offset = offset.astype(jnp.float32)
    folded = {}
    for c in range(held):
        wave = wave_ref[pl.ds(first + c, 1), :]
        degree = offset + wave
        basis = basis_ref[c]
        sides = []
        for shard in range(shards):
            strips = []
            for j in range(pairs):
                strip = jnp.zeros((senders, LANES), jnp.float32)
                for part in range(2):
                    for block, lane, place, size in segments(j * rows, rows):
                        row, block, lane = home(part, c, block, lane)
                        source = fan_in[chunk_rows(shard, block, row), :]
                        target = part * rows + place
                        here = (lane_at >= target) & (lane_at < target + size)
                        strip = jnp.where(here, turn(source, target - lane, 1), strip)
                strips.append(strip.astype(jnp.bfloat16))
            sides.append(jnp.concatenate(strips, axis=0))
        spectra = lax.dot_general(
            basis,
            jnp.concatenate(sides, axis=1),
            (((0,), (0,)), ((), ())),
            preferred_element_type=jnp.float32,
        )
        scaled = []
        for shard in range(shards):
            side = spectra[:, shard * LANES : (shard + 1) * LANES]
            factor = 1.0 / (1.0 + stiffness_ref[shard : shard + 1, :] * degree * (degree + 1.0))
            damping = jnp.where(degree < float(width), factor, 0.0)
            other = jnp.where(south, turn(side, fields, 1), turn(side, -fields, 1))
            scaled.append(((side + parity * other) * damping).astype(jnp.bfloat16))
        returned = jnp.dot(
            basis, jnp.concatenate(scaled, axis=1), preferred_element_type=jnp.float32
        )
        weight = jnp.where(wave == 0.0, 1.0, 2.0)
        for shard in range(shards):
            side = returned[:, shard * LANES : (shard + 1) * LANES] * weight
            for part in range(2):
                built = {}
                for j in range(pairs):
                    strip = side[j * senders : (j + 1) * senders]
                    for block, lane, place, size in segments(j * rows, rows):
                        row, block, lane = home(part, c, block, lane)
                        key = (shard, block, row)
                        here = (lane_at >= lane) & (lane_at < lane + size)
                        moved = turn(strip, lane - part * rows - place, 1)
                        held_in = folded if row % HALF == HALF - 1 else built
                        before = held_in.get(key, jnp.zeros((senders, LANES), jnp.float32))
                        held_in[key] = jnp.where(here, moved, before)
                for key, value in built.items():
                    fan_out[chunk_rows(*key), :] = value
    empty = jnp.zeros((senders, LANES), jnp.float32)
    for shard in range(shards):
        for block in range(blocks):
            for part in range(2):
                for place in range(held, HALF):
                    key = (shard, block, part * HALF + place)
                    fan_out[chunk_rows(*key), :] = folded.get(key, empty)
    send_ref[...] = fan_out[...].reshape(owners, blocks, ROWS, LANES).astype(jnp.bfloat16)


def synthesis_kernel(held, limit_ref, recv_ref, table_ref, grid_hbm, values, left):
    owners, blocks, _, _ = recv_ref.shape
    pairs = table_ref.shape[0]
    slots = owners * HALF
    points = grid_hbm.shape[1]
    rows = grid_hbm.shape[0] // pairs
    rest = pairs * rows - blocks * LANES
    groups = slots // ROWS
    low = lax.broadcasted_iota(jnp.int32, (1, ROWS, LANES), 1) < HALF
    parts = ([], [])
    for block in range(blocks):
        both = recv_ref[:, block].astype(jnp.float32).reshape(groups, 2, ROWS, LANES)
        even, odd = both[:, 0], both[:, 1]
        parts[0].append(jnp.where(low, even, turn(odd, HALF, 1)))
        parts[1].append(jnp.where(low, turn(even, HALF, 1), odd))
    if rest:
        for part in parts:
            part.append(unfold_rest(part[-1], held, rest))
    operand = jnp.concatenate(
        [
            jnp.concatenate([part[block].reshape(slots, LANES) for part in parts], axis=0).T
            for block in range(len(parts[0]))
        ],
        axis=0,
    ).astype(jnp.bfloat16)
    position = lax.broadcasted_iota(jnp.int32, (1, points), 1).astype(jnp.float32)
    copies = []
    for j in range(pairs):
        product = jnp.dot(
            operand[j * rows : (j + 1) * rows], table_ref[j], preferred_element_type=jnp.float32
        )
        kept = jnp.where(position < limit_ref[j : j + 1, :1], product[:, :points], 0.0)
        at = pl.ds(j * rows, rows)
        values[at, :] = kept.astype(jnp.bfloat16)
        copies.append(pltpu.make_async_copy(values.at[at, :], grid_hbm.at[at, :], left.at[j]))
        copies[-1].start()
    for copy in copies:
        copy.wait()


def on_device(mesh, grid, point_counts, waves, legendre, weights, stiffness):
    pairs, _, fields, points = grid.shape
    width = waves.shape[0]
    shards = mesh.shape["lev"]
    owners = mesh.shape["lat"] * shards
    held = width // owners
    slots = owners * HALF
    rows = 2 * fields
    padded = -(-points // LANES) * LANES
    blocks = pairs * rows // LANES
    own_basis = (held,) + legendre.shape[1:]
    vmem = pl.BlockSpec(memory_space=pltpu.VMEM)
    hbm = pl.BlockSpec(memory_space=pltpu.HBM)
    limits = pltpu.CompilerParams(vmem_limit_bytes=KERNEL_BYTES)
    exchanged = jax.ShapeDtypeStruct((owners, blocks, ROWS, LANES), jnp.bfloat16)
    coefficients, tables, basis, wave_rows, levels, ends = pl.pallas_call(
        functools.partial(analysis_kernel, held, fields),
        out_shape=(
            exchanged,
            jax.ShapeDtypeStruct((pairs, 2 * slots, padded), jnp.bfloat16),
            jax.ShapeDtypeStruct(own_basis, jnp.bfloat16),
            jax.ShapeDtypeStruct((slots, LANES), jnp.float32),
            jax.ShapeDtypeStruct((shards, LANES), jnp.float32),
            jax.ShapeDtypeStruct((pairs, LANES), jnp.float32),
        ),
        in_specs=[hbm] * 6,
        out_specs=(vmem,) * 6,
        scratch_shapes=[
            pltpu.SMEM((pairs,), jnp.int32),
            pltpu.SMEM((pairs,), jnp.float32),
            pltpu.VMEM((1, width), jnp.int32),
            pltpu.VMEM((1, stiffness.shape[0]), jnp.float32),
            pltpu.VMEM((pairs * rows, points), jnp.bfloat16),
            pltpu.VMEM(own_basis, jnp.bfloat16),
            pltpu.VMEM(own_basis, jnp.float32),
            pltpu.SemaphoreType.DMA((6,)),
        ],
        compiler_params=limits,
        name="analysis",
    )(
        *(
            pltpu.with_memory_space_constraint(array, pltpu.HBM)
            for array in (
                point_counts, weights, waves.reshape(1, width), stiffness.reshape(1, -1), legendre,
                grid.reshape(pairs * rows, points),
            )
        )
    )
    everyone = ("lat", "lev")
    received = lax.all_to_all(coefficients, everyone, split_axis=0, concat_axis=0, tiled=True)
    synthesised = pl.pallas_call(
        functools.partial(legendre_kernel, held, fields),
        out_shape=exchanged,
        in_specs=[vmem] * 4,
        out_specs=vmem,
        scratch_shapes=[
            pltpu.VMEM((owners * blocks * ROWS, LANES), jnp.float32),
            pltpu.VMEM((owners * blocks * ROWS, LANES), jnp.float32),
        ],
        compiler_params=limits,
        name="legendre",
    )(wave_rows, levels, basis, received)
    returned = lax.all_to_all(synthesised, everyone, split_axis=0, concat_axis=0, tiled=True)
    result = pl.pallas_call(
        functools.partial(synthesis_kernel, held),
        out_shape=jax.ShapeDtypeStruct((pairs * rows, points), jnp.bfloat16),
        in_specs=[vmem] * 3,
        out_specs=hbm,
        scratch_shapes=[
            pltpu.VMEM((pairs * rows, points), jnp.bfloat16),
            pltpu.SemaphoreType.DMA((pairs,)),
        ],
        compiler_params=limits,
        name="synthesis",
    )(ends, returned, tables)
    return result.reshape(grid.shape)


def fourier_tables(count, wavenumbers, quarter_max):
    quarter = count // 4
    step_angle = TWO_PI / quarter.astype(jnp.float32)
    coarse_count = (quarter_max + FINE_STEPS - 1) // FINE_STEPS
    coarse_pos = FINE_STEPS * jnp.arange(coarse_count, dtype=jnp.int32)
    fine_pos = jnp.arange(FINE_STEPS, dtype=jnp.int32)
    coarse_angle = (coarse_pos[:, None] * wavenumbers[None, :] % quarter).astype(
        jnp.float32
    ) * step_angle
    fine_angle = (fine_pos[:, None] * wavenumbers[None, :] % quarter).astype(
        jnp.float32
    ) * step_angle
    coarse_cos = jnp.cos(coarse_angle)[:, None, :]
    coarse_sin = jnp.sin(coarse_angle)[:, None, :]
    fine_cos = jnp.cos(fine_angle)[None, :, :]
    fine_sin = jnp.sin(fine_angle)[None, :, :]
    full_cos = (coarse_cos * fine_cos - coarse_sin * fine_sin).reshape(
        coarse_count * FINE_STEPS, -1
    )[:quarter_max]
    full_sin = (coarse_sin * fine_cos + coarse_cos * fine_sin).reshape(
        coarse_count * FINE_STEPS, -1
    )[:quarter_max]
    positions = jnp.arange(quarter_max, dtype=jnp.int32)
    inside = (positions < quarter)[:, None]
    cosine = jnp.where(inside, full_cos, 0.0)
    sine = jnp.where(inside, full_sin, 0.0)
    matrix = jnp.concatenate([cosine, sine], axis=1).astype(jnp.bfloat16)
    offsets = jnp.arange(4, dtype=jnp.int32)
    twist = offsets[:, None] * wavenumbers[None, :] % count
    theta = twist.astype(jnp.float32) * (TWO_PI / count.astype(jnp.float32))
    return (matrix, jnp.cos(theta), jnp.sin(theta))


def helmholtz(spectra, wavenumbers, offsets, stiffness_local, width):
    full_shape = spectra.shape
    quartered = spectra.reshape(full_shape[:-2] + (full_shape[-2] // 4, 2, 2, full_shape[-1]))
    parity = (1 - 2 * (offsets % 2)).astype(jnp.float32)
    combined = quartered[..., 0, :] + parity * quartered[..., 1, :]
    degrees = (wavenumbers + offsets).astype(jnp.float32)
    inside_band = offsets < width - wavenumbers
    factor = 1.0 / (
        1.0 + stiffness_local[:, None] * degrees[..., None, :] * (degrees[..., None, :] + 1.0)
    )
    damping = jnp.where(inside_band[..., None, :], factor, 0.0)
    scaled = (combined * damping[..., :, None, :]).astype(jnp.bfloat16)
    flipped = scaled * parity.astype(jnp.bfloat16)
    return jnp.stack([scaled, flipped], axis=-2).reshape(full_shape)


def spectral(received, wavenumbers, basis, stiffness_local):
    width = basis.shape[2]
    spectra = jnp.einsum("jcr,cjl->crl", received, basis, preferred_element_type=jnp.float32)
    offsets = jnp.arange(width, dtype=jnp.int32)
    operand = helmholtz(spectra, wavenumbers[:, None], offsets, stiffness_local, width)
    returned = jnp.einsum("crl,cjl->jcr", operand, basis, preferred_element_type=jnp.float32)
    return returned.astype(jnp.bfloat16)


def on_device_blocked(grid, point_counts, waves, legendre, weights, stiffness):
    pairs, _, fields, points = grid.shape
    quarter_max = points // 4
    width = waves.shape[0]
    held_slots = legendre.shape[0]
    lat_index = lax.axis_index("lat")
    lev_index = lax.axis_index("lev")

    def analyse(pieces):
        latitude, count, weight = pieces
        matrix, twist_cos, twist_sin = fourier_tables(count, waves, quarter_max)
        values = latitude.reshape(2, fields, quarter_max, 4)
        partial_value = jnp.einsum(
            "hfab,at->hfbt", values, matrix, preferred_element_type=jnp.float32
        )
        cos_part = partial_value[..., :width]
        sin_part = partial_value[..., width:]
        real = jnp.sum(twist_cos * cos_part - twist_sin * sin_part, axis=2)
        imag = -jnp.sum(twist_sin * cos_part + twist_cos * sin_part, axis=2)
        factor = jnp.where(2 * waves < count, weight / count.astype(jnp.float32), 0.0)
        stacked = jnp.stack([real * factor, imag * factor], axis=0)
        packed = jnp.transpose(stacked, (3, 2, 0, 1)).reshape(width, 4 * fields)
        return (packed.astype(jnp.bfloat16), matrix, twist_cos, twist_sin)

    coefficients, matrices, twist_cos, twist_sin = lax.map(analyse, (grid, point_counts, weights))
    received = lax.all_to_all(coefficients, "lat", split_axis=1, concat_axis=0, tiled=True)
    owned = lax.dynamic_slice_in_dim(waves, lat_index * held_slots, held_slots)
    own_stiffness = lax.dynamic_slice_in_dim(stiffness, lev_index * fields, fields)
    synthesised = spectral(received, owned, legendre, own_stiffness)
    returned = lax.all_to_all(synthesised, "lat", split_axis=0, concat_axis=1, tiled=True)

    def synthesise(pieces):
        packed, matrix, turn_cos, turn_sin, count = pieces
        values = packed.astype(jnp.float32).reshape(width, fields, 2, 2)
        real = values[:, :, 0, :]
        imag = values[:, :, 1, :]
        factor = jnp.where(2 * waves < count, jnp.where(waves == 0, 1.0, 2.0), 0.0)[:, None, None]
        cosines = turn_cos[:, :, None, None]
        sines = turn_sin[:, :, None, None]
        turned_real = factor * (real * cosines - imag * sines)
        turned_imag = factor * (real * sines + imag * cosines)
        operand = jnp.concatenate([turned_real, -turned_imag], axis=1)
        upper = operand.astype(jnp.bfloat16)
        lower = (operand - upper.astype(jnp.float32)).astype(jnp.bfloat16)
        result = jnp.einsum("bmfh,am->hfab", upper, matrix, preferred_element_type=jnp.float32)
        result = result + jnp.einsum(
            "bmfh,am->hfab", lower, matrix, preferred_element_type=jnp.float32
        )
        return result.reshape(2, fields, points).astype(jnp.bfloat16)

    return lax.map(synthesise, (returned, matrices, twist_cos, twist_sin, point_counts))


def fits_on_chip(mesh, grid, waves, stiffness):
    shards = mesh.shape["lev"]
    owners = mesh.shape["lat"] * shards
    pairs, fields = grid.shape[0] // mesh.shape["lat"], grid.shape[2] // shards
    held = waves.shape[0] // owners
    lanes = 2 * pairs * fields
    return (
        waves.shape[0] % owners == 0
        and 4 * pairs * owners * HALF * grid.shape[3] <= TABLE_BUDGET
        and held < HALF
        and lanes >= LANES
        and held * (lanes % LANES) <= LANES
        and 4 * fields <= LANES
        and fields % ROWS == 0
        and owners * HALF % (2 * ROWS) == 0
        and mesh.shape["lat"] % (2 * ROWS) == 0
        and stiffness.shape[0] <= LANES
    )


def solution(mesh):
    in_specs = (P("lat", None, "lev", None), P("lat"), P(), P("lat", None, None), P("lat"), P())
    out_specs = P("lat", None, "lev", None)

    def program(grid, point_counts, waves, legendre, weights, stiffness):
        fits = fits_on_chip(mesh, grid, waves, stiffness)
        body = functools.partial(on_device, mesh) if fits else on_device_blocked
        return jax.shard_map(
            body, mesh=mesh, in_specs=in_specs, out_specs=out_specs, check_vma=False
        )(grid, point_counts, waves, legendre, weights, stiffness)

    return program
```

```python
import functools
import math

import jax
import jax.numpy as jnp
from jax import lax
from jax.experimental import pallas as pl
from jax.experimental.pallas import tpu as pltpu
from jax.sharding import PartitionSpec as P

TWO_PI = 2.0 * math.pi
FINE_STEPS = 32
LANES = 128
ROWS = 8
TABLE_BUDGET = 4 << 20
KERNEL_BYTES = 8 << 20

COS_TURN = (
    0.9999999998781397, -19.739208740145937, 64.9393888386778, -85.45665201444898,
    60.24205245141228, -26.404165331517056, 7.79855301354287, -1.4511773940976733,
)
SIN_TURN = (
    6.2831853022485955, -41.341700317335295, 81.60512671223316, -76.70292598092092,
    42.02516399730493, -14.896874459689428, 3.233831551278599,
)


def polynomial(coefficients, u):
    total = coefficients[-1] * u + coefficients[-2]
    for value in coefficients[-3::-1]:
        total = total * u + value
    return total


def cos_minus_sin(steps, count, inverse):
    reduced = steps - jnp.floor(steps * inverse + 0.5) * count
    turn = reduced * inverse
    square = turn * turn
    return polynomial(COS_TURN, square), -turn * polynomial(SIN_TURN, square)


def slot_choice(waves_ref, held, first, slots):
    width = waves_ref.shape[1]
    owners = slots // ROWS
    row = lax.broadcasted_iota(jnp.int32, (slots, width), 0)
    lane = lax.broadcasted_iota(jnp.int32, (slots, width), 1)
    place = row & (ROWS - 1)
    owner = (row >> 3) + first
    owner = jnp.where(owner >= owners, owner - owners, owner)
    chosen = (owner * held + place == lane) & (place < held)
    waves = jnp.broadcast_to(waves_ref[...].astype(jnp.float32) + 1.0, (slots, width))
    column = jnp.sum(jnp.where(chosen, waves, 0.0), axis=1, keepdims=True)
    mode = lax.broadcasted_iota(jnp.int32, (slots, LANES), 1).astype(jnp.float32) + 1.0
    return jnp.where(mode == column, 1.0, 0.0).astype(jnp.bfloat16)


def segments(start, length):
    done = 0
    while done < length:
        block, lane = divmod(start + done, LANES)
        size = min(length - done, LANES - lane)
        yield block, lane, done, size
        done += size


def turn(x, shift, axis):
    shift %= x.shape[axis]
    return pltpu.roll(x, shift, axis) if shift else x


def lane_row(lane, pieces, rows):
    out = []
    for block in range(-(-len(pieces) * rows // LANES)):
        total = jnp.zeros((1, LANES), jnp.float32)
        for j, piece in enumerate(pieces):
            start, stop = j * rows - block * LANES, (j + 1) * rows - block * LANES
            if start < LANES and stop > 0:
                total = jnp.where((lane >= start) & (lane < stop), piece, total)
        out.append(total)
    return out


def rest_home(c, held, rest):
    fit = LANES // rest
    return held + c // fit, (c % fit) * rest


def fold_rest(whole, part, held, rest):
    sublane = lax.broadcasted_iota(jnp.int32, (1, ROWS, LANES), 1)
    lane = lax.broadcasted_iota(jnp.int32, (1, ROWS, LANES), 2)
    for c in range(held):
        row, start = rest_home(c, held, rest)
        moved = turn(turn(part, row - c, 1), start, 2)
        here = (sublane == row) & (lane >= start) & (lane < start + rest)
        whole = jnp.where(here, moved, whole)
    return whole


def unfold_rest(whole, held, rest):
    sublane = lax.broadcasted_iota(jnp.int32, (1, ROWS, LANES), 1)
    part = whole
    for c in range(held):
        row, start = rest_home(c, held, rest)
        part = jnp.where(sublane == c, turn(turn(whole, c - row, 1), -start, 2), part)
    return part


def fill_tables(table_ref, width, least):
    candidates, _, padded = table_ref.shape
    blocks = padded // LANES
    sublane = lax.broadcasted_iota(jnp.int32, (ROWS, LANES), 0)
    lane = lax.broadcasted_iota(jnp.int32, (ROWS, LANES), 1)
    strides = (ROWS * (sublane * LANES + lane)).astype(jnp.float32)
    steps = [(sublane * (lane + b * LANES)).astype(jnp.float32) for b in range(blocks)]
    for i in range(candidates):
        count = jnp.full((1, LANES), (least + 4 * i).astype(jnp.float32))
        inverse = 1.0 / count
        stride_cos, stride_sin = cos_minus_sin(strides, count, inverse)
        for b in range(blocks):
            turn_cos, turn_sin = stride_cos[b : b + 1], stride_sin[b : b + 1]
            twice = turn_cos + turn_cos
            cosine, sine = cos_minus_sin(steps[b], count, inverse)
            cosines = [cosine, cosine * turn_cos - sine * turn_sin]
            sines = [sine, sine * turn_cos + cosine * turn_sin]
            while len(cosines) * ROWS < width:
                cosines.append(twice * cosines[-1] - cosines[-2])
                sines.append(twice * sines[-1] - sines[-2])
            at = pl.ds(b * LANES, LANES)
            table_ref[i, :width, at] = jnp.concatenate(cosines, axis=0).astype(jnp.bfloat16)
            table_ref[i, width:, at] = jnp.concatenate(sines, axis=0).astype(jnp.bfloat16)


def least_count(pairs):
    return 4 * pairs * lax.axis_index("lat") + 16


def candidate_of(count, j, least):
    return j + jnp.clip((count - least - 4 * j) >> 2, 0, 1)


def analysis_kernel(
    held, fields, first,
    counts_hbm, weights_hbm, waves_hbm, stiffness_hbm, basis_hbm, grid_hbm,
    coef_ref, table_ref, choice_ref, basis_ref, wave_ref, stiffness_ref, limit_ref,
    counts, weights, waves, levels, values, given, widened, arrived,
):
    owners, blocks = coef_ref.shape[:2]
    pairs = limit_ref.shape[0]
    slots = owners * ROWS
    width = basis_ref.shape[2]
    points = grid_hbm.shape[1]
    rows = grid_hbm.shape[0] // pairs
    rest = pairs * rows - blocks * LANES
    needed = [
        pltpu.make_async_copy(source, target, arrived.at[k])
        for k, (source, target) in enumerate(
            [(counts_hbm, counts), (waves_hbm, waves), (weights_hbm, weights),
             (stiffness_hbm, levels), (grid_hbm, values), (basis_hbm, given)]
        )
    ]
    for copy in needed:
        copy.start()
    least = least_count(pairs)
    fill_tables(table_ref, width, least)
    for copy in needed:
        copy.wait()
    choice = slot_choice(waves, held, first, slots)
    choice_ref[...] = choice
    widened[...] = given[...].astype(jnp.float32)
    for c in range(held):
        for j in range(pairs):
            strip = widened[c, pl.ds(j, owners, stride=pairs), :]
            basis_ref[c, j * owners : (j + 1) * owners, :] = turn(strip, -first, 0).astype(
                jnp.bfloat16
            )
    lane = lax.broadcasted_iota(jnp.int32, (1, LANES), 1)
    padding = jnp.zeros((1, LANES - width), jnp.float32)
    own_waves = jnp.concatenate([waves[...].astype(jnp.float32), padding], axis=1)
    own_waves = pltpu.roll(own_waves, (LANES - lax.axis_index("lat") * held) % LANES, 1)
    for c in range(held):
        wave_ref[c : c + 1, :] = jnp.broadcast_to(own_waves[:, c : c + 1], (1, LANES))
    all_levels = levels.shape[1]
    own = jnp.concatenate([levels[...], jnp.zeros((1, LANES - all_levels), jnp.float32)], axis=1)
    own = pltpu.roll(own, (LANES - lax.axis_index("lev") * fields) % LANES, 1)
    own = jnp.where(lane < fields, own, 0.0)
    stiffness = own
    for copy in range(1, 4):
        stiffness = stiffness + turn(own, copy * fields, 1)
    stiffness_ref[...] = stiffness
    position = lax.broadcasted_iota(jnp.int32, (1, points), 1)
    real, imaginary, ends, scales = [], [], [], []
    for j in range(pairs):
        count = jnp.full((1, LANES), counts[j].astype(jnp.float32))
        limit_ref[j : j + 1, :] = count
        ends.append(count)
        scales.append(jnp.full((1, LANES), weights[j]) / count)
        inside = jnp.where(position < counts[j], 1.0, 0.0).astype(jnp.bfloat16)
        latitude = values[j * rows : (j + 1) * rows, :] * inside
        product = lax.dot_general(
            table_ref[candidate_of(counts[j], j, least), :, :points],
            latitude,
            (((1,), (1,)), ((), ())),
            preferred_element_type=jnp.float32,
        )
        real.append(product[:width])
        imaginary.append(product[width:])
    end_rows = lane_row(lane, ends, rows)
    scale_rows = lane_row(lane, scales, rows)
    mode = lax.broadcasted_iota(jnp.int32, (width, 1), 0).astype(jnp.float32)
    tail = [jnp.zeros((width, LANES - rest), jnp.float32)] if rest else []
    for part, pieces in enumerate((real, imaginary)):
        whole = jnp.concatenate(pieces + tail, axis=1)
        cut = []
        for block, (end, scale) in enumerate(zip(end_rows, scale_rows)):
            strip = whole[:, block * LANES : (block + 1) * LANES]
            cut.append(jnp.where(2.0 * mode < end, strip * scale, 0.0).astype(jnp.bfloat16))
        placed = jnp.dot(
            choice[:, :width], jnp.concatenate(cut, axis=1), preferred_element_type=jnp.float32
        )
        cut = [
            placed[:, block * LANES : (block + 1) * LANES].reshape(owners, ROWS, LANES)
            for block in range(len(cut))
        ]
        if rest:
            cut[-2] = fold_rest(cut[-2], cut[-1], held, rest)
        for block in range(blocks):
            coef_ref[:, block, part] = cut[block].astype(jnp.bfloat16)


def legendre_kernel(
    held, fields, wave_ref, stiffness_ref, basis_ref, recv_ref, send_ref, fan_in, fan_out
):
    owners, blocks = recv_ref.shape[:2]
    latitudes, width = basis_ref.shape[1:]
    pairs = latitudes // owners
    rows = 2 * fields
    rest = pairs * rows - blocks * LANES
    chunk = blocks * 2 * ROWS
    fan_in[...] = recv_ref[...].astype(jnp.float32).reshape(owners * chunk, LANES)

    def chunk_rows(block, part, row):
        return pl.ds((block * 2 + part) * ROWS + row, owners, stride=chunk)

    def home(c, block, lane):
        if block == blocks:
            row, start = rest_home(c, held, rest)
            return row, block - 1, start + lane
        return c, block, lane

    lane_at = lax.broadcasted_iota(jnp.int32, (1, LANES), 1)
    south = ((lane_at >= fields) & (lane_at < 2 * fields)) | (lane_at >= 3 * fields)
    offset = lax.broadcasted_iota(jnp.int32, (width, 1), 0)
    parity = jnp.where((offset & 1) == 0, 1.0, -1.0)
    offset = offset.astype(jnp.float32)
    empty = jnp.zeros((owners, LANES), jnp.float32)
    folded = {}
    for c in range(held):
        wave = wave_ref[c : c + 1, :]
        degree = offset + wave
        basis = basis_ref[c]
        strips = []
        for j in range(pairs):
            strip = empty
            for part in range(2):
                for block, lane, place, size in segments(j * rows, rows):
                    row, block, lane = home(c, block, lane)
                    source = fan_in[chunk_rows(block, part, row), :]
                    target = part * rows + place
                    here = (lane_at >= target) & (lane_at < target + size)
                    strip = jnp.where(here, turn(source, target - lane, 1), strip)
            strips.append(strip.astype(jnp.bfloat16))
        spectra = lax.dot_general(
            basis,
            jnp.concatenate(strips, axis=0),
            (((0,), (0,)), ((), ())),
            preferred_element_type=jnp.float32,
        )
        factor = 1.0 / (1.0 + stiffness_ref[...] * degree * (degree + 1.0))
        damping = jnp.where(degree < float(width), factor, 0.0)
        other = jnp.where(south, turn(spectra, fields, 1), turn(spectra, -fields, 1))
        scaled = ((spectra + parity * other) * damping).astype(jnp.bfloat16)
        returned = jnp.dot(basis, scaled, preferred_element_type=jnp.float32)
        returned = returned * jnp.where(wave == 0.0, 1.0, 2.0)
        for part in range(2):
            built = {}
            for j in range(pairs):
                strip = returned[j * owners : (j + 1) * owners]
                for block, lane, place, size in segments(j * rows, rows):
                    row, block, lane = home(c, block, lane)
                    key = (block, part, row)
                    here = (lane_at >= lane) & (lane_at < lane + size)
                    moved = turn(strip, lane - part * rows - place, 1)
                    held_in = folded if row >= held else built
                    held_in[key] = jnp.where(here, moved, held_in.get(key, empty))
            for key, value in built.items():
                fan_out[chunk_rows(*key), :] = value
    for block in range(blocks):
        for part in range(2):
            for row in range(held, ROWS):
                key = (block, part, row)
                fan_out[chunk_rows(*key), :] = folded.get(key, empty)
    send_ref[...] = fan_out[...].astype(jnp.bfloat16).reshape(send_ref.shape)


def synthesis_kernel(
    held, limit_ref, choice_ref, recv_ref, table_ref, grid_hbm, values, left
):
    owners, blocks = recv_ref.shape[:2]
    pairs = limit_ref.shape[0]
    slots = owners * ROWS
    width = table_ref.shape[1] // 2
    points = grid_hbm.shape[1]
    rows = grid_hbm.shape[0] // pairs
    rest = pairs * rows - blocks * LANES
    least = least_count(pairs)
    choice = choice_ref[...]
    operands = []
    for part in range(2):
        cut = [recv_ref[:, block, part].astype(jnp.float32) for block in range(blocks)]
        if rest:
            cut.append(unfold_rest(cut[-1], held, rest))
        across = jnp.concatenate([strip.reshape(slots, LANES).T for strip in cut], axis=0)
        operands.append(
            jnp.dot(
                across[: pairs * rows].astype(jnp.bfloat16),
                choice,
                preferred_element_type=jnp.float32,
            )
        )
    position = lax.broadcasted_iota(jnp.int32, (1, points), 1).astype(jnp.float32)
    mode = lax.broadcasted_iota(jnp.int32, (1, LANES), 1).astype(jnp.float32)
    copies = []
    for j in range(pairs):
        end = limit_ref[j : j + 1, :]
        at = pl.ds(j * rows, rows)
        candidate = candidate_of(jnp.max(end).astype(jnp.int32), j, least)
        product = None
        for part in range(2):
            operand = operands[part][j * rows : (j + 1) * rows]
            operand = jnp.where(2.0 * mode < end, operand, 0.0).astype(jnp.bfloat16)
            term = jnp.dot(
                operand[:, :width],
                table_ref[candidate, part * width : (part + 1) * width, :],
                preferred_element_type=jnp.float32,
            )
            product = term if product is None else product + term
        kept = jnp.where(position < end[:, :1], product[:, :points], 0.0)
        values[at, :] = kept.astype(jnp.bfloat16)
        copies.append(pltpu.make_async_copy(values.at[at, :], grid_hbm.at[at, :], left.at[j]))
        copies[-1].start()
    for copy in copies:
        copy.wait()


def on_device(mesh, grid, point_counts, waves, legendre, weights, stiffness):
    pairs, _, fields, points = grid.shape
    width = waves.shape[0]
    owners = mesh.shape["lat"]
    held = width // owners
    slots = owners * ROWS
    rows = 2 * fields
    padded = -(-points // LANES) * LANES
    blocks = pairs * rows // LANES
    chunk = blocks * 2 * ROWS
    first = 5 * owners // 8
    groups = [[(place + first) % owners for place in range(owners)]]
    vmem = pl.BlockSpec(memory_space=pltpu.VMEM)
    hbm = pl.BlockSpec(memory_space=pltpu.HBM)
    limits = pltpu.CompilerParams(vmem_limit_bytes=KERNEL_BYTES)
    exchanged = jax.ShapeDtypeStruct((owners, blocks, 2, ROWS, LANES), jnp.bfloat16)
    coefficients, tables, choice, basis, wave_rows, levels, ends = pl.pallas_call(
        functools.partial(analysis_kernel, held, fields, first),
        out_shape=(
            exchanged,
            jax.ShapeDtypeStruct((pairs + 1, 2 * width, padded), jnp.bfloat16),
            jax.ShapeDtypeStruct((slots, LANES), jnp.bfloat16),
            jax.ShapeDtypeStruct(legendre.shape, jnp.bfloat16),
            jax.ShapeDtypeStruct((held, LANES), jnp.float32),
            jax.ShapeDtypeStruct((1, LANES), jnp.float32),
            jax.ShapeDtypeStruct((pairs, LANES), jnp.float32),
        ),
        in_specs=[hbm] * 6,
        out_specs=(vmem,) * 7,
        scratch_shapes=[
            pltpu.SMEM((pairs,), jnp.int32),
            pltpu.SMEM((pairs,), jnp.float32),
            pltpu.VMEM((1, width), jnp.int32),
            pltpu.VMEM((1, stiffness.shape[0]), jnp.float32),
            pltpu.VMEM((pairs * rows, points), jnp.bfloat16),
            pltpu.VMEM(legendre.shape, jnp.bfloat16),
            pltpu.VMEM(legendre.shape, jnp.float32),
            pltpu.SemaphoreType.DMA((6,)),
        ],
        compiler_params=limits,
        name="analysis",
    )(
        *(
            pltpu.with_memory_space_constraint(array, pltpu.HBM)
            for array in (
                point_counts, weights, waves.reshape(1, width), stiffness.reshape(1, -1), legendre,
                grid.reshape(pairs * rows, points),
            )
        )
    )

    def exchange(array):
        return lax.all_to_all(
            array, "lat", split_axis=0, concat_axis=0, axis_index_groups=groups, tiled=True
        )

    synthesised = pl.pallas_call(
        functools.partial(legendre_kernel, held, fields),
        out_shape=exchanged,
        in_specs=[vmem] * 4,
        out_specs=vmem,
        scratch_shapes=[
            pltpu.VMEM((owners * chunk, LANES), jnp.float32),
            pltpu.VMEM((owners * chunk, LANES), jnp.float32),
        ],
        compiler_params=limits,
        name="legendre",
    )(wave_rows, levels, basis, exchange(coefficients))
    result = pl.pallas_call(
        functools.partial(synthesis_kernel, held),
        out_shape=jax.ShapeDtypeStruct((pairs * rows, points), jnp.bfloat16),
        in_specs=[vmem] * 4,
        out_specs=hbm,
        scratch_shapes=[
            pltpu.VMEM((pairs * rows, points), jnp.bfloat16),
            pltpu.SemaphoreType.DMA((pairs,)),
        ],
        compiler_params=limits,
        name="synthesis",
    )(ends, choice, exchange(synthesised), tables)
    return result.reshape(grid.shape)


def fourier_tables(count, wavenumbers, quarter_max):
    quarter = count // 4
    step_angle = TWO_PI / quarter.astype(jnp.float32)
    coarse_count = (quarter_max + FINE_STEPS - 1) // FINE_STEPS
    coarse_pos = FINE_STEPS * jnp.arange(coarse_count, dtype=jnp.int32)
    fine_pos = jnp.arange(FINE_STEPS, dtype=jnp.int32)
    coarse_angle = (coarse_pos[:, None] * wavenumbers[None, :] % quarter).astype(
        jnp.float32
    ) * step_angle
    fine_angle = (fine_pos[:, None] * wavenumbers[None, :] % quarter).astype(
        jnp.float32
    ) * step_angle
    coarse_cos = jnp.cos(coarse_angle)[:, None, :]
    coarse_sin = jnp.sin(coarse_angle)[:, None, :]
    fine_cos = jnp.cos(fine_angle)[None, :, :]
    fine_sin = jnp.sin(fine_angle)[None, :, :]
    full_cos = (coarse_cos * fine_cos - coarse_sin * fine_sin).reshape(
        coarse_count * FINE_STEPS, -1
    )[:quarter_max]
    full_sin = (coarse_sin * fine_cos + coarse_cos * fine_sin).reshape(
        coarse_count * FINE_STEPS, -1
    )[:quarter_max]
    positions = jnp.arange(quarter_max, dtype=jnp.int32)
    inside = (positions < quarter)[:, None]
    cosine = jnp.where(inside, full_cos, 0.0)
    sine = jnp.where(inside, full_sin, 0.0)
    matrix = jnp.concatenate([cosine, sine], axis=1).astype(jnp.bfloat16)
    offsets = jnp.arange(4, dtype=jnp.int32)
    twist = offsets[:, None] * wavenumbers[None, :] % count
    theta = twist.astype(jnp.float32) * (TWO_PI / count.astype(jnp.float32))
    return (matrix, jnp.cos(theta), jnp.sin(theta))


def helmholtz(spectra, wavenumbers, offsets, stiffness_local, width):
    full_shape = spectra.shape
    quartered = spectra.reshape(full_shape[:-2] + (full_shape[-2] // 4, 2, 2, full_shape[-1]))
    parity = (1 - 2 * (offsets % 2)).astype(jnp.float32)
    combined = quartered[..., 0, :] + parity * quartered[..., 1, :]
    degrees = (wavenumbers + offsets).astype(jnp.float32)
    inside_band = offsets < width - wavenumbers
    factor = 1.0 / (
        1.0 + stiffness_local[:, None] * degrees[..., None, :] * (degrees[..., None, :] + 1.0)
    )
    damping = jnp.where(inside_band[..., None, :], factor, 0.0)
    scaled = (combined * damping[..., :, None, :]).astype(jnp.bfloat16)
    flipped = scaled * parity.astype(jnp.bfloat16)
    return jnp.stack([scaled, flipped], axis=-2).reshape(full_shape)


def spectral(received, wavenumbers, basis, stiffness_local):
    width = basis.shape[2]
    spectra = jnp.einsum("jcr,cjl->crl", received, basis, preferred_element_type=jnp.float32)
    offsets = jnp.arange(width, dtype=jnp.int32)
    operand = helmholtz(spectra, wavenumbers[:, None], offsets, stiffness_local, width)
    returned = jnp.einsum("crl,cjl->jcr", operand, basis, preferred_element_type=jnp.float32)
    return returned.astype(jnp.bfloat16)


def on_device_blocked(grid, point_counts, waves, legendre, weights, stiffness):
    pairs, _, fields, points = grid.shape
    quarter_max = points // 4
    width = waves.shape[0]
    held_slots = legendre.shape[0]
    lat_index = lax.axis_index("lat")
    lev_index = lax.axis_index("lev")

    def analyse(pieces):
        latitude, count, weight = pieces
        matrix, twist_cos, twist_sin = fourier_tables(count, waves, quarter_max)
        values = latitude.reshape(2, fields, quarter_max, 4)
        partial_value = jnp.einsum(
            "hfab,at->hfbt", values, matrix, preferred_element_type=jnp.float32
        )
        cos_part = partial_value[..., :width]
        sin_part = partial_value[..., width:]
        real = jnp.sum(twist_cos * cos_part - twist_sin * sin_part, axis=2)
        imag = -jnp.sum(twist_sin * cos_part + twist_cos * sin_part, axis=2)
        factor = jnp.where(2 * waves < count, weight / count.astype(jnp.float32), 0.0)
        stacked = jnp.stack([real * factor, imag * factor], axis=0)
        packed = jnp.transpose(stacked, (3, 2, 0, 1)).reshape(width, 4 * fields)
        return (packed.astype(jnp.bfloat16), matrix, twist_cos, twist_sin)

    coefficients, matrices, twist_cos, twist_sin = lax.map(analyse, (grid, point_counts, weights))
    received = lax.all_to_all(coefficients, "lat", split_axis=1, concat_axis=0, tiled=True)
    owned = lax.dynamic_slice_in_dim(waves, lat_index * held_slots, held_slots)
    own_stiffness = lax.dynamic_slice_in_dim(stiffness, lev_index * fields, fields)
    synthesised = spectral(received, owned, legendre, own_stiffness)
    returned = lax.all_to_all(synthesised, "lat", split_axis=0, concat_axis=1, tiled=True)

    def synthesise(pieces):
        packed, matrix, turn_cos, turn_sin, count = pieces
        values = packed.astype(jnp.float32).reshape(width, fields, 2, 2)
        real = values[:, :, 0, :]
        imag = values[:, :, 1, :]
        factor = jnp.where(2 * waves < count, jnp.where(waves == 0, 1.0, 2.0), 0.0)[:, None, None]
        cosines = turn_cos[:, :, None, None]
        sines = turn_sin[:, :, None, None]
        turned_real = factor * (real * cosines - imag * sines)
        turned_imag = factor * (real * sines + imag * cosines)
        operand = jnp.concatenate([turned_real, -turned_imag], axis=1)
        upper = operand.astype(jnp.bfloat16)
        lower = (operand - upper.astype(jnp.float32)).astype(jnp.bfloat16)
        result = jnp.einsum("bmfh,am->hfab", upper, matrix, preferred_element_type=jnp.float32)
        result = result + jnp.einsum(
            "bmfh,am->hfab", lower, matrix, preferred_element_type=jnp.float32
        )
        return result.reshape(2, fields, points).astype(jnp.bfloat16)

    return lax.map(synthesise, (returned, matrices, twist_cos, twist_sin, point_counts))


def fits_on_chip(mesh, grid, waves, stiffness):
    owners = mesh.shape["lat"]
    pairs, fields = grid.shape[0] // owners, grid.shape[2] // mesh.shape["lev"]
    width, points = waves.shape[0], grid.shape[3]
    held = width // owners
    lanes = 2 * pairs * fields
    rest = lanes % LANES
    return (
        width % owners == 0
        and width % (2 * ROWS) == 0
        and width <= LANES
        and 4 * (pairs + 1) * width * points <= TABLE_BUDGET
        and points <= ROWS * LANES
        and held <= ROWS
        and lanes >= LANES
        and (rest == 0 or held * rest <= (ROWS - held) * (LANES - LANES % rest))
        and 4 * fields <= LANES
        and fields % ROWS == 0
        and owners % (2 * ROWS) == 0
        and stiffness.shape[0] <= LANES
    )


def solution(mesh):
    in_specs = (P("lat", None, "lev", None), P("lat"), P(), P("lat", None, None), P("lat"), P())
    out_specs = P("lat", None, "lev", None)

    def program(grid, point_counts, waves, legendre, weights, stiffness):
        fits = fits_on_chip(mesh, grid, waves, stiffness)
        body = functools.partial(on_device, mesh) if fits else on_device_blocked
        return jax.shard_map(
            body, mesh=mesh, in_specs=in_specs, out_specs=out_specs, check_vma=False
        )(grid, point_counts, waves, legendre, weights, stiffness)

    return program
```

```python
import functools
import math

import jax
import jax.numpy as jnp
from jax import lax
from jax.experimental import pallas as pl
from jax.experimental.pallas import tpu as pltpu
from jax.sharding import PartitionSpec as P

TWO_PI = 2.0 * math.pi
FINE_STEPS = 32
LANES = 128
ROWS = 8
TABLE_BUDGET = 4 << 20
KERNEL_BYTES = 8 << 20

COS_TURN = (
    0.9999999998781397, -19.739208740145937, 64.9393888386778, -85.45665201444898,
    60.24205245141228, -26.404165331517056, 7.79855301354287, -1.4511773940976733,
)
SIN_TURN = (
    6.2831853022485955, -41.341700317335295, 81.60512671223316, -76.70292598092092,
    42.02516399730493, -14.896874459689428, 3.233831551278599,
)


def polynomial(coefficients, u):
    total = coefficients[-1] * u + coefficients[-2]
    for value in coefficients[-3::-1]:
        total = total * u + value
    return total


def cos_minus_sin(steps, count, inverse):
    reduced = steps - jnp.floor(steps * inverse + 0.5) * count
    turn = reduced * inverse
    square = turn * turn
    return polynomial(COS_TURN, square), -turn * polynomial(SIN_TURN, square)


def slot_choice(waves_ref, held, first, slots):
    width = waves_ref.shape[1]
    owners = slots // ROWS
    row = lax.broadcasted_iota(jnp.int32, (slots, width), 0)
    lane = lax.broadcasted_iota(jnp.int32, (slots, width), 1)
    place = row & (ROWS - 1)
    owner = (row >> 3) + first
    owner = jnp.where(owner >= owners, owner - owners, owner)
    chosen = (owner * held + place == lane) & (place < held)
    waves = jnp.broadcast_to(waves_ref[...].astype(jnp.float32) + 1.0, (slots, width))
    column = jnp.sum(jnp.where(chosen, waves, 0.0), axis=1, keepdims=True)
    mode = lax.broadcasted_iota(jnp.int32, (slots, LANES), 1).astype(jnp.float32) + 1.0
    return jnp.where(mode == column, 1.0, 0.0)


def segments(start, length):
    done = 0
    while done < length:
        block, lane = divmod(start + done, LANES)
        size = min(length - done, LANES - lane)
        yield block, lane, done, size
        done += size


def turn(x, shift, axis):
    shift %= x.shape[axis]
    return pltpu.roll(x, shift, axis) if shift else x


def lane_row(lane, pieces, rows):
    out = []
    for block in range(-(-len(pieces) * rows // LANES)):
        total = jnp.zeros((1, LANES), jnp.float32)
        for j, piece in enumerate(pieces):
            start, stop = j * rows - block * LANES, (j + 1) * rows - block * LANES
            if start < LANES and stop > 0:
                total = jnp.where((lane >= start) & (lane < stop), piece, total)
        out.append(total)
    return out


def rest_home(c, held, rest):
    fit = LANES // rest
    return held + c // fit, (c % fit) * rest


def rest_choices(choice, held, rest):
    owners = choice.shape[0] // ROWS
    grouped = choice.reshape(owners, ROWS, LANES)
    sublane = lax.broadcasted_iota(jnp.int32, (1, ROWS, LANES), 1)
    fit = LANES // rest
    out = []
    for group in range(min(fit, held)):
        total = jnp.zeros_like(grouped)
        for c in range(group, held, fit):
            row, _ = rest_home(c, held, rest)
            total = jnp.where(sublane == row, turn(grouped, row - c, 1), total)
        out.append(total.reshape(choice.shape))
    return out


def fill_tables(table_ref, width, least):
    candidates, _, padded = table_ref.shape
    blocks = padded // LANES
    sublane = lax.broadcasted_iota(jnp.int32, (ROWS, LANES), 0)
    lane = lax.broadcasted_iota(jnp.int32, (ROWS, LANES), 1)
    strides = (ROWS * (sublane * LANES + lane)).astype(jnp.float32)
    steps = [(sublane * (lane + b * LANES)).astype(jnp.float32) for b in range(blocks)]
    for i in range(candidates):
        count = jnp.full((1, LANES), (least + 4 * i).astype(jnp.float32))
        inverse = 1.0 / count
        stride_cos, stride_sin = cos_minus_sin(strides, count, inverse)
        for b in range(blocks):
            turn_cos, turn_sin = stride_cos[b : b + 1], stride_sin[b : b + 1]
            twice = turn_cos + turn_cos
            cosine, sine = cos_minus_sin(steps[b], count, inverse)
            cosines = [cosine, cosine * turn_cos - sine * turn_sin]
            sines = [sine, sine * turn_cos + cosine * turn_sin]
            while len(cosines) * ROWS < width:
                cosines.append(twice * cosines[-1] - cosines[-2])
                sines.append(twice * sines[-1] - sines[-2])
            at = pl.ds(b * LANES, LANES)
            table_ref[i, :width, at] = jnp.concatenate(cosines, axis=0).astype(jnp.bfloat16)
            table_ref[i, width:, at] = jnp.concatenate(sines, axis=0).astype(jnp.bfloat16)


def least_count(pairs):
    return 4 * pairs * lax.axis_index("lat") + 16


def candidate_of(count, j, least):
    return j + jnp.clip((count - least - 4 * j) >> 2, 0, 1)


def analysis_kernel(
    held, fields, first,
    counts_hbm, weights_hbm, waves_hbm, stiffness_hbm, basis_hbm, grid_hbm,
    coef_ref, table_ref, choice_ref, basis_ref, wave_ref, stiffness_ref, limit_ref,
    counts, weights, waves, levels, values, given, widened, arrived, grid_arrived,
):
    owners, blocks = coef_ref.shape[:2]
    pairs = limit_ref.shape[0]
    slots = owners * ROWS
    width = basis_ref.shape[2]
    points = grid_hbm.shape[1]
    rows = grid_hbm.shape[0] // pairs
    rest = pairs * rows - blocks * LANES
    small = [
        pltpu.make_async_copy(source, target, arrived.at[k])
        for k, (source, target) in enumerate(
            [(counts_hbm, counts), (waves_hbm, waves), (weights_hbm, weights), (stiffness_hbm, levels)]
        )
    ]
    latitudes = [pl.ds(j * rows, rows) for j in range(pairs)]
    fields_in = [pltpu.make_async_copy(grid_hbm, values, grid_arrived)]
    basis_in = pltpu.make_async_copy(basis_hbm, given, arrived.at[len(small)])
    for copy in (*fields_in, *small, basis_in):
        copy.start()
    least = least_count(pairs)
    fill_tables(table_ref, width, least)
    for copy in (*small, *fields_in, basis_in):
        copy.wait()
    choice = slot_choice(waves, held, first, slots)
    choices = [choice] + (rest_choices(choice, held, rest) if rest else [])
    choices = [each.astype(jnp.bfloat16) for each in choices]
    for k, each in enumerate(choices):
        choice_ref[k * slots : (k + 1) * slots, :] = each
    widened[...] = given[...].astype(jnp.float32)
    for c in range(held):
        for j in range(pairs):
            strip = widened[c, pl.ds(j, owners, stride=pairs), :]
            basis_ref[c, j * owners : (j + 1) * owners, :] = turn(strip, -first, 0).astype(
                jnp.bfloat16
            )
    lane = lax.broadcasted_iota(jnp.int32, (1, LANES), 1)
    padding = jnp.zeros((1, LANES - width), jnp.float32)
    own_waves = jnp.concatenate([waves[...].astype(jnp.float32), padding], axis=1)
    own_waves = pltpu.roll(own_waves, (LANES - lax.axis_index("lat") * held) % LANES, 1)
    for c in range(held):
        wave_ref[c : c + 1, :] = jnp.broadcast_to(own_waves[:, c : c + 1], (1, LANES))
    all_levels = levels.shape[1]
    own = jnp.concatenate([levels[...], jnp.zeros((1, LANES - all_levels), jnp.float32)], axis=1)
    own = pltpu.roll(own, (LANES - lax.axis_index("lev") * fields) % LANES, 1)
    own = jnp.where(lane < fields, own, 0.0)
    stiffness = own
    for copy in range(1, 4):
        stiffness = stiffness + turn(own, copy * fields, 1)
    stiffness_ref[...] = stiffness
    position = lax.broadcasted_iota(jnp.int32, (1, points), 1)
    real, imaginary, ends, scales = [], [], [], []
    for j in range(pairs):
        count = jnp.full((1, LANES), counts[j].astype(jnp.float32))
        limit_ref[j : j + 1, :] = count
        ends.append(count)
        scales.append(jnp.full((1, LANES), weights[j]) / count)
    end_rows = lane_row(lane, ends, rows)
    scale_rows = lane_row(lane, scales, rows)
    for j in range(pairs):
        inside = jnp.where(position < counts[j], 1.0, 0.0).astype(jnp.bfloat16)
        product = lax.dot_general(
            table_ref[candidate_of(counts[j], j, least), :, :points],
            values[latitudes[j], :] * inside,
            (((1,), (1,)), ((), ())),
            preferred_element_type=jnp.float32,
        )
        real.append(product[:width])
        imaginary.append(product[width:])
    mode = lax.broadcasted_iota(jnp.int32, (width, 1), 0).astype(jnp.float32)
    tail = [jnp.zeros((width, LANES - rest), jnp.float32)] if rest else []
    cut = [[] for _ in end_rows]
    for pieces in (real, imaginary):
        whole = jnp.concatenate(pieces + tail, axis=1)
        for block, (end, scale) in enumerate(zip(end_rows, scale_rows)):
            strip = whole[:, block * LANES : (block + 1) * LANES]
            cut[block].append(jnp.where(2.0 * mode < end, strip * scale, 0.0))
    cut = [jnp.concatenate(both, axis=1) for both in cut]
    unread = jnp.zeros((LANES - width, 2 * LANES), jnp.bfloat16)
    for block in range(blocks):
        taken, modes = [choices[0]], [cut[block].astype(jnp.bfloat16), unread]
        if rest and block == blocks - 1:
            for group, each in enumerate(choices[1:]):
                moved = [turn(cut[-1][:, k * LANES : (k + 1) * LANES], group * rest, 1) for k in range(2)]
                taken.append(each)
                modes += [jnp.concatenate(moved, axis=1).astype(jnp.bfloat16), unread]
        placed = jnp.dot(
            jnp.concatenate(taken, axis=1),
            jnp.concatenate(modes, axis=0),
            preferred_element_type=jnp.float32,
        )
        for part in range(2):
            strip = placed[:, part * LANES : (part + 1) * LANES]
            coef_ref[:, block, part] = strip.reshape(owners, ROWS, LANES).astype(jnp.bfloat16)


def legendre_kernel(
    held, fields, wave_ref, stiffness_ref, basis_ref, recv_ref, send_ref, fan_in, fan_out
):
    owners, blocks = recv_ref.shape[:2]
    latitudes, width = basis_ref.shape[1:]
    pairs = latitudes // owners
    rows = 2 * fields
    rest = pairs * rows - blocks * LANES
    for block in range(blocks):
        for part in range(2):
            plane = recv_ref[:, block, part].astype(jnp.float32).reshape(owners * ROWS, LANES)
            fan_in[block * 2 + part] = plane

    def chunk_rows(block, part, row):
        return block * 2 + part, pl.ds(row, owners, stride=ROWS), slice(None)

    def home(c, block, lane):
        if block == blocks:
            row, start = rest_home(c, held, rest)
            return row, block - 1, start + lane
        return c, block, lane

    lane_at = lax.broadcasted_iota(jnp.int32, (1, LANES), 1)
    south = ((lane_at >= fields) & (lane_at < 2 * fields)) | (lane_at >= 3 * fields)
    offset = lax.broadcasted_iota(jnp.int32, (width, 1), 0)
    parity = jnp.where((offset & 1) == 0, 1.0, -1.0)
    offset = offset.astype(jnp.float32)
    empty = jnp.zeros((owners, LANES), jnp.float32)
    folded = {}
    for c in range(held):
        wave = wave_ref[c : c + 1, :]
        degree = offset + wave
        basis = basis_ref[c]
        strips = []
        for j in range(pairs):
            strip = empty
            for part in range(2):
                for block, lane, place, size in segments(j * rows, rows):
                    row, block, lane = home(c, block, lane)
                    source = fan_in[chunk_rows(block, part, row)]
                    target = part * rows + place
                    here = (lane_at >= target) & (lane_at < target + size)
                    strip = jnp.where(here, turn(source, target - lane, 1), strip)
            strips.append(strip.astype(jnp.bfloat16))
        spectra = lax.dot_general(
            basis,
            jnp.concatenate(strips, axis=0),
            (((0,), (0,)), ((), ())),
            preferred_element_type=jnp.float32,
        )
        factor = 1.0 / (1.0 + stiffness_ref[...] * degree * (degree + 1.0))
        damping = jnp.where(degree < float(width), factor, 0.0)
        other = jnp.where(south, turn(spectra, fields, 1), turn(spectra, -fields, 1))
        scaled = ((spectra + parity * other) * damping).astype(jnp.bfloat16)
        returned = jnp.dot(basis, scaled, preferred_element_type=jnp.float32)
        returned = returned * jnp.where(wave == 0.0, 1.0, 2.0)
        for part in range(2):
            built = {}
            for j in range(pairs):
                strip = returned[j * owners : (j + 1) * owners]
                for block, lane, place, size in segments(j * rows, rows):
                    row, block, lane = home(c, block, lane)
                    key = (block, part, row)
                    here = (lane_at >= lane) & (lane_at < lane + size)
                    moved = turn(strip, lane - part * rows - place, 1)
                    held_in = folded if row >= held else built
                    held_in[key] = jnp.where(here, moved, held_in.get(key, empty))
            for key, value in built.items():
                fan_out[chunk_rows(*key)] = value
    for block in range(blocks):
        for part in range(2):
            for row in range(held, ROWS):
                key = (block, part, row)
                fan_out[chunk_rows(*key)] = folded.get(key, empty)
    for block in range(blocks):
        for part in range(2):
            plane = fan_out[block * 2 + part].reshape(owners, ROWS, LANES)
            send_ref[:, block, part] = plane.astype(jnp.bfloat16)


def synthesis_kernel(
    held, limit_ref, choice_ref, recv_ref, table_ref, grid_hbm, values, left
):
    owners, blocks = recv_ref.shape[:2]
    pairs = limit_ref.shape[0]
    slots = owners * ROWS
    width = table_ref.shape[1] // 2
    points = grid_hbm.shape[1]
    rows = grid_hbm.shape[0] // pairs
    rest = pairs * rows - blocks * LANES
    least = least_count(pairs)
    operands = []
    for part in range(2):
        turned = []
        for block in range(blocks):
            plane = recv_ref[:, block, part].astype(jnp.float32).reshape(slots, LANES)
            turned.append(plane.T.astype(jnp.bfloat16))
        found = [
            jnp.dot(
                jnp.concatenate(turned, axis=0),
                choice_ref[:slots, :],
                preferred_element_type=jnp.float32,
            )
        ]
        if rest:
            groups = choice_ref.shape[0] // slots - 1
            folded = [turned[-1][group * rest : (group + 1) * rest] for group in range(groups)]
            found.append(
                jnp.dot(
                    jnp.concatenate(folded, axis=1),
                    choice_ref[slots:, :],
                    preferred_element_type=jnp.float32,
                )
            )
        operands.append(jnp.concatenate(found, axis=0))
    position = lax.broadcasted_iota(jnp.int32, (1, points), 1).astype(jnp.float32)
    mode = lax.broadcasted_iota(jnp.int32, (1, LANES), 1).astype(jnp.float32)
    copies = []
    for j in range(pairs):
        end = limit_ref[j : j + 1, :]
        at = pl.ds(j * rows, rows)
        candidate = candidate_of(jnp.max(end).astype(jnp.int32), j, least)
        product = None
        for part in range(2):
            operand = operands[part][j * rows : (j + 1) * rows]
            operand = jnp.where(2.0 * mode < end, operand, 0.0).astype(jnp.bfloat16)
            term = jnp.dot(
                operand[:, :width],
                table_ref[candidate, part * width : (part + 1) * width, :],
                preferred_element_type=jnp.float32,
            )
            product = term if product is None else product + term
        kept = jnp.where(position < end[:, :1], product[:, :points], 0.0)
        values[at, :] = kept.astype(jnp.bfloat16)
        copies.append(pltpu.make_async_copy(values.at[at, :], grid_hbm.at[at, :], left.at[j]))
        copies[-1].start()
    for copy in copies:
        copy.wait()


def on_device(mesh, grid, point_counts, waves, legendre, weights, stiffness):
    pairs, _, fields, points = grid.shape
    width = waves.shape[0]
    owners = mesh.shape["lat"]
    held = width // owners
    slots = owners * ROWS
    rows = 2 * fields
    padded = -(-points // LANES) * LANES
    blocks = pairs * rows // LANES
    rest = pairs * rows % LANES
    choices = 1 + (min(LANES // rest, held) if rest else 0)
    first = 5 * owners // 8
    groups = [[(place + first) % owners for place in range(owners)]]
    vmem = pl.BlockSpec(memory_space=pltpu.VMEM)
    hbm = pl.BlockSpec(memory_space=pltpu.HBM)
    limits = pltpu.CompilerParams(vmem_limit_bytes=KERNEL_BYTES)
    exchanged = jax.ShapeDtypeStruct((owners, blocks, 2, ROWS, LANES), jnp.bfloat16)
    coefficients, tables, choice, basis, wave_rows, levels, ends = pl.pallas_call(
        functools.partial(analysis_kernel, held, fields, first),
        out_shape=(
            exchanged,
            jax.ShapeDtypeStruct((pairs + 1, 2 * width, padded), jnp.bfloat16),
            jax.ShapeDtypeStruct((choices * slots, LANES), jnp.bfloat16),
            jax.ShapeDtypeStruct(legendre.shape, jnp.bfloat16),
            jax.ShapeDtypeStruct((held, LANES), jnp.float32),
            jax.ShapeDtypeStruct((1, LANES), jnp.float32),
            jax.ShapeDtypeStruct((pairs, LANES), jnp.float32),
        ),
        in_specs=[hbm] * 6,
        out_specs=(vmem,) * 7,
        scratch_shapes=[
            pltpu.SMEM((pairs,), jnp.int32),
            pltpu.SMEM((pairs,), jnp.float32),
            pltpu.VMEM((1, width), jnp.int32),
            pltpu.VMEM((1, stiffness.shape[0]), jnp.float32),
            pltpu.VMEM((pairs * rows, points), jnp.bfloat16),
            pltpu.VMEM(legendre.shape, jnp.bfloat16),
            pltpu.VMEM(legendre.shape, jnp.float32),
            pltpu.SemaphoreType.DMA((5,)),
            pltpu.SemaphoreType.DMA,
        ],
        compiler_params=limits,
        name="analysis",
    )(
        *(
            pltpu.with_memory_space_constraint(array, pltpu.HBM)
            for array in (
                point_counts, weights, waves.reshape(1, width), stiffness.reshape(1, -1), legendre,
                grid.reshape(pairs * rows, points),
            )
        )
    )

    def exchange(array):
        return lax.all_to_all(
            array, "lat", split_axis=0, concat_axis=0, axis_index_groups=groups, tiled=True
        )

    synthesised = pl.pallas_call(
        functools.partial(legendre_kernel, held, fields),
        out_shape=exchanged,
        in_specs=[vmem] * 4,
        out_specs=vmem,
        scratch_shapes=[
            pltpu.VMEM((blocks * 2, slots, LANES), jnp.float32),
            pltpu.VMEM((blocks * 2, slots, LANES), jnp.float32),
        ],
        compiler_params=limits,
        name="legendre",
    )(wave_rows, levels, basis, exchange(coefficients))
    result = pl.pallas_call(
        functools.partial(synthesis_kernel, held),
        out_shape=jax.ShapeDtypeStruct((pairs * rows, points), jnp.bfloat16),
        in_specs=[vmem] * 4,
        out_specs=hbm,
        scratch_shapes=[
            pltpu.VMEM((pairs * rows, points), jnp.bfloat16),
            pltpu.SemaphoreType.DMA((pairs,)),
        ],
        compiler_params=limits,
        name="synthesis",
    )(ends, choice, exchange(synthesised), tables)
    return result.reshape(grid.shape)


def fourier_tables(count, wavenumbers, quarter_max):
    quarter = count // 4
    step_angle = TWO_PI / quarter.astype(jnp.float32)
    coarse_count = (quarter_max + FINE_STEPS - 1) // FINE_STEPS
    coarse_pos = FINE_STEPS * jnp.arange(coarse_count, dtype=jnp.int32)
    fine_pos = jnp.arange(FINE_STEPS, dtype=jnp.int32)
    coarse_angle = (coarse_pos[:, None] * wavenumbers[None, :] % quarter).astype(
        jnp.float32
    ) * step_angle
    fine_angle = (fine_pos[:, None] * wavenumbers[None, :] % quarter).astype(
        jnp.float32
    ) * step_angle
    coarse_cos = jnp.cos(coarse_angle)[:, None, :]
    coarse_sin = jnp.sin(coarse_angle)[:, None, :]
    fine_cos = jnp.cos(fine_angle)[None, :, :]
    fine_sin = jnp.sin(fine_angle)[None, :, :]
    full_cos = (coarse_cos * fine_cos - coarse_sin * fine_sin).reshape(
        coarse_count * FINE_STEPS, -1
    )[:quarter_max]
    full_sin = (coarse_sin * fine_cos + coarse_cos * fine_sin).reshape(
        coarse_count * FINE_STEPS, -1
    )[:quarter_max]
    positions = jnp.arange(quarter_max, dtype=jnp.int32)
    inside = (positions < quarter)[:, None]
    cosine = jnp.where(inside, full_cos, 0.0)
    sine = jnp.where(inside, full_sin, 0.0)
    matrix = jnp.concatenate([cosine, sine], axis=1).astype(jnp.bfloat16)
    offsets = jnp.arange(4, dtype=jnp.int32)
    twist = offsets[:, None] * wavenumbers[None, :] % count
    theta = twist.astype(jnp.float32) * (TWO_PI / count.astype(jnp.float32))
    return (matrix, jnp.cos(theta), jnp.sin(theta))


def helmholtz(spectra, wavenumbers, offsets, stiffness_local, width):
    full_shape = spectra.shape
    quartered = spectra.reshape(full_shape[:-2] + (full_shape[-2] // 4, 2, 2, full_shape[-1]))
    parity = (1 - 2 * (offsets % 2)).astype(jnp.float32)
    combined = quartered[..., 0, :] + parity * quartered[..., 1, :]
    degrees = (wavenumbers + offsets).astype(jnp.float32)
    inside_band = offsets < width - wavenumbers
    factor = 1.0 / (
        1.0 + stiffness_local[:, None] * degrees[..., None, :] * (degrees[..., None, :] + 1.0)
    )
    damping = jnp.where(inside_band[..., None, :], factor, 0.0)
    scaled = (combined * damping[..., :, None, :]).astype(jnp.bfloat16)
    flipped = scaled * parity.astype(jnp.bfloat16)
    return jnp.stack([scaled, flipped], axis=-2).reshape(full_shape)


def spectral(received, wavenumbers, basis, stiffness_local):
    width = basis.shape[2]
    spectra = jnp.einsum("jcr,cjl->crl", received, basis, preferred_element_type=jnp.float32)
    offsets = jnp.arange(width, dtype=jnp.int32)
    operand = helmholtz(spectra, wavenumbers[:, None], offsets, stiffness_local, width)
    returned = jnp.einsum("crl,cjl->jcr", operand, basis, preferred_element_type=jnp.float32)
    return returned.astype(jnp.bfloat16)


def on_device_blocked(grid, point_counts, waves, legendre, weights, stiffness):
    pairs, _, fields, points = grid.shape
    quarter_max = points // 4
    width = waves.shape[0]
    held_slots = legendre.shape[0]
    lat_index = lax.axis_index("lat")
    lev_index = lax.axis_index("lev")

    def analyse(pieces):
        latitude, count, weight = pieces
        matrix, twist_cos, twist_sin = fourier_tables(count, waves, quarter_max)
        values = latitude.reshape(2, fields, quarter_max, 4)
        partial_value = jnp.einsum(
            "hfab,at->hfbt", values, matrix, preferred_element_type=jnp.float32
        )
        cos_part = partial_value[..., :width]
        sin_part = partial_value[..., width:]
        real = jnp.sum(twist_cos * cos_part - twist_sin * sin_part, axis=2)
        imag = -jnp.sum(twist_sin * cos_part + twist_cos * sin_part, axis=2)
        factor = jnp.where(2 * waves < count, weight / count.astype(jnp.float32), 0.0)
        stacked = jnp.stack([real * factor, imag * factor], axis=0)
        packed = jnp.transpose(stacked, (3, 2, 0, 1)).reshape(width, 4 * fields)
        return (packed.astype(jnp.bfloat16), matrix, twist_cos, twist_sin)

    coefficients, matrices, twist_cos, twist_sin = lax.map(analyse, (grid, point_counts, weights))
    received = lax.all_to_all(coefficients, "lat", split_axis=1, concat_axis=0, tiled=True)
    owned = lax.dynamic_slice_in_dim(waves, lat_index * held_slots, held_slots)
    own_stiffness = lax.dynamic_slice_in_dim(stiffness, lev_index * fields, fields)
    synthesised = spectral(received, owned, legendre, own_stiffness)
    returned = lax.all_to_all(synthesised, "lat", split_axis=0, concat_axis=1, tiled=True)

    def synthesise(pieces):
        packed, matrix, turn_cos, turn_sin, count = pieces
        values = packed.astype(jnp.float32).reshape(width, fields, 2, 2)
        real = values[:, :, 0, :]
        imag = values[:, :, 1, :]
        factor = jnp.where(2 * waves < count, jnp.where(waves == 0, 1.0, 2.0), 0.0)[:, None, None]
        cosines = turn_cos[:, :, None, None]
        sines = turn_sin[:, :, None, None]
        turned_real = factor * (real * cosines - imag * sines)
        turned_imag = factor * (real * sines + imag * cosines)
        operand = jnp.concatenate([turned_real, -turned_imag], axis=1)
        upper = operand.astype(jnp.bfloat16)
        lower = (operand - upper.astype(jnp.float32)).astype(jnp.bfloat16)
        result = jnp.einsum("bmfh,am->hfab", upper, matrix, preferred_element_type=jnp.float32)
        result = result + jnp.einsum(
            "bmfh,am->hfab", lower, matrix, preferred_element_type=jnp.float32
        )
        return result.reshape(2, fields, points).astype(jnp.bfloat16)

    return lax.map(synthesise, (returned, matrices, twist_cos, twist_sin, point_counts))


def fits_on_chip(mesh, grid, waves, stiffness):
    owners = mesh.shape["lat"]
    pairs, fields = grid.shape[0] // owners, grid.shape[2] // mesh.shape["lev"]
    width, points = waves.shape[0], grid.shape[3]
    held = width // owners
    lanes = 2 * pairs * fields
    rest = lanes % LANES
    return (
        width % owners == 0
        and width % (2 * ROWS) == 0
        and width <= LANES
        and 4 * (pairs + 1) * width * points <= TABLE_BUDGET
        and points <= ROWS * LANES
        and held <= ROWS
        and lanes >= LANES
        and (rest == 0 or rest % (2 * ROWS) == 0)
        and (rest == 0 or held <= (ROWS - held) * (LANES // rest))
        and 4 * fields <= LANES
        and fields % ROWS == 0
        and owners % (2 * ROWS) == 0
        and stiffness.shape[0] <= LANES
    )


def solution(mesh):
    in_specs = (P("lat", None, "lev", None), P("lat"), P(), P("lat", None, None), P("lat"), P())
    out_specs = P("lat", None, "lev", None)

    def program(grid, point_counts, waves, legendre, weights, stiffness):
        fits = fits_on_chip(mesh, grid, waves, stiffness)
        body = functools.partial(on_device, mesh) if fits else on_device_blocked
        return jax.shard_map(
            body, mesh=mesh, in_specs=in_specs, out_specs=out_specs, check_vma=False
        )(grid, point_counts, waves, legendre, weights, stiffness)

    return program
```

```python
import functools
import math

import jax
import jax.numpy as jnp
from jax import lax
from jax.experimental import pallas as pl
from jax.experimental.pallas import tpu as pltpu
from jax.sharding import PartitionSpec as P

TWO_PI = 2.0 * math.pi
FINE_STEPS = 32
LANES = 128
ROWS = 8
TABLE_BUDGET = 4 << 20
KERNEL_BYTES = 8 << 20

COS_TURN = (
    0.9999999998781397, -19.739208740145937, 64.9393888386778, -85.45665201444898,
    60.24205245141228, -26.404165331517056, 7.79855301354287, -1.4511773940976733,
)
SIN_TURN = (
    6.2831853022485955, -41.341700317335295, 81.60512671223316, -76.70292598092092,
    42.02516399730493, -14.896874459689428, 3.233831551278599,
)


def polynomial(coefficients, u):
    total = coefficients[-1] * u + coefficients[-2]
    for value in coefficients[-3::-1]:
        total = total * u + value
    return total


def cos_minus_sin(steps, count, inverse):
    reduced = steps - jnp.floor(steps * inverse + 0.5) * count
    turn = reduced * inverse
    square = turn * turn
    return polynomial(COS_TURN, square), -turn * polynomial(SIN_TURN, square)


def slot_choice(waves_ref, held, first, slots):
    width = waves_ref.shape[1]
    owners = slots // ROWS
    row = lax.broadcasted_iota(jnp.int32, (slots, width), 0)
    lane = lax.broadcasted_iota(jnp.int32, (slots, width), 1)
    place = row & (ROWS - 1)
    owner = (row >> 3) + first
    owner = jnp.where(owner >= owners, owner - owners, owner)
    chosen = (owner * held + place == lane) & (place < held)
    waves = jnp.broadcast_to(waves_ref[...].astype(jnp.float32) + 1.0, (slots, width))
    column = jnp.sum(jnp.where(chosen, waves, 0.0), axis=1, keepdims=True)
    mode = lax.broadcasted_iota(jnp.int32, (slots, LANES), 1).astype(jnp.float32) + 1.0
    return jnp.where(mode == column, 1.0, 0.0)


def segments(start, length):
    done = 0
    while done < length:
        block, lane = divmod(start + done, LANES)
        size = min(length - done, LANES - lane)
        yield block, lane, done, size
        done += size


def turn(x, shift, axis):
    shift %= x.shape[axis]
    return pltpu.roll(x, shift, axis) if shift else x


def rest_home(c, held, rest):
    fit = LANES // rest
    return held + c // fit, (c % fit) * rest


def rest_choices(choice, held, rest):
    owners = choice.shape[0] // ROWS
    grouped = choice.reshape(owners, ROWS, LANES)
    sublane = lax.broadcasted_iota(jnp.int32, (1, ROWS, LANES), 1)
    fit = LANES // rest
    out = []
    for group in range(min(fit, held)):
        total = jnp.zeros_like(grouped)
        for c in range(group, held, fit):
            row, _ = rest_home(c, held, rest)
            total = jnp.where(sublane == row, turn(grouped, row - c, 1), total)
        out.append(total.reshape(choice.shape))
    return out


def fill_tables(table_ref, width, least):
    candidates, _, padded = table_ref.shape
    blocks = padded // LANES
    sublane = lax.broadcasted_iota(jnp.int32, (ROWS, LANES), 0)
    lane = lax.broadcasted_iota(jnp.int32, (ROWS, LANES), 1)
    strides = (ROWS * (sublane * LANES + lane)).astype(jnp.float32)
    steps = [(sublane * (lane + b * LANES)).astype(jnp.float32) for b in range(blocks)]
    for i in range(candidates):
        count = jnp.full((1, LANES), (least + 4 * i).astype(jnp.float32))
        inverse = 1.0 / count
        stride_cos, stride_sin = cos_minus_sin(strides, count, inverse)
        for b in range(blocks):
            turn_cos, turn_sin = stride_cos[b : b + 1], stride_sin[b : b + 1]
            twice = turn_cos + turn_cos
            cosine, sine = cos_minus_sin(steps[b], count, inverse)
            cosines = [cosine, cosine * turn_cos - sine * turn_sin]
            sines = [sine, sine * turn_cos + cosine * turn_sin]
            while len(cosines) * ROWS < width:
                cosines.append(twice * cosines[-1] - cosines[-2])
                sines.append(twice * sines[-1] - sines[-2])
            at = pl.ds(b * LANES, LANES)
            for part, values in enumerate((cosines, sines)):
                rows = pl.ds(part * width, width)
                table_ref[i, rows, at] = jnp.concatenate(values, axis=0).astype(jnp.bfloat16)


def fill_turned(turned_ref, least):
    candidates, points, _ = turned_ref.shape
    sublane = lax.broadcasted_iota(jnp.int32, (ROWS, LANES), 0)
    lane = lax.broadcasted_iota(jnp.int32, (ROWS, LANES), 1)
    strides = (ROWS * lane).astype(jnp.float32)
    for i in range(candidates):
        count = jnp.full((1, LANES), (least + 4 * i).astype(jnp.float32))
        inverse = 1.0 / count
        turn_cos, turn_sin = cos_minus_sin(strides, count, inverse)
        twice = turn_cos + turn_cos
        for start in range(0, points, LANES):
            rows = min(LANES, points - start)
            steps = ((sublane + start) * lane).astype(jnp.float32)
            cosine, sine = cos_minus_sin(steps, count, inverse)
            cosines = [cosine, cosine * turn_cos - sine * turn_sin]
            sines = [sine, sine * turn_cos + cosine * turn_sin]
            while len(cosines) * ROWS < rows:
                cosines.append(twice * cosines[-1] - cosines[-2])
                sines.append(twice * sines[-1] - sines[-2])
            for part, values in enumerate((cosines, sines)):
                at = pl.ds(start, rows), pl.ds(part * LANES, LANES)
                turned_ref[i, at[0], at[1]] = jnp.concatenate(values, axis=0).astype(jnp.bfloat16)


def least_count(pairs):
    return 4 * pairs * lax.axis_index("lat") + 16


def candidate_of(count, j, least):
    return j + jnp.clip((count - least - 4 * j) >> 2, 0, 1)


def analysis_kernel(
    held, fields, first,
    counts_hbm, weights_hbm, waves_hbm, stiffness_hbm, basis_hbm, grid_hbm,
    coef_ref, table_ref, choice_ref, basis_ref, wave_ref, stiffness_ref, limit_ref,
    counts, weights, waves, levels, values, given, widened, turned_ref, arrived, grid_arrived,
):
    owners, blocks = coef_ref.shape[:2]
    pairs = limit_ref.shape[0]
    slots = owners * ROWS
    width = basis_ref.shape[2]
    points = grid_hbm.shape[1]
    rows = grid_hbm.shape[0] // pairs
    rest = pairs * rows - blocks * LANES
    small = [
        pltpu.make_async_copy(source, target, arrived.at[k])
        for k, (source, target) in enumerate(
            [(counts_hbm, counts), (waves_hbm, waves), (weights_hbm, weights), (stiffness_hbm, levels)]
        )
    ]
    latitudes = [pl.ds(j * rows, rows) for j in range(pairs)]
    fields_in = [pltpu.make_async_copy(grid_hbm, values, grid_arrived)]
    basis_in = pltpu.make_async_copy(basis_hbm, given, arrived.at[len(small)])
    for copy in (*fields_in, *small, basis_in):
        copy.start()
    least = least_count(pairs)
    fill_turned(turned_ref, least)
    fill_tables(table_ref, width, least)
    for copy in (*small, *fields_in):
        copy.wait()
    choice = slot_choice(waves, held, first, slots)
    choices = [choice] + (rest_choices(choice, held, rest) if rest else [])
    choices = [each.astype(jnp.bfloat16) for each in choices]
    for k, each in enumerate(choices):
        choice_ref[k * slots : (k + 1) * slots, :] = each
    lane = lax.broadcasted_iota(jnp.int32, (1, LANES), 1)
    padding = jnp.zeros((1, LANES - width), jnp.float32)
    own_waves = jnp.concatenate([waves[...].astype(jnp.float32), padding], axis=1)
    own_waves = pltpu.roll(own_waves, (LANES - lax.axis_index("lat") * held) % LANES, 1)
    for c in range(held):
        wave_ref[c : c + 1, :] = jnp.broadcast_to(own_waves[:, c : c + 1], (1, LANES))
    all_levels = levels.shape[1]
    own = jnp.concatenate([levels[...], jnp.zeros((1, LANES - all_levels), jnp.float32)], axis=1)
    own = pltpu.roll(own, (LANES - lax.axis_index("lev") * fields) % LANES, 1)
    own = jnp.where(lane < fields, own, 0.0)
    stiffness = own
    for copy in range(1, 4):
        stiffness = stiffness + turn(own, copy * fields, 1)
    stiffness_ref[...] = stiffness
    position = lax.broadcasted_iota(jnp.int32, (1, points), 1)
    mode = lax.broadcasted_iota(jnp.int32, (1, 2 * LANES), 1) & (LANES - 1)
    pieces = []
    for j in range(pairs):
        limit_ref[j : j + 1, :] = jnp.full((1, LANES), counts[j].astype(jnp.float32))
        inside = jnp.where(position < counts[j], 1.0, 0.0).astype(jnp.bfloat16)
        product = jnp.dot(
            values[latitudes[j], :] * inside,
            turned_ref[candidate_of(counts[j], j, least)],
            preferred_element_type=jnp.float32,
        )
        scale = jnp.full((1, 1), weights[j]) / jnp.full((1, 1), counts[j].astype(jnp.float32))
        scale = jnp.where(2 * mode < counts[j], scale, 0.0)
        pieces.append((product * scale).astype(jnp.bfloat16))
    whole = jnp.concatenate(pieces, axis=0)
    parts = [whole[:, part * LANES : (part + 1) * LANES] for part in range(2)]
    for block in range(blocks):
        taken = [choices[0]]
        modes = [[part[block * LANES : (block + 1) * LANES] for part in parts]]
        if rest and block == blocks - 1:
            for group, each in enumerate(choices[1:]):
                taken.append(each)
                above = jnp.zeros((group * rest, LANES), jnp.bfloat16)
                below = jnp.zeros((LANES - (group + 1) * rest, LANES), jnp.bfloat16)
                modes.append(
                    [
                        jnp.concatenate(
                            [x for x in (above, part[blocks * LANES :], below) if x.shape[0]], axis=0
                        )
                        for part in parts
                    ]
                )
        placed = lax.dot_general(
            jnp.concatenate(taken, axis=1),
            jnp.concatenate([jnp.concatenate(both, axis=0) for both in modes], axis=1),
            (((1,), (1,)), ((), ())),
            preferred_element_type=jnp.float32,
        )
        for part in range(2):
            strip = placed[:, part * LANES : (part + 1) * LANES]
            coef_ref[:, block, part] = strip.reshape(owners, ROWS, LANES).astype(jnp.bfloat16)
    basis_in.wait()
    widened[...] = given[...].astype(jnp.float32)
    for c in range(held):
        for j in range(pairs):
            strip = widened[c, pl.ds(j, owners, stride=pairs), :]
            basis_ref[c, j * owners : (j + 1) * owners, :] = turn(strip, -first, 0).astype(
                jnp.bfloat16
            )


def legendre_kernel(
    held, fields, wave_ref, stiffness_ref, basis_ref, recv_ref, send_ref, fan_in, fan_out
):
    owners, blocks = recv_ref.shape[:2]
    latitudes, width = basis_ref.shape[1:]
    pairs = latitudes // owners
    rows = 2 * fields
    rest = pairs * rows - blocks * LANES
    for block in range(blocks):
        for part in range(2):
            plane = recv_ref[:, block, part].astype(jnp.float32).reshape(owners * ROWS, LANES)
            fan_in[block * 2 + part] = plane

    def chunk_rows(block, part, row):
        return block * 2 + part, pl.ds(row, owners, stride=ROWS), slice(None)

    def home(c, block, lane):
        if block == blocks:
            row, start = rest_home(c, held, rest)
            return row, block - 1, start + lane
        return c, block, lane

    lane_at = lax.broadcasted_iota(jnp.int32, (1, LANES), 1)
    south = ((lane_at >= fields) & (lane_at < 2 * fields)) | (lane_at >= 3 * fields)
    offset = lax.broadcasted_iota(jnp.int32, (width, 1), 0)
    parity = jnp.where((offset & 1) == 0, 1.0, -1.0)
    offset = offset.astype(jnp.float32)
    empty = jnp.zeros((owners, LANES), jnp.float32)
    folded = {}
    for c in range(held):
        wave = wave_ref[c : c + 1, :]
        degree = offset + wave
        basis = basis_ref[c]
        strips = []
        for j in range(pairs):
            strip = empty
            for part in range(2):
                for block, lane, place, size in segments(j * rows, rows):
                    row, block, lane = home(c, block, lane)
                    source = fan_in[chunk_rows(block, part, row)]
                    target = part * rows + place
                    here = (lane_at >= target) & (lane_at < target + size)
                    strip = jnp.where(here, turn(source, target - lane, 1), strip)
            strips.append(strip.astype(jnp.bfloat16))
        spectra = lax.dot_general(
            basis,
            jnp.concatenate(strips, axis=0),
            (((0,), (0,)), ((), ())),
            preferred_element_type=jnp.float32,
        )
        factor = 1.0 / (1.0 + stiffness_ref[...] * degree * (degree + 1.0))
        damping = jnp.where(degree < float(width), factor, 0.0)
        other = jnp.where(south, turn(spectra, fields, 1), turn(spectra, -fields, 1))
        scaled = ((spectra + parity * other) * damping).astype(jnp.bfloat16)
        returned = jnp.dot(basis, scaled, preferred_element_type=jnp.float32)
        returned = returned * jnp.where(wave == 0.0, 1.0, 2.0)
        for part in range(2):
            built = {}
            for j in range(pairs):
                strip = returned[j * owners : (j + 1) * owners]
                for block, lane, place, size in segments(j * rows, rows):
                    row, block, lane = home(c, block, lane)
                    key = (block, part, row)
                    here = (lane_at >= lane) & (lane_at < lane + size)
                    moved = turn(strip, lane - part * rows - place, 1)
                    held_in = folded if row >= held else built
                    held_in[key] = jnp.where(here, moved, held_in.get(key, empty))
            for key, value in built.items():
                fan_out[chunk_rows(*key)] = value
    for block in range(blocks):
        for part in range(2):
            for row in range(held, ROWS):
                key = (block, part, row)
                fan_out[chunk_rows(*key)] = folded.get(key, empty)
    for block in range(blocks):
        for part in range(2):
            plane = fan_out[block * 2 + part].reshape(owners, ROWS, LANES)
            send_ref[:, block, part] = plane.astype(jnp.bfloat16)


def synthesis_kernel(
    held, limit_ref, choice_ref, recv_ref, table_ref, grid_hbm, values, left
):
    owners, blocks = recv_ref.shape[:2]
    pairs = limit_ref.shape[0]
    slots = owners * ROWS
    width = table_ref.shape[1] // 2
    points = grid_hbm.shape[1]
    rows = grid_hbm.shape[0] // pairs
    rest = pairs * rows - blocks * LANES
    least = least_count(pairs)
    operands = []
    for part in range(2):
        turned = []
        for block in range(blocks):
            plane = recv_ref[:, block, part].astype(jnp.float32).reshape(slots, LANES)
            turned.append(plane.T.astype(jnp.bfloat16))
        found = [
            jnp.dot(
                jnp.concatenate(turned, axis=0),
                choice_ref[:slots, :],
                preferred_element_type=jnp.float32,
            )
        ]
        if rest:
            groups = choice_ref.shape[0] // slots - 1
            folded = [turned[-1][group * rest : (group + 1) * rest] for group in range(groups)]
            found.append(
                jnp.dot(
                    jnp.concatenate(folded, axis=1),
                    choice_ref[slots:, :],
                    preferred_element_type=jnp.float32,
                )
            )
        operands.append(jnp.concatenate(found, axis=0))
    position = lax.broadcasted_iota(jnp.int32, (1, points), 1).astype(jnp.float32)
    mode = lax.broadcasted_iota(jnp.int32, (1, LANES), 1).astype(jnp.float32)
    copies = []
    for j in range(pairs):
        end = limit_ref[j : j + 1, :]
        at = pl.ds(j * rows, rows)
        candidate = candidate_of(jnp.max(end).astype(jnp.int32), j, least)
        product = None
        for part in range(2):
            operand = operands[part][j * rows : (j + 1) * rows]
            operand = jnp.where(2.0 * mode < end, operand, 0.0).astype(jnp.bfloat16)
            term = jnp.dot(
                operand[:, :width],
                table_ref[candidate, part * width : (part + 1) * width, :],
                preferred_element_type=jnp.float32,
            )
            product = term if product is None else product + term
        kept = jnp.where(position < end[:, :1], product[:, :points], 0.0)
        values[at, :] = kept.astype(jnp.bfloat16)
        copies.append(pltpu.make_async_copy(values.at[at, :], grid_hbm.at[at, :], left.at[j]))
        copies[-1].start()
    for copy in copies:
        copy.wait()


def on_device(mesh, grid, point_counts, waves, legendre, weights, stiffness):
    pairs, _, fields, points = grid.shape
    width = waves.shape[0]
    owners = mesh.shape["lat"]
    held = width // owners
    slots = owners * ROWS
    rows = 2 * fields
    padded = -(-points // LANES) * LANES
    blocks = pairs * rows // LANES
    rest = pairs * rows % LANES
    choices = 1 + (min(LANES // rest, held) if rest else 0)
    first = 5 * owners // 8
    groups = [[(place + first) % owners for place in range(owners)]]
    vmem = pl.BlockSpec(memory_space=pltpu.VMEM)
    hbm = pl.BlockSpec(memory_space=pltpu.HBM)
    limits = pltpu.CompilerParams(vmem_limit_bytes=KERNEL_BYTES)
    exchanged = jax.ShapeDtypeStruct((owners, blocks, 2, ROWS, LANES), jnp.bfloat16)
    coefficients, tables, choice, basis, wave_rows, levels, ends = pl.pallas_call(
        functools.partial(analysis_kernel, held, fields, first),
        out_shape=(
            exchanged,
            jax.ShapeDtypeStruct((pairs + 1, 2 * width, padded), jnp.bfloat16),
            jax.ShapeDtypeStruct((choices * slots, LANES), jnp.bfloat16),
            jax.ShapeDtypeStruct(legendre.shape, jnp.bfloat16),
            jax.ShapeDtypeStruct((held, LANES), jnp.float32),
            jax.ShapeDtypeStruct((1, LANES), jnp.float32),
            jax.ShapeDtypeStruct((pairs, LANES), jnp.float32),
        ),
        in_specs=[hbm] * 6,
        out_specs=(vmem,) * 7,
        scratch_shapes=[
            pltpu.SMEM((pairs,), jnp.int32),
            pltpu.SMEM((pairs,), jnp.float32),
            pltpu.VMEM((1, width), jnp.int32),
            pltpu.VMEM((1, stiffness.shape[0]), jnp.float32),
            pltpu.VMEM((pairs * rows, points), jnp.bfloat16),
            pltpu.VMEM(legendre.shape, jnp.bfloat16),
            pltpu.VMEM(legendre.shape, jnp.float32),
            pltpu.VMEM((pairs + 1, points, 2 * LANES), jnp.bfloat16),
            pltpu.SemaphoreType.DMA((5,)),
            pltpu.SemaphoreType.DMA,
        ],
        compiler_params=limits,
        name="analysis",
    )(
        *(
            pltpu.with_memory_space_constraint(array, pltpu.HBM)
            for array in (
                point_counts, weights, waves.reshape(1, width), stiffness.reshape(1, -1), legendre,
                grid.reshape(pairs * rows, points),
            )
        )
    )

    def exchange(array):
        return lax.all_to_all(
            array, "lat", split_axis=0, concat_axis=0, axis_index_groups=groups, tiled=True
        )

    synthesised = pl.pallas_call(
        functools.partial(legendre_kernel, held, fields),
        out_shape=exchanged,
        in_specs=[vmem] * 4,
        out_specs=vmem,
        scratch_shapes=[
            pltpu.VMEM((blocks * 2, slots, LANES), jnp.float32),
            pltpu.VMEM((blocks * 2, slots, LANES), jnp.float32),
        ],
        compiler_params=limits,
        name="legendre",
    )(wave_rows, levels, basis, exchange(coefficients))
    result = pl.pallas_call(
        functools.partial(synthesis_kernel, held),
        out_shape=jax.ShapeDtypeStruct((pairs * rows, points), jnp.bfloat16),
        in_specs=[vmem] * 4,
        out_specs=hbm,
        scratch_shapes=[
            pltpu.VMEM((pairs * rows, points), jnp.bfloat16),
            pltpu.SemaphoreType.DMA((pairs,)),
        ],
        compiler_params=limits,
        name="synthesis",
    )(ends, choice, exchange(synthesised), tables)
    return result.reshape(grid.shape)


def fourier_tables(count, wavenumbers, quarter_max):
    quarter = count // 4
    step_angle = TWO_PI / quarter.astype(jnp.float32)
    coarse_count = (quarter_max + FINE_STEPS - 1) // FINE_STEPS
    coarse_pos = FINE_STEPS * jnp.arange(coarse_count, dtype=jnp.int32)
    fine_pos = jnp.arange(FINE_STEPS, dtype=jnp.int32)
    coarse_angle = (coarse_pos[:, None] * wavenumbers[None, :] % quarter).astype(
        jnp.float32
    ) * step_angle
    fine_angle = (fine_pos[:, None] * wavenumbers[None, :] % quarter).astype(
        jnp.float32
    ) * step_angle
    coarse_cos = jnp.cos(coarse_angle)[:, None, :]
    coarse_sin = jnp.sin(coarse_angle)[:, None, :]
    fine_cos = jnp.cos(fine_angle)[None, :, :]
    fine_sin = jnp.sin(fine_angle)[None, :, :]
    full_cos = (coarse_cos * fine_cos - coarse_sin * fine_sin).reshape(
        coarse_count * FINE_STEPS, -1
    )[:quarter_max]
    full_sin = (coarse_sin * fine_cos + coarse_cos * fine_sin).reshape(
        coarse_count * FINE_STEPS, -1
    )[:quarter_max]
    positions = jnp.arange(quarter_max, dtype=jnp.int32)
    inside = (positions < quarter)[:, None]
    cosine = jnp.where(inside, full_cos, 0.0)
    sine = jnp.where(inside, full_sin, 0.0)
    matrix = jnp.concatenate([cosine, sine], axis=1).astype(jnp.bfloat16)
    offsets = jnp.arange(4, dtype=jnp.int32)
    twist = offsets[:, None] * wavenumbers[None, :] % count
    theta = twist.astype(jnp.float32) * (TWO_PI / count.astype(jnp.float32))
    return (matrix, jnp.cos(theta), jnp.sin(theta))


def helmholtz(spectra, wavenumbers, offsets, stiffness_local, width):
    full_shape = spectra.shape
    quartered = spectra.reshape(full_shape[:-2] + (full_shape[-2] // 4, 2, 2, full_shape[-1]))
    parity = (1 - 2 * (offsets % 2)).astype(jnp.float32)
    combined = quartered[..., 0, :] + parity * quartered[..., 1, :]
    degrees = (wavenumbers + offsets).astype(jnp.float32)
    inside_band = offsets < width - wavenumbers
    factor = 1.0 / (
        1.0 + stiffness_local[:, None] * degrees[..., None, :] * (degrees[..., None, :] + 1.0)
    )
    damping = jnp.where(inside_band[..., None, :], factor, 0.0)
    scaled = (combined * damping[..., :, None, :]).astype(jnp.bfloat16)
    flipped = scaled * parity.astype(jnp.bfloat16)
    return jnp.stack([scaled, flipped], axis=-2).reshape(full_shape)


def spectral(received, wavenumbers, basis, stiffness_local):
    width = basis.shape[2]
    spectra = jnp.einsum("jcr,cjl->crl", received, basis, preferred_element_type=jnp.float32)
    offsets = jnp.arange(width, dtype=jnp.int32)
    operand = helmholtz(spectra, wavenumbers[:, None], offsets, stiffness_local, width)
    returned = jnp.einsum("crl,cjl->jcr", operand, basis, preferred_element_type=jnp.float32)
    return returned.astype(jnp.bfloat16)


def on_device_blocked(grid, point_counts, waves, legendre, weights, stiffness):
    pairs, _, fields, points = grid.shape
    quarter_max = points // 4
    width = waves.shape[0]
    held_slots = legendre.shape[0]
    lat_index = lax.axis_index("lat")
    lev_index = lax.axis_index("lev")

    def analyse(pieces):
        latitude, count, weight = pieces
        matrix, twist_cos, twist_sin = fourier_tables(count, waves, quarter_max)
        values = latitude.reshape(2, fields, quarter_max, 4)
        partial_value = jnp.einsum(
            "hfab,at->hfbt", values, matrix, preferred_element_type=jnp.float32
        )
        cos_part = partial_value[..., :width]
        sin_part = partial_value[..., width:]
        real = jnp.sum(twist_cos * cos_part - twist_sin * sin_part, axis=2)
        imag = -jnp.sum(twist_sin * cos_part + twist_cos * sin_part, axis=2)
        factor = jnp.where(2 * waves < count, weight / count.astype(jnp.float32), 0.0)
        stacked = jnp.stack([real * factor, imag * factor], axis=0)
        packed = jnp.transpose(stacked, (3, 2, 0, 1)).reshape(width, 4 * fields)
        return (packed.astype(jnp.bfloat16), matrix, twist_cos, twist_sin)

    coefficients, matrices, twist_cos, twist_sin = lax.map(analyse, (grid, point_counts, weights))
    received = lax.all_to_all(coefficients, "lat", split_axis=1, concat_axis=0, tiled=True)
    owned = lax.dynamic_slice_in_dim(waves, lat_index * held_slots, held_slots)
    own_stiffness = lax.dynamic_slice_in_dim(stiffness, lev_index * fields, fields)
    synthesised = spectral(received, owned, legendre, own_stiffness)
    returned = lax.all_to_all(synthesised, "lat", split_axis=0, concat_axis=1, tiled=True)

    def synthesise(pieces):
        packed, matrix, turn_cos, turn_sin, count = pieces
        values = packed.astype(jnp.float32).reshape(width, fields, 2, 2)
        real = values[:, :, 0, :]
        imag = values[:, :, 1, :]
        factor = jnp.where(2 * waves < count, jnp.where(waves == 0, 1.0, 2.0), 0.0)[:, None, None]
        cosines = turn_cos[:, :, None, None]
        sines = turn_sin[:, :, None, None]
        turned_real = factor * (real * cosines - imag * sines)
        turned_imag = factor * (real * sines + imag * cosines)
        operand = jnp.concatenate([turned_real, -turned_imag], axis=1)
        upper = operand.astype(jnp.bfloat16)
        lower = (operand - upper.astype(jnp.float32)).astype(jnp.bfloat16)
        result = jnp.einsum("bmfh,am->hfab", upper, matrix, preferred_element_type=jnp.float32)
        result = result + jnp.einsum(
            "bmfh,am->hfab", lower, matrix, preferred_element_type=jnp.float32
        )
        return result.reshape(2, fields, points).astype(jnp.bfloat16)

    return lax.map(synthesise, (returned, matrices, twist_cos, twist_sin, point_counts))


def fits_on_chip(mesh, grid, waves, stiffness):
    owners = mesh.shape["lat"]
    pairs, fields = grid.shape[0] // owners, grid.shape[2] // mesh.shape["lev"]
    width, points = waves.shape[0], grid.shape[3]
    held = width // owners
    lanes = 2 * pairs * fields
    rest = lanes % LANES
    return (
        width % owners == 0
        and width % (2 * ROWS) == 0
        and width <= LANES
        and 4 * (pairs + 1) * LANES * points <= TABLE_BUDGET
        and points <= ROWS * LANES
        and points % (2 * ROWS) == 0
        and held <= ROWS
        and lanes >= LANES
        and (rest == 0 or rest % (2 * ROWS) == 0)
        and (rest == 0 or held <= (ROWS - held) * (LANES // rest))
        and 4 * fields <= LANES
        and fields % ROWS == 0
        and owners % (2 * ROWS) == 0
        and stiffness.shape[0] <= LANES
    )


def solution(mesh):
    in_specs = (P("lat", None, "lev", None), P("lat"), P(), P("lat", None, None), P("lat"), P())
    out_specs = P("lat", None, "lev", None)

    def program(grid, point_counts, waves, legendre, weights, stiffness):
        fits = fits_on_chip(mesh, grid, waves, stiffness)
        body = functools.partial(on_device, mesh) if fits else on_device_blocked
        return jax.shard_map(
            body, mesh=mesh, in_specs=in_specs, out_specs=out_specs, check_vma=False
        )(grid, point_counts, waves, legendre, weights, stiffness)

    return program
```

```python
import functools
import math

import jax
import jax.numpy as jnp
from jax import lax
from jax.experimental import pallas as pl
from jax.experimental.pallas import tpu as pltpu
from jax.sharding import PartitionSpec as P

TWO_PI = 2.0 * math.pi
FINE_STEPS = 32
LANES = 128
ROWS = 8
TABLE_BUDGET = 4 << 20
KERNEL_BYTES = 8 << 20

COS_TURN = (
    0.9999999998781397, -19.739208740145937, 64.9393888386778, -85.45665201444898,
    60.24205245141228, -26.404165331517056, 7.79855301354287, -1.4511773940976733,
)
SIN_TURN = (
    6.2831853022485955, -41.341700317335295, 81.60512671223316, -76.70292598092092,
    42.02516399730493, -14.896874459689428, 3.233831551278599,
)


def polynomial(coefficients, u):
    total = coefficients[-1] * u + coefficients[-2]
    for value in coefficients[-3::-1]:
        total = total * u + value
    return total


def cos_minus_sin(steps, count, inverse):
    reduced = steps - jnp.floor(steps * inverse + 0.5) * count
    turn = reduced * inverse
    square = turn * turn
    return polynomial(COS_TURN, square), -turn * polynomial(SIN_TURN, square)


def slot_choice(waves_ref, held, first, slots):
    width = waves_ref.shape[1]
    owners = slots // ROWS
    row = lax.broadcasted_iota(jnp.int32, (slots, width), 0)
    lane = lax.broadcasted_iota(jnp.int32, (slots, width), 1)
    place = row & (ROWS - 1)
    owner = (row >> 3) + first
    owner = jnp.where(owner >= owners, owner - owners, owner)
    chosen = (owner * held + place == lane) & (place < held)
    waves = jnp.broadcast_to(waves_ref[...].astype(jnp.float32) + 1.0, (slots, width))
    column = jnp.sum(jnp.where(chosen, waves, 0.0), axis=1, keepdims=True)
    mode = lax.broadcasted_iota(jnp.int32, (slots, LANES), 1).astype(jnp.float32) + 1.0
    return jnp.where(mode == column, 1.0, 0.0)


def segments(start, length):
    done = 0
    while done < length:
        block, lane = divmod(start + done, LANES)
        size = min(length - done, LANES - lane)
        yield block, lane, done, size
        done += size


def turn(x, shift, axis):
    shift %= x.shape[axis]
    return pltpu.roll(x, shift, axis) if shift else x


def rest_home(c, held, rest):
    fit = LANES // rest
    return held + c // fit, (c % fit) * rest


def rest_choices(choice, held, rest):
    owners = choice.shape[0] // ROWS
    grouped = choice.reshape(owners, ROWS, LANES)
    sublane = lax.broadcasted_iota(jnp.int32, (1, ROWS, LANES), 1)
    fit = LANES // rest
    out = []
    for group in range(min(fit, held)):
        total = jnp.zeros_like(grouped)
        for c in range(group, held, fit):
            row, _ = rest_home(c, held, rest)
            total = jnp.where(sublane == row, turn(grouped, row - c, 1), total)
        out.append(total.reshape(choice.shape))
    return out


def fill_tables(table_ref, width, least):
    candidates, _, padded = table_ref.shape
    blocks = padded // LANES
    sublane = lax.broadcasted_iota(jnp.int32, (ROWS, LANES), 0)
    lane = lax.broadcasted_iota(jnp.int32, (ROWS, LANES), 1)
    strides = (ROWS * (sublane * LANES + lane)).astype(jnp.float32)
    steps = [(sublane * (lane + b * LANES)).astype(jnp.float32) for b in range(blocks)]
    for i in range(candidates):
        count = jnp.full((1, LANES), (least + 4 * i).astype(jnp.float32))
        inverse = 1.0 / count
        stride_cos, stride_sin = cos_minus_sin(strides, count, inverse)
        for b in range(blocks):
            turn_cos, turn_sin = stride_cos[b : b + 1], stride_sin[b : b + 1]
            twice = turn_cos + turn_cos
            cosine, sine = cos_minus_sin(steps[b], count, inverse)
            cosines = [cosine, cosine * turn_cos - sine * turn_sin]
            sines = [sine, sine * turn_cos + cosine * turn_sin]
            while len(cosines) * ROWS < width:
                cosines.append(twice * cosines[-1] - cosines[-2])
                sines.append(twice * sines[-1] - sines[-2])
            at = pl.ds(b * LANES, LANES)
            for part, values in enumerate((cosines, sines)):
                rows = pl.ds(part * width, width)
                table_ref[i, rows, at] = jnp.concatenate(values, axis=0).astype(jnp.bfloat16)


def fill_turned(turned_ref, least):
    candidates, points, _ = turned_ref.shape
    sublane = lax.broadcasted_iota(jnp.int32, (ROWS, LANES), 0)
    lane = lax.broadcasted_iota(jnp.int32, (ROWS, LANES), 1)
    strides = (ROWS * lane).astype(jnp.float32)
    for i in range(candidates):
        count = jnp.full((1, LANES), (least + 4 * i).astype(jnp.float32))
        inverse = 1.0 / count
        turn_cos, turn_sin = cos_minus_sin(strides, count, inverse)
        twice = turn_cos + turn_cos
        for start in range(0, points, LANES):
            rows = min(LANES, points - start)
            steps = ((sublane + start) * lane).astype(jnp.float32)
            cosine, sine = cos_minus_sin(steps, count, inverse)
            cosines = [cosine, cosine * turn_cos - sine * turn_sin]
            sines = [sine, sine * turn_cos + cosine * turn_sin]
            while len(cosines) * ROWS < rows:
                cosines.append(twice * cosines[-1] - cosines[-2])
                sines.append(twice * sines[-1] - sines[-2])
            for part, values in enumerate((cosines, sines)):
                at = pl.ds(start, rows), pl.ds(part * LANES, LANES)
                turned_ref[i, at[0], at[1]] = jnp.concatenate(values, axis=0).astype(jnp.bfloat16)


def least_count(pairs):
    return 4 * pairs * lax.axis_index("lat") + 16


def candidate_of(count, j, least):
    return j + jnp.clip((count - least - 4 * j) >> 2, 0, 1)


def analysis_kernel(
    held, fields, first,
    counts_hbm, weights_hbm, waves_hbm, stiffness_hbm, basis_hbm, grid_hbm,
    coef_ref, table_ref, choice_ref, basis_ref, wave_ref, stiffness_ref, limit_ref,
    counts, weights, waves, levels, values, given, widened, turned_ref, arrived, grid_arrived,
):
    owners, blocks = coef_ref.shape[:2]
    pairs = limit_ref.shape[0]
    slots = owners * ROWS
    width = basis_ref.shape[2]
    points = grid_hbm.shape[1]
    rows = grid_hbm.shape[0] // pairs
    rest = pairs * rows - blocks * LANES
    small = [
        pltpu.make_async_copy(source, target, arrived.at[k])
        for k, (source, target) in enumerate(
            [(counts_hbm, counts), (waves_hbm, waves), (weights_hbm, weights), (stiffness_hbm, levels)]
        )
    ]
    latitudes = [pl.ds(j * rows, rows) for j in range(pairs)]
    fields_in = [pltpu.make_async_copy(grid_hbm, values, grid_arrived)]
    basis_in = pltpu.make_async_copy(basis_hbm, given, arrived.at[len(small)])
    for copy in (*fields_in, *small, basis_in):
        copy.start()
    least = least_count(pairs)
    fill_turned(turned_ref, least)
    fill_tables(table_ref, width, least)
    for copy in (*small, *fields_in):
        copy.wait()
    choice = slot_choice(waves, held, first, slots)
    choices = [choice] + (rest_choices(choice, held, rest) if rest else [])
    choices = [each.astype(jnp.bfloat16) for each in choices]
    for k, each in enumerate(choices):
        choice_ref[k * slots : (k + 1) * slots, :] = each
    lane = lax.broadcasted_iota(jnp.int32, (1, LANES), 1)
    padding = jnp.zeros((1, LANES - width), jnp.float32)
    own_waves = jnp.concatenate([waves[...].astype(jnp.float32), padding], axis=1)
    own_waves = pltpu.roll(own_waves, (LANES - lax.axis_index("lat") * held) % LANES, 1)
    for c in range(held):
        wave_ref[c : c + 1, :] = jnp.broadcast_to(own_waves[:, c : c + 1], (1, LANES))
    all_levels = levels.shape[1]
    own = jnp.concatenate([levels[...], jnp.zeros((1, LANES - all_levels), jnp.float32)], axis=1)
    own = pltpu.roll(own, (LANES - lax.axis_index("lev") * fields) % LANES, 1)
    own = jnp.where(lane < fields, own, 0.0)
    stiffness = own
    for copy in range(1, 4):
        stiffness = stiffness + turn(own, copy * fields, 1)
    stiffness_ref[...] = stiffness
    position = lax.broadcasted_iota(jnp.int32, (1, points), 1)
    mode = lax.broadcasted_iota(jnp.int32, (1, 2 * LANES), 1) & (LANES - 1)
    pieces = []
    for j in range(pairs):
        limit_ref[j : j + 1, :] = jnp.full((1, LANES), counts[j].astype(jnp.float32))
        inside = jnp.where(position < counts[j], 1.0, 0.0).astype(jnp.bfloat16)
        product = jnp.dot(
            values[latitudes[j], :] * inside,
            turned_ref[candidate_of(counts[j], j, least)],
            preferred_element_type=jnp.float32,
        )
        scale = jnp.full((1, 1), weights[j]) / jnp.full((1, 1), counts[j].astype(jnp.float32))
        scale = jnp.where(2 * mode < counts[j], scale, 0.0)
        pieces.append((product * scale).astype(jnp.bfloat16))
    whole = jnp.concatenate(pieces, axis=0)
    parts = [whole[:, part * LANES : (part + 1) * LANES] for part in range(2)]
    for block in range(blocks):
        taken = [choices[0]]
        modes = [[part[block * LANES : (block + 1) * LANES] for part in parts]]
        if rest and block == blocks - 1:
            for group, each in enumerate(choices[1:]):
                taken.append(each)
                above = jnp.zeros((group * rest, LANES), jnp.bfloat16)
                below = jnp.zeros((LANES - (group + 1) * rest, LANES), jnp.bfloat16)
                modes.append(
                    [
                        jnp.concatenate(
                            [x for x in (above, part[blocks * LANES :], below) if x.shape[0]], axis=0
                        )
                        for part in parts
                    ]
                )
        placed = lax.dot_general(
            jnp.concatenate(taken, axis=1),
            jnp.concatenate([jnp.concatenate(both, axis=0) for both in modes], axis=1),
            (((1,), (1,)), ((), ())),
            preferred_element_type=jnp.float32,
        )
        for part in range(2):
            strip = placed[:, part * LANES : (part + 1) * LANES]
            coef_ref[:, block, part] = strip.reshape(owners, ROWS, LANES).astype(jnp.bfloat16)
    basis_in.wait()
    widened[...] = given[...].astype(jnp.float32)
    for c in range(held):
        for j in range(pairs):
            strip = widened[c, pl.ds(j, owners, stride=pairs), :]
            basis_ref[c, j * owners : (j + 1) * owners, :] = turn(strip, -first, 0).astype(
                jnp.bfloat16
            )


def legendre_kernel(
    held, fields, wave_ref, stiffness_ref, basis_ref, recv_ref, send_ref, fan_in, fan_out
):
    owners, blocks = recv_ref.shape[:2]
    latitudes, width = basis_ref.shape[1:]
    pairs = latitudes // owners
    rows = 2 * fields
    rest = pairs * rows - blocks * LANES
    for block in range(blocks):
        for part in range(2):
            plane = recv_ref[:, block, part].astype(jnp.float32).reshape(owners * ROWS, LANES)
            fan_in[block * 2 + part] = plane

    def chunk_rows(block, part, row):
        return block * 2 + part, pl.ds(row, owners, stride=ROWS), slice(None)

    def home(c, block, lane):
        if block == blocks:
            row, start = rest_home(c, held, rest)
            return row, block - 1, start + lane
        return c, block, lane

    lane_at = lax.broadcasted_iota(jnp.int32, (1, LANES), 1)
    south = ((lane_at >= fields) & (lane_at < 2 * fields)) | (lane_at >= 3 * fields)
    offset = lax.broadcasted_iota(jnp.int32, (width, 1), 0)
    parity = jnp.where((offset & 1) == 0, 1.0, -1.0)
    offset = offset.astype(jnp.float32)
    empty = jnp.zeros((owners, LANES), jnp.float32)
    folded = {}
    for c in range(held):
        wave = wave_ref[c : c + 1, :]
        degree = offset + wave
        basis = basis_ref[c]
        strips = []
        for j in range(pairs):
            strip = empty
            for part in range(2):
                for block, lane, place, size in segments(j * rows, rows):
                    row, block, lane = home(c, block, lane)
                    source = fan_in[chunk_rows(block, part, row)]
                    target = part * rows + place
                    here = (lane_at >= target) & (lane_at < target + size)
                    strip = jnp.where(here, turn(source, target - lane, 1), strip)
            strips.append(strip.astype(jnp.bfloat16))
        spectra = lax.dot_general(
            basis,
            jnp.concatenate(strips, axis=0),
            (((0,), (0,)), ((), ())),
            preferred_element_type=jnp.float32,
        )
        factor = 1.0 / (1.0 + stiffness_ref[...] * degree * (degree + 1.0))
        damping = jnp.where(degree < float(width), factor, 0.0)
        other = jnp.where(south, turn(spectra, fields, 1), turn(spectra, -fields, 1))
        scaled = ((spectra + parity * other) * damping).astype(jnp.bfloat16)
        returned = jnp.dot(basis, scaled, preferred_element_type=jnp.float32)
        returned = returned * jnp.where(wave == 0.0, 1.0, 2.0)
        for part in range(2):
            built = {}
            for j in range(pairs):
                strip = returned[j * owners : (j + 1) * owners]
                for block, lane, place, size in segments(j * rows, rows):
                    row, block, lane = home(c, block, lane)
                    key = (block, part, row)
                    here = (lane_at >= lane) & (lane_at < lane + size)
                    moved = turn(strip, lane - part * rows - place, 1)
                    held_in = folded if row >= held else built
                    held_in[key] = jnp.where(here, moved, held_in.get(key, empty))
            for key, value in built.items():
                fan_out[chunk_rows(*key)] = value
    for block in range(blocks):
        for part in range(2):
            for row in range(held, ROWS):
                key = (block, part, row)
                fan_out[chunk_rows(*key)] = folded.get(key, empty)
    for block in range(blocks):
        for part in range(2):
            plane = fan_out[block * 2 + part].reshape(owners, ROWS, LANES)
            send_ref[:, block, part] = plane.astype(jnp.bfloat16)


def synthesis_kernel(
    held, limit_ref, choice_ref, recv_ref, table_ref, grid_hbm, values, left
):
    owners, blocks = recv_ref.shape[:2]
    pairs = limit_ref.shape[0]
    slots = owners * ROWS
    width = table_ref.shape[1] // 2
    points = grid_hbm.shape[1]
    rows = grid_hbm.shape[0] // pairs
    rest = pairs * rows - blocks * LANES
    least = least_count(pairs)
    operands = []
    for part in range(2):
        turned = []
        for block in range(blocks):
            plane = recv_ref[:, block, part].astype(jnp.float32).reshape(slots, LANES)
            turned.append(plane.T.astype(jnp.bfloat16))
        found = [
            jnp.dot(
                jnp.concatenate(turned, axis=0),
                choice_ref[:slots, :],
                preferred_element_type=jnp.float32,
            )
        ]
        if rest:
            groups = choice_ref.shape[0] // slots - 1
            folded = [turned[-1][group * rest : (group + 1) * rest] for group in range(groups)]
            found.append(
                jnp.dot(
                    jnp.concatenate(folded, axis=1),
                    choice_ref[slots:, :],
                    preferred_element_type=jnp.float32,
                )
            )
        operands.append(jnp.concatenate(found, axis=0))
    position = lax.broadcasted_iota(jnp.int32, (1, points), 1).astype(jnp.float32)
    mode = lax.broadcasted_iota(jnp.int32, (1, LANES), 1).astype(jnp.float32)
    copies = []
    for j in range(pairs):
        end = limit_ref[j : j + 1, :]
        at = pl.ds(j * rows, rows)
        candidate = candidate_of(jnp.max(end).astype(jnp.int32), j, least)
        product = None
        for part in range(2):
            operand = operands[part][j * rows : (j + 1) * rows]
            operand = jnp.where(2.0 * mode < end, operand, 0.0).astype(jnp.bfloat16)
            term = jnp.dot(
                operand[:, :width],
                table_ref[candidate, part * width : (part + 1) * width, :],
                preferred_element_type=jnp.float32,
            )
            product = term if product is None else product + term
        kept = jnp.where(position < end[:, :1], product[:, :points], 0.0)
        values[at, :] = kept.astype(jnp.bfloat16)
        copies.append(pltpu.make_async_copy(values.at[at, :], grid_hbm.at[at, :], left.at[j]))
        copies[-1].start()
    for copy in copies:
        copy.wait()


def on_device(mesh, grid, point_counts, waves, legendre, weights, stiffness):
    pairs, _, fields, points = grid.shape
    width = waves.shape[0]
    owners = mesh.shape["lat"]
    held = width // owners
    slots = owners * ROWS
    rows = 2 * fields
    padded = -(-points // LANES) * LANES
    blocks = pairs * rows // LANES
    rest = pairs * rows % LANES
    choices = 1 + (min(LANES // rest, held) if rest else 0)
    first = 11 * owners // 16
    groups = [[(place + first) % owners for place in range(owners)]]
    vmem = pl.BlockSpec(memory_space=pltpu.VMEM)
    hbm = pl.BlockSpec(memory_space=pltpu.HBM)
    limits = pltpu.CompilerParams(vmem_limit_bytes=KERNEL_BYTES)
    exchanged = jax.ShapeDtypeStruct((owners, blocks, 2, ROWS, LANES), jnp.bfloat16)
    coefficients, tables, choice, basis, wave_rows, levels, ends = pl.pallas_call(
        functools.partial(analysis_kernel, held, fields, first),
        out_shape=(
            exchanged,
            jax.ShapeDtypeStruct((pairs + 1, 2 * width, padded), jnp.bfloat16),
            jax.ShapeDtypeStruct((choices * slots, LANES), jnp.bfloat16),
            jax.ShapeDtypeStruct(legendre.shape, jnp.bfloat16),
            jax.ShapeDtypeStruct((held, LANES), jnp.float32),
            jax.ShapeDtypeStruct((1, LANES), jnp.float32),
            jax.ShapeDtypeStruct((pairs, LANES), jnp.float32),
        ),
        in_specs=[hbm] * 6,
        out_specs=(vmem,) * 7,
        scratch_shapes=[
            pltpu.SMEM((pairs,), jnp.int32),
            pltpu.SMEM((pairs,), jnp.float32),
            pltpu.VMEM((1, width), jnp.int32),
            pltpu.VMEM((1, stiffness.shape[0]), jnp.float32),
            pltpu.VMEM((pairs * rows, points), jnp.bfloat16),
            pltpu.VMEM(legendre.shape, jnp.bfloat16),
            pltpu.VMEM(legendre.shape, jnp.float32),
            pltpu.VMEM((pairs + 1, points, 2 * LANES), jnp.bfloat16),
            pltpu.SemaphoreType.DMA((5,)),
            pltpu.SemaphoreType.DMA,
        ],
        compiler_params=limits,
        name="analysis",
    )(
        *(
            pltpu.with_memory_space_constraint(array, pltpu.HBM)
            for array in (
                point_counts, weights, waves.reshape(1, width), stiffness.reshape(1, -1), legendre,
                grid.reshape(pairs * rows, points),
            )
        )
    )

    def exchange(array):
        return lax.all_to_all(
            array, "lat", split_axis=0, concat_axis=0, axis_index_groups=groups, tiled=True
        )

    synthesised = pl.pallas_call(
        functools.partial(legendre_kernel, held, fields),
        out_shape=exchanged,
        in_specs=[vmem] * 4,
        out_specs=vmem,
        scratch_shapes=[
            pltpu.VMEM((blocks * 2, slots, LANES), jnp.float32),
            pltpu.VMEM((blocks * 2, slots, LANES), jnp.float32),
        ],
        compiler_params=limits,
        name="legendre",
    )(wave_rows, levels, basis, exchange(coefficients))
    result = pl.pallas_call(
        functools.partial(synthesis_kernel, held),
        out_shape=jax.ShapeDtypeStruct((pairs * rows, points), jnp.bfloat16),
        in_specs=[vmem] * 4,
        out_specs=hbm,
        scratch_shapes=[
            pltpu.VMEM((pairs * rows, points), jnp.bfloat16),
            pltpu.SemaphoreType.DMA((pairs,)),
        ],
        compiler_params=limits,
        name="synthesis",
    )(ends, choice, exchange(synthesised), tables)
    return result.reshape(grid.shape)


def fourier_tables(count, wavenumbers, quarter_max):
    quarter = count // 4
    step_angle = TWO_PI / quarter.astype(jnp.float32)
    coarse_count = (quarter_max + FINE_STEPS - 1) // FINE_STEPS
    coarse_pos = FINE_STEPS * jnp.arange(coarse_count, dtype=jnp.int32)
    fine_pos = jnp.arange(FINE_STEPS, dtype=jnp.int32)
    coarse_angle = (coarse_pos[:, None] * wavenumbers[None, :] % quarter).astype(
        jnp.float32
    ) * step_angle
    fine_angle = (fine_pos[:, None] * wavenumbers[None, :] % quarter).astype(
        jnp.float32
    ) * step_angle
    coarse_cos = jnp.cos(coarse_angle)[:, None, :]
    coarse_sin = jnp.sin(coarse_angle)[:, None, :]
    fine_cos = jnp.cos(fine_angle)[None, :, :]
    fine_sin = jnp.sin(fine_angle)[None, :, :]
    full_cos = (coarse_cos * fine_cos - coarse_sin * fine_sin).reshape(
        coarse_count * FINE_STEPS, -1
    )[:quarter_max]
    full_sin = (coarse_sin * fine_cos + coarse_cos * fine_sin).reshape(
        coarse_count * FINE_STEPS, -1
    )[:quarter_max]
    positions = jnp.arange(quarter_max, dtype=jnp.int32)
    inside = (positions < quarter)[:, None]
    cosine = jnp.where(inside, full_cos, 0.0)
    sine = jnp.where(inside, full_sin, 0.0)
    matrix = jnp.concatenate([cosine, sine], axis=1).astype(jnp.bfloat16)
    offsets = jnp.arange(4, dtype=jnp.int32)
    twist = offsets[:, None] * wavenumbers[None, :] % count
    theta = twist.astype(jnp.float32) * (TWO_PI / count.astype(jnp.float32))
    return (matrix, jnp.cos(theta), jnp.sin(theta))


def helmholtz(spectra, wavenumbers, offsets, stiffness_local, width):
    full_shape = spectra.shape
    quartered = spectra.reshape(full_shape[:-2] + (full_shape[-2] // 4, 2, 2, full_shape[-1]))
    parity = (1 - 2 * (offsets % 2)).astype(jnp.float32)
    combined = quartered[..., 0, :] + parity * quartered[..., 1, :]
    degrees = (wavenumbers + offsets).astype(jnp.float32)
    inside_band = offsets < width - wavenumbers
    factor = 1.0 / (
        1.0 + stiffness_local[:, None] * degrees[..., None, :] * (degrees[..., None, :] + 1.0)
    )
    damping = jnp.where(inside_band[..., None, :], factor, 0.0)
    scaled = (combined * damping[..., :, None, :]).astype(jnp.bfloat16)
    flipped = scaled * parity.astype(jnp.bfloat16)
    return jnp.stack([scaled, flipped], axis=-2).reshape(full_shape)


def spectral(received, wavenumbers, basis, stiffness_local):
    width = basis.shape[2]
    spectra = jnp.einsum("jcr,cjl->crl", received, basis, preferred_element_type=jnp.float32)
    offsets = jnp.arange(width, dtype=jnp.int32)
    operand = helmholtz(spectra, wavenumbers[:, None], offsets, stiffness_local, width)
    returned = jnp.einsum("crl,cjl->jcr", operand, basis, preferred_element_type=jnp.float32)
    return returned.astype(jnp.bfloat16)


def on_device_blocked(grid, point_counts, waves, legendre, weights, stiffness):
    pairs, _, fields, points = grid.shape
    quarter_max = points // 4
    width = waves.shape[0]
    held_slots = legendre.shape[0]
    lat_index = lax.axis_index("lat")
    lev_index = lax.axis_index("lev")

    def analyse(pieces):
        latitude, count, weight = pieces
        matrix, twist_cos, twist_sin = fourier_tables(count, waves, quarter_max)
        values = latitude.reshape(2, fields, quarter_max, 4)
        partial_value = jnp.einsum(
            "hfab,at->hfbt", values, matrix, preferred_element_type=jnp.float32
        )
        cos_part = partial_value[..., :width]
        sin_part = partial_value[..., width:]
        real = jnp.sum(twist_cos * cos_part - twist_sin * sin_part, axis=2)
        imag = -jnp.sum(twist_sin * cos_part + twist_cos * sin_part, axis=2)
        factor = jnp.where(2 * waves < count, weight / count.astype(jnp.float32), 0.0)
        stacked = jnp.stack([real * factor, imag * factor], axis=0)
        packed = jnp.transpose(stacked, (3, 2, 0, 1)).reshape(width, 4 * fields)
        return (packed.astype(jnp.bfloat16), matrix, twist_cos, twist_sin)

    coefficients, matrices, twist_cos, twist_sin = lax.map(analyse, (grid, point_counts, weights))
    received = lax.all_to_all(coefficients, "lat", split_axis=1, concat_axis=0, tiled=True)
    owned = lax.dynamic_slice_in_dim(waves, lat_index * held_slots, held_slots)
    own_stiffness = lax.dynamic_slice_in_dim(stiffness, lev_index * fields, fields)
    synthesised = spectral(received, owned, legendre, own_stiffness)
    returned = lax.all_to_all(synthesised, "lat", split_axis=0, concat_axis=1, tiled=True)

    def synthesise(pieces):
        packed, matrix, turn_cos, turn_sin, count = pieces
        values = packed.astype(jnp.float32).reshape(width, fields, 2, 2)
        real = values[:, :, 0, :]
        imag = values[:, :, 1, :]
        factor = jnp.where(2 * waves < count, jnp.where(waves == 0, 1.0, 2.0), 0.0)[:, None, None]
        cosines = turn_cos[:, :, None, None]
        sines = turn_sin[:, :, None, None]
        turned_real = factor * (real * cosines - imag * sines)
        turned_imag = factor * (real * sines + imag * cosines)
        operand = jnp.concatenate([turned_real, -turned_imag], axis=1)
        upper = operand.astype(jnp.bfloat16)
        lower = (operand - upper.astype(jnp.float32)).astype(jnp.bfloat16)
        result = jnp.einsum("bmfh,am->hfab", upper, matrix, preferred_element_type=jnp.float32)
        result = result + jnp.einsum(
            "bmfh,am->hfab", lower, matrix, preferred_element_type=jnp.float32
        )
        return result.reshape(2, fields, points).astype(jnp.bfloat16)

    return lax.map(synthesise, (returned, matrices, twist_cos, twist_sin, point_counts))


def fits_on_chip(mesh, grid, waves, stiffness):
    owners = mesh.shape["lat"]
    pairs, fields = grid.shape[0] // owners, grid.shape[2] // mesh.shape["lev"]
    width, points = waves.shape[0], grid.shape[3]
    held = width // owners
    lanes = 2 * pairs * fields
    rest = lanes % LANES
    return (
        width % owners == 0
        and width % (2 * ROWS) == 0
        and width <= LANES
        and 4 * (pairs + 1) * LANES * points <= TABLE_BUDGET
        and points <= ROWS * LANES
        and points % (2 * ROWS) == 0
        and held <= ROWS
        and lanes >= LANES
        and (rest == 0 or rest % (2 * ROWS) == 0)
        and (rest == 0 or held <= (ROWS - held) * (LANES // rest))
        and 4 * fields <= LANES
        and fields % ROWS == 0
        and owners % (2 * ROWS) == 0
        and stiffness.shape[0] <= LANES
    )


def solution(mesh):
    in_specs = (P("lat", None, "lev", None), P("lat"), P(), P("lat", None, None), P("lat"), P())
    out_specs = P("lat", None, "lev", None)

    def program(grid, point_counts, waves, legendre, weights, stiffness):
        fits = fits_on_chip(mesh, grid, waves, stiffness)
        body = functools.partial(on_device, mesh) if fits else on_device_blocked
        return jax.shard_map(
            body, mesh=mesh, in_specs=in_specs, out_specs=out_specs, check_vma=False
        )(grid, point_counts, waves, legendre, weights, stiffness)

    return program
```

```python
import functools
import math

import jax
import jax.numpy as jnp
from jax import lax
from jax.experimental import pallas as pl
from jax.experimental.pallas import tpu as pltpu
from jax.sharding import PartitionSpec as P

TWO_PI = 2.0 * math.pi
FINE_STEPS = 32
LANES = 128
ROWS = 8
TABLE_BUDGET = 4 << 20
KERNEL_BYTES = 8 << 20

COS_TURN = (
    0.9999999998781397, -19.739208740145937, 64.9393888386778, -85.45665201444898,
    60.24205245141228, -26.404165331517056, 7.79855301354287, -1.4511773940976733,
)
SIN_TURN = (
    6.2831853022485955, -41.341700317335295, 81.60512671223316, -76.70292598092092,
    42.02516399730493, -14.896874459689428, 3.233831551278599,
)


def polynomial(coefficients, u):
    total = coefficients[-1] * u + coefficients[-2]
    for value in coefficients[-3::-1]:
        total = total * u + value
    return total


def cos_minus_sin(steps, count, inverse):
    reduced = steps - jnp.floor(steps * inverse + 0.5) * count
    turn = reduced * inverse
    square = turn * turn
    return polynomial(COS_TURN, square), -turn * polynomial(SIN_TURN, square)


def slot_choice(waves_ref, held, first, slots):
    width = waves_ref.shape[1]
    owners = slots // ROWS
    row = lax.broadcasted_iota(jnp.int32, (slots, width), 0)
    lane = lax.broadcasted_iota(jnp.int32, (slots, width), 1)
    place = row & (ROWS - 1)
    owner = (row >> 3) + first
    owner = jnp.where(owner >= owners, owner - owners, owner)
    chosen = (owner * held + place == lane) & (place < held)
    waves = jnp.broadcast_to(waves_ref[...].astype(jnp.float32) + 1.0, (slots, width))
    column = jnp.sum(jnp.where(chosen, waves, 0.0), axis=1, keepdims=True)
    mode = lax.broadcasted_iota(jnp.int32, (slots, LANES), 1).astype(jnp.float32) + 1.0
    return jnp.where(mode == column, 1.0, 0.0)


def segments(start, length):
    done = 0
    while done < length:
        block, lane = divmod(start + done, LANES)
        size = min(length - done, LANES - lane)
        yield block, lane, done, size
        done += size


def turn(x, shift, axis):
    shift %= x.shape[axis]
    return pltpu.roll(x, shift, axis) if shift else x


def rest_home(c, held, rest):
    fit = LANES // rest
    return held + c // fit, (c % fit) * rest


def rest_choices(choice, held, rest):
    owners = choice.shape[0] // ROWS
    grouped = choice.reshape(owners, ROWS, LANES)
    sublane = lax.broadcasted_iota(jnp.int32, (1, ROWS, LANES), 1)
    fit = LANES // rest
    out = []
    for group in range(min(fit, held)):
        total = jnp.zeros_like(grouped)
        for c in range(group, held, fit):
            row, _ = rest_home(c, held, rest)
            total = jnp.where(sublane == row, turn(grouped, row - c, 1), total)
        out.append(total.reshape(choice.shape))
    return out


def fill_tables(table_ref, width, least):
    candidates, _, padded = table_ref.shape
    blocks = padded // LANES
    sublane = lax.broadcasted_iota(jnp.int32, (ROWS, LANES), 0)
    lane = lax.broadcasted_iota(jnp.int32, (ROWS, LANES), 1)
    strides = (ROWS * (sublane * LANES + lane)).astype(jnp.float32)
    steps = [(sublane * (lane + b * LANES)).astype(jnp.float32) for b in range(blocks)]
    for i in range(candidates):
        count = jnp.full((1, LANES), (least + 4 * i).astype(jnp.float32))
        inverse = 1.0 / count
        stride_cos, stride_sin = cos_minus_sin(strides, count, inverse)
        for b in range(blocks):
            turn_cos, turn_sin = stride_cos[b : b + 1], stride_sin[b : b + 1]
            twice = turn_cos + turn_cos
            cosine, sine = cos_minus_sin(steps[b], count, inverse)
            cosines = [cosine, cosine * turn_cos - sine * turn_sin]
            sines = [sine, sine * turn_cos + cosine * turn_sin]
            while len(cosines) * ROWS < width:
                cosines.append(twice * cosines[-1] - cosines[-2])
                sines.append(twice * sines[-1] - sines[-2])
            at = pl.ds(b * LANES, LANES)
            for part, values in enumerate((cosines, sines)):
                rows = pl.ds(part * width, width)
                table_ref[i, rows, at] = jnp.concatenate(values, axis=0).astype(jnp.bfloat16)


def fill_turned(turned_ref, least):
    candidates, points, _ = turned_ref.shape
    sublane = lax.broadcasted_iota(jnp.int32, (ROWS, LANES), 0)
    lane = lax.broadcasted_iota(jnp.int32, (ROWS, LANES), 1)
    strides = (ROWS * lane).astype(jnp.float32)
    for i in range(candidates):
        count = jnp.full((1, LANES), (least + 4 * i).astype(jnp.float32))
        inverse = 1.0 / count
        turn_cos, turn_sin = cos_minus_sin(strides, count, inverse)
        twice = turn_cos + turn_cos
        for start in range(0, points, LANES):
            rows = min(LANES, points - start)
            steps = ((sublane + start) * lane).astype(jnp.float32)
            cosine, sine = cos_minus_sin(steps, count, inverse)
            cosines = [cosine, cosine * turn_cos - sine * turn_sin]
            sines = [sine, sine * turn_cos + cosine * turn_sin]
            while len(cosines) * ROWS < rows:
                cosines.append(twice * cosines[-1] - cosines[-2])
                sines.append(twice * sines[-1] - sines[-2])
            for part, values in enumerate((cosines, sines)):
                at = pl.ds(start, rows), pl.ds(part * LANES, LANES)
                turned_ref[i, at[0], at[1]] = jnp.concatenate(values, axis=0).astype(jnp.bfloat16)


def least_count(pairs):
    return 4 * pairs * lax.axis_index("lat") + 16


def candidate_of(count, j, least):
    return j + jnp.clip((count - least - 4 * j) >> 2, 0, 1)


def analysis_kernel(
    held, fields, first,
    counts_hbm, weights_hbm, waves_hbm, stiffness_hbm, basis_hbm, grid_hbm,
    coef_ref, table_ref, choice_ref, basis_ref, wave_ref, stiffness_ref, limit_ref,
    counts, weights, waves, levels, values, given, widened, turned_ref, arrived, grid_arrived,
):
    owners, blocks = coef_ref.shape[:2]
    pairs = limit_ref.shape[0]
    slots = owners * ROWS
    width = basis_ref.shape[2]
    points = grid_hbm.shape[1]
    rows = grid_hbm.shape[0] // pairs
    rest = pairs * rows - blocks * LANES
    small = [
        pltpu.make_async_copy(source, target, arrived.at[k])
        for k, (source, target) in enumerate(
            [(counts_hbm, counts), (waves_hbm, waves), (weights_hbm, weights), (stiffness_hbm, levels)]
        )
    ]
    latitudes = [pl.ds(j * rows, rows) for j in range(pairs)]
    fields_in = [pltpu.make_async_copy(grid_hbm, values, grid_arrived)]
    basis_in = pltpu.make_async_copy(basis_hbm, given, arrived.at[len(small)])
    for copy in (*fields_in, *small, basis_in):
        copy.start()
    least = least_count(pairs)
    fill_turned(turned_ref, least)
    fill_tables(table_ref, width, least)
    small[1].wait()
    choice = slot_choice(waves, held, first, slots)
    choices = [choice] + (rest_choices(choice, held, rest) if rest else [])
    choices = [each.astype(jnp.bfloat16) for each in choices]
    for k, each in enumerate(choices):
        choice_ref[k * slots : (k + 1) * slots, :] = each
    lane = lax.broadcasted_iota(jnp.int32, (1, LANES), 1)
    for copy in (small[0], *small[2:], *fields_in):
        copy.wait()
    padding = jnp.zeros((1, LANES - width), jnp.float32)
    own_waves = jnp.concatenate([waves[...].astype(jnp.float32), padding], axis=1)
    own_waves = pltpu.roll(own_waves, (LANES - lax.axis_index("lat") * held) % LANES, 1)
    for c in range(held):
        wave_ref[c : c + 1, :] = jnp.broadcast_to(own_waves[:, c : c + 1], (1, LANES))
    all_levels = levels.shape[1]
    own = jnp.concatenate([levels[...], jnp.zeros((1, LANES - all_levels), jnp.float32)], axis=1)
    own = pltpu.roll(own, (LANES - lax.axis_index("lev") * fields) % LANES, 1)
    own = jnp.where(lane < fields, own, 0.0)
    stiffness = own
    for copy in range(1, 4):
        stiffness = stiffness + turn(own, copy * fields, 1)
    stiffness_ref[...] = stiffness
    position = lax.broadcasted_iota(jnp.int32, (1, points), 1)
    mode = lax.broadcasted_iota(jnp.int32, (1, 2 * LANES), 1) & (LANES - 1)
    pieces = []
    for j in range(pairs):
        limit_ref[j : j + 1, :] = jnp.full((1, LANES), counts[j].astype(jnp.float32))
        inside = jnp.where(position < counts[j], 1.0, 0.0).astype(jnp.bfloat16)
        product = jnp.dot(
            values[latitudes[j], :] * inside,
            turned_ref[candidate_of(counts[j], j, least)],
            preferred_element_type=jnp.float32,
        )
        scale = jnp.full((1, 1), weights[j]) / jnp.full((1, 1), counts[j].astype(jnp.float32))
        scale = jnp.where(2 * mode < counts[j], scale, 0.0)
        pieces.append((product * scale).astype(jnp.bfloat16))
    basis_in.wait()
    widened[...] = given[...].astype(jnp.float32)
    for c in range(held):
        for j in range(pairs):
            strip = widened[c, pl.ds(j, owners, stride=pairs), :]
            basis_ref[c, j * owners : (j + 1) * owners, :] = turn(strip, -first, 0).astype(
                jnp.bfloat16
            )
    whole = jnp.concatenate(pieces, axis=0)
    parts = [whole[:, part * LANES : (part + 1) * LANES] for part in range(2)]
    for block in range(blocks):
        taken = [choices[0]]
        modes = [[part[block * LANES : (block + 1) * LANES] for part in parts]]
        if rest and block == blocks - 1:
            for group, each in enumerate(choices[1:]):
                taken.append(each)
                above = jnp.zeros((group * rest, LANES), jnp.bfloat16)
                below = jnp.zeros((LANES - (group + 1) * rest, LANES), jnp.bfloat16)
                modes.append(
                    [
                        jnp.concatenate(
                            [x for x in (above, part[blocks * LANES :], below) if x.shape[0]], axis=0
                        )
                        for part in parts
                    ]
                )
        placed = lax.dot_general(
            jnp.concatenate(taken, axis=1),
            jnp.concatenate([jnp.concatenate(both, axis=0) for both in modes], axis=1),
            (((1,), (1,)), ((), ())),
            preferred_element_type=jnp.float32,
        )
        for part in range(2):
            strip = placed[:, part * LANES : (part + 1) * LANES]
            coef_ref[:, block, part] = strip.reshape(owners, ROWS, LANES).astype(jnp.bfloat16)


def legendre_kernel(
    held, fields, wave_ref, stiffness_ref, basis_ref, recv_ref, send_ref, fan_in, fan_out
):
    owners, blocks = recv_ref.shape[:2]
    latitudes, width = basis_ref.shape[1:]
    pairs = latitudes // owners
    rows = 2 * fields
    rest = pairs * rows - blocks * LANES
    for block in range(blocks):
        for part in range(2):
            plane = recv_ref[:, block, part].astype(jnp.float32).reshape(owners * ROWS, LANES)
            fan_in[block * 2 + part] = plane

    def chunk_rows(block, part, row):
        return block * 2 + part, pl.ds(row, owners, stride=ROWS), slice(None)

    def home(c, block, lane):
        if block == blocks:
            row, start = rest_home(c, held, rest)
            return row, block - 1, start + lane
        return c, block, lane

    lane_at = lax.broadcasted_iota(jnp.int32, (1, LANES), 1)
    south = ((lane_at >= fields) & (lane_at < 2 * fields)) | (lane_at >= 3 * fields)
    offset = lax.broadcasted_iota(jnp.int32, (width, 1), 0)
    parity = jnp.where((offset & 1) == 0, 1.0, -1.0)
    offset = offset.astype(jnp.float32)
    empty = jnp.zeros((owners, LANES), jnp.float32)
    folded = {}
    for c in range(held):
        wave = wave_ref[c : c + 1, :]
        degree = offset + wave
        basis = basis_ref[c]
        strips = []
        for j in range(pairs):
            strip = empty
            for part in range(2):
                for block, lane, place, size in segments(j * rows, rows):
                    row, block, lane = home(c, block, lane)
                    source = fan_in[chunk_rows(block, part, row)]
                    target = part * rows + place
                    here = (lane_at >= target) & (lane_at < target + size)
                    strip = jnp.where(here, turn(source, target - lane, 1), strip)
            strips.append(strip.astype(jnp.bfloat16))
        spectra = lax.dot_general(
            basis,
            jnp.concatenate(strips, axis=0),
            (((0,), (0,)), ((), ())),
            preferred_element_type=jnp.float32,
        )
        factor = 1.0 / (1.0 + stiffness_ref[...] * degree * (degree + 1.0))
        damping = jnp.where(degree < float(width), factor, 0.0)
        other = jnp.where(south, turn(spectra, fields, 1), turn(spectra, -fields, 1))
        scaled = ((spectra + parity * other) * damping).astype(jnp.bfloat16)
        returned = jnp.dot(basis, scaled, preferred_element_type=jnp.float32)
        returned = returned * jnp.where(wave == 0.0, 1.0, 2.0)
        for part in range(2):
            built = {}
            for j in range(pairs):
                strip = returned[j * owners : (j + 1) * owners]
                for block, lane, place, size in segments(j * rows, rows):
                    row, block, lane = home(c, block, lane)
                    key = (block, part, row)
                    here = (lane_at >= lane) & (lane_at < lane + size)
                    moved = turn(strip, lane - part * rows - place, 1)
                    held_in = folded if row >= held else built
                    held_in[key] = jnp.where(here, moved, held_in.get(key, empty))
            for key, value in built.items():
                fan_out[chunk_rows(*key)] = value
    for block in range(blocks):
        for part in range(2):
            for row in range(held, ROWS):
                key = (block, part, row)
                fan_out[chunk_rows(*key)] = folded.get(key, empty)
    for block in range(blocks):
        for part in range(2):
            plane = fan_out[block * 2 + part].reshape(owners, ROWS, LANES)
            send_ref[:, block, part] = plane.astype(jnp.bfloat16)


def synthesis_kernel(
    held, limit_ref, choice_ref, recv_ref, table_ref, grid_hbm, values, left
):
    owners, blocks = recv_ref.shape[:2]
    pairs = limit_ref.shape[0]
    slots = owners * ROWS
    width = table_ref.shape[1] // 2
    points = grid_hbm.shape[1]
    rows = grid_hbm.shape[0] // pairs
    rest = pairs * rows - blocks * LANES
    least = least_count(pairs)
    operands = []
    for part in range(2):
        turned = []
        for block in range(blocks):
            plane = recv_ref[:, block, part].astype(jnp.float32).reshape(slots, LANES)
            turned.append(plane.T.astype(jnp.bfloat16))
        found = [
            jnp.dot(
                jnp.concatenate(turned, axis=0),
                choice_ref[:slots, :],
                preferred_element_type=jnp.float32,
            )
        ]
        if rest:
            groups = choice_ref.shape[0] // slots - 1
            folded = [turned[-1][group * rest : (group + 1) * rest] for group in range(groups)]
            found.append(
                jnp.dot(
                    jnp.concatenate(folded, axis=1),
                    choice_ref[slots:, :],
                    preferred_element_type=jnp.float32,
                )
            )
        operands.append(jnp.concatenate(found, axis=0))
    position = lax.broadcasted_iota(jnp.int32, (1, points), 1).astype(jnp.float32)
    mode = lax.broadcasted_iota(jnp.int32, (1, LANES), 1).astype(jnp.float32)
    copies = []
    for j in range(pairs):
        end = limit_ref[j : j + 1, :]
        at = pl.ds(j * rows, rows)
        candidate = candidate_of(jnp.max(end).astype(jnp.int32), j, least)
        product = None
        for part in range(2):
            operand = operands[part][j * rows : (j + 1) * rows]
            operand = jnp.where(2.0 * mode < end, operand, 0.0).astype(jnp.bfloat16)
            term = jnp.dot(
                operand[:, :width],
                table_ref[candidate, part * width : (part + 1) * width, :],
                preferred_element_type=jnp.float32,
            )
            product = term if product is None else product + term
        kept = jnp.where(position < end[:, :1], product[:, :points], 0.0)
        values[at, :] = kept.astype(jnp.bfloat16)
        copies.append(pltpu.make_async_copy(values.at[at, :], grid_hbm.at[at, :], left.at[j]))
        copies[-1].start()
    for copy in copies:
        copy.wait()


def on_device(mesh, grid, point_counts, waves, legendre, weights, stiffness):
    pairs, _, fields, points = grid.shape
    width = waves.shape[0]
    owners = mesh.shape["lat"]
    held = width // owners
    slots = owners * ROWS
    rows = 2 * fields
    padded = -(-points // LANES) * LANES
    blocks = pairs * rows // LANES
    rest = pairs * rows % LANES
    choices = 1 + (min(LANES // rest, held) if rest else 0)
    first = 11 * owners // 16
    groups = [[(place + first) % owners for place in range(owners)]]
    vmem = pl.BlockSpec(memory_space=pltpu.VMEM)
    hbm = pl.BlockSpec(memory_space=pltpu.HBM)
    limits = pltpu.CompilerParams(vmem_limit_bytes=KERNEL_BYTES)
    exchanged = jax.ShapeDtypeStruct((owners, blocks, 2, ROWS, LANES), jnp.bfloat16)
    coefficients, tables, choice, basis, wave_rows, levels, ends = pl.pallas_call(
        functools.partial(analysis_kernel, held, fields, first),
        out_shape=(
            exchanged,
            jax.ShapeDtypeStruct((pairs + 1, 2 * width, padded), jnp.bfloat16),
            jax.ShapeDtypeStruct((choices * slots, LANES), jnp.bfloat16),
            jax.ShapeDtypeStruct(legendre.shape, jnp.bfloat16),
            jax.ShapeDtypeStruct((held, LANES), jnp.float32),
            jax.ShapeDtypeStruct((1, LANES), jnp.float32),
            jax.ShapeDtypeStruct((pairs, LANES), jnp.float32),
        ),
        in_specs=[hbm] * 6,
        out_specs=(vmem,) * 7,
        scratch_shapes=[
            pltpu.SMEM((pairs,), jnp.int32),
            pltpu.SMEM((pairs,), jnp.float32),
            pltpu.VMEM((1, width), jnp.int32),
            pltpu.VMEM((1, stiffness.shape[0]), jnp.float32),
            pltpu.VMEM((pairs * rows, points), jnp.bfloat16),
            pltpu.VMEM(legendre.shape, jnp.bfloat16),
            pltpu.VMEM(legendre.shape, jnp.float32),
            pltpu.VMEM((pairs + 1, points, 2 * LANES), jnp.bfloat16),
            pltpu.SemaphoreType.DMA((5,)),
            pltpu.SemaphoreType.DMA,
        ],
        compiler_params=limits,
        name="analysis",
    )(
        *(
            pltpu.with_memory_space_constraint(array, pltpu.HBM)
            for array in (
                point_counts, weights, waves.reshape(1, width), stiffness.reshape(1, -1), legendre,
                grid.reshape(pairs * rows, points),
            )
        )
    )

    def exchange(array):
        return lax.all_to_all(
            array, "lat", split_axis=0, concat_axis=0, axis_index_groups=groups, tiled=True
        )

    synthesised = pl.pallas_call(
        functools.partial(legendre_kernel, held, fields),
        out_shape=exchanged,
        in_specs=[vmem] * 4,
        out_specs=vmem,
        scratch_shapes=[
            pltpu.VMEM((blocks * 2, slots, LANES), jnp.float32),
            pltpu.VMEM((blocks * 2, slots, LANES), jnp.float32),
        ],
        compiler_params=limits,
        name="legendre",
    )(wave_rows, levels, basis, exchange(coefficients))
    result = pl.pallas_call(
        functools.partial(synthesis_kernel, held),
        out_shape=jax.ShapeDtypeStruct((pairs * rows, points), jnp.bfloat16),
        in_specs=[vmem] * 4,
        out_specs=hbm,
        scratch_shapes=[
            pltpu.VMEM((pairs * rows, points), jnp.bfloat16),
            pltpu.SemaphoreType.DMA((pairs,)),
        ],
        compiler_params=limits,
        name="synthesis",
    )(ends, choice, exchange(synthesised), tables)
    return result.reshape(grid.shape)


def fourier_tables(count, wavenumbers, quarter_max):
    quarter = count // 4
    step_angle = TWO_PI / quarter.astype(jnp.float32)
    coarse_count = (quarter_max + FINE_STEPS - 1) // FINE_STEPS
    coarse_pos = FINE_STEPS * jnp.arange(coarse_count, dtype=jnp.int32)
    fine_pos = jnp.arange(FINE_STEPS, dtype=jnp.int32)
    coarse_angle = (coarse_pos[:, None] * wavenumbers[None, :] % quarter).astype(
        jnp.float32
    ) * step_angle
    fine_angle = (fine_pos[:, None] * wavenumbers[None, :] % quarter).astype(
        jnp.float32
    ) * step_angle
    coarse_cos = jnp.cos(coarse_angle)[:, None, :]
    coarse_sin = jnp.sin(coarse_angle)[:, None, :]
    fine_cos = jnp.cos(fine_angle)[None, :, :]
    fine_sin = jnp.sin(fine_angle)[None, :, :]
    full_cos = (coarse_cos * fine_cos - coarse_sin * fine_sin).reshape(
        coarse_count * FINE_STEPS, -1
    )[:quarter_max]
    full_sin = (coarse_sin * fine_cos + coarse_cos * fine_sin).reshape(
        coarse_count * FINE_STEPS, -1
    )[:quarter_max]
    positions = jnp.arange(quarter_max, dtype=jnp.int32)
    inside = (positions < quarter)[:, None]
    cosine = jnp.where(inside, full_cos, 0.0)
    sine = jnp.where(inside, full_sin, 0.0)
    matrix = jnp.concatenate([cosine, sine], axis=1).astype(jnp.bfloat16)
    offsets = jnp.arange(4, dtype=jnp.int32)
    twist = offsets[:, None] * wavenumbers[None, :] % count
    theta = twist.astype(jnp.float32) * (TWO_PI / count.astype(jnp.float32))
    return (matrix, jnp.cos(theta), jnp.sin(theta))


def helmholtz(spectra, wavenumbers, offsets, stiffness_local, width):
    full_shape = spectra.shape
    quartered = spectra.reshape(full_shape[:-2] + (full_shape[-2] // 4, 2, 2, full_shape[-1]))
    parity = (1 - 2 * (offsets % 2)).astype(jnp.float32)
    combined = quartered[..., 0, :] + parity * quartered[..., 1, :]
    degrees = (wavenumbers + offsets).astype(jnp.float32)
    inside_band = offsets < width - wavenumbers
    factor = 1.0 / (
        1.0 + stiffness_local[:, None] * degrees[..., None, :] * (degrees[..., None, :] + 1.0)
    )
    damping = jnp.where(inside_band[..., None, :], factor, 0.0)
    scaled = (combined * damping[..., :, None, :]).astype(jnp.bfloat16)
    flipped = scaled * parity.astype(jnp.bfloat16)
    return jnp.stack([scaled, flipped], axis=-2).reshape(full_shape)


def spectral(received, wavenumbers, basis, stiffness_local):
    width = basis.shape[2]
    spectra = jnp.einsum("jcr,cjl->crl", received, basis, preferred_element_type=jnp.float32)
    offsets = jnp.arange(width, dtype=jnp.int32)
    operand = helmholtz(spectra, wavenumbers[:, None], offsets, stiffness_local, width)
    returned = jnp.einsum("crl,cjl->jcr", operand, basis, preferred_element_type=jnp.float32)
    return returned.astype(jnp.bfloat16)


def on_device_blocked(grid, point_counts, waves, legendre, weights, stiffness):
    pairs, _, fields, points = grid.shape
    quarter_max = points // 4
    width = waves.shape[0]
    held_slots = legendre.shape[0]
    lat_index = lax.axis_index("lat")
    lev_index = lax.axis_index("lev")

    def analyse(pieces):
        latitude, count, weight = pieces
        matrix, twist_cos, twist_sin = fourier_tables(count, waves, quarter_max)
        values = latitude.reshape(2, fields, quarter_max, 4)
        partial_value = jnp.einsum(
            "hfab,at->hfbt", values, matrix, preferred_element_type=jnp.float32
        )
        cos_part = partial_value[..., :width]
        sin_part = partial_value[..., width:]
        real = jnp.sum(twist_cos * cos_part - twist_sin * sin_part, axis=2)
        imag = -jnp.sum(twist_sin * cos_part + twist_cos * sin_part, axis=2)
        factor = jnp.where(2 * waves < count, weight / count.astype(jnp.float32), 0.0)
        stacked = jnp.stack([real * factor, imag * factor], axis=0)
        packed = jnp.transpose(stacked, (3, 2, 0, 1)).reshape(width, 4 * fields)
        return (packed.astype(jnp.bfloat16), matrix, twist_cos, twist_sin)

    coefficients, matrices, twist_cos, twist_sin = lax.map(analyse, (grid, point_counts, weights))
    received = lax.all_to_all(coefficients, "lat", split_axis=1, concat_axis=0, tiled=True)
    owned = lax.dynamic_slice_in_dim(waves, lat_index * held_slots, held_slots)
    own_stiffness = lax.dynamic_slice_in_dim(stiffness, lev_index * fields, fields)
    synthesised = spectral(received, owned, legendre, own_stiffness)
    returned = lax.all_to_all(synthesised, "lat", split_axis=0, concat_axis=1, tiled=True)

    def synthesise(pieces):
        packed, matrix, turn_cos, turn_sin, count = pieces
        values = packed.astype(jnp.float32).reshape(width, fields, 2, 2)
        real = values[:, :, 0, :]
        imag = values[:, :, 1, :]
        factor = jnp.where(2 * waves < count, jnp.where(waves == 0, 1.0, 2.0), 0.0)[:, None, None]
        cosines = turn_cos[:, :, None, None]
        sines = turn_sin[:, :, None, None]
        turned_real = factor * (real * cosines - imag * sines)
        turned_imag = factor * (real * sines + imag * cosines)
        operand = jnp.concatenate([turned_real, -turned_imag], axis=1)
        upper = operand.astype(jnp.bfloat16)
        lower = (operand - upper.astype(jnp.float32)).astype(jnp.bfloat16)
        result = jnp.einsum("bmfh,am->hfab", upper, matrix, preferred_element_type=jnp.float32)
        result = result + jnp.einsum(
            "bmfh,am->hfab", lower, matrix, preferred_element_type=jnp.float32
        )
        return result.reshape(2, fields, points).astype(jnp.bfloat16)

    return lax.map(synthesise, (returned, matrices, twist_cos, twist_sin, point_counts))


def fits_on_chip(mesh, grid, waves, stiffness):
    owners = mesh.shape["lat"]
    pairs, fields = grid.shape[0] // owners, grid.shape[2] // mesh.shape["lev"]
    width, points = waves.shape[0], grid.shape[3]
    held = width // owners
    lanes = 2 * pairs * fields
    rest = lanes % LANES
    return (
        width % owners == 0
        and width % (2 * ROWS) == 0
        and width <= LANES
        and 4 * (pairs + 1) * LANES * points <= TABLE_BUDGET
        and points <= ROWS * LANES
        and points % (2 * ROWS) == 0
        and held <= ROWS
        and lanes >= LANES
        and (rest == 0 or rest % (2 * ROWS) == 0)
        and (rest == 0 or held <= (ROWS - held) * (LANES // rest))
        and 4 * fields <= LANES
        and fields % ROWS == 0
        and owners % (2 * ROWS) == 0
        and stiffness.shape[0] <= LANES
    )


def solution(mesh):
    in_specs = (P("lat", None, "lev", None), P("lat"), P(), P("lat", None, None), P("lat"), P())
    out_specs = P("lat", None, "lev", None)

    def program(grid, point_counts, waves, legendre, weights, stiffness):
        fits = fits_on_chip(mesh, grid, waves, stiffness)
        body = functools.partial(on_device, mesh) if fits else on_device_blocked
        return jax.shard_map(
            body, mesh=mesh, in_specs=in_specs, out_specs=out_specs, check_vma=False
        )(grid, point_counts, waves, legendre, weights, stiffness)

    return program
```

```python
import functools
import math

import jax
import jax.numpy as jnp
from jax import lax
from jax.experimental import pallas as pl
from jax.experimental.pallas import tpu as pltpu
from jax.sharding import PartitionSpec as P

TWO_PI = 2.0 * math.pi
FINE_STEPS = 32
LANES = 128
ROWS = 8
TABLE_BUDGET = 4 << 20
KERNEL_BYTES = 8 << 20

COS_TURN = (
    0.9999999998781397, -19.739208740145937, 64.9393888386778, -85.45665201444898,
    60.24205245141228, -26.404165331517056, 7.79855301354287, -1.4511773940976733,
)
SIN_TURN = (
    6.2831853022485955, -41.341700317335295, 81.60512671223316, -76.70292598092092,
    42.02516399730493, -14.896874459689428, 3.233831551278599,
)


def polynomial(coefficients, u):
    total = coefficients[-1] * u + coefficients[-2]
    for value in coefficients[-3::-1]:
        total = total * u + value
    return total


def cos_minus_sin(steps, count, inverse):
    reduced = steps - jnp.floor(steps * inverse + 0.5) * count
    turn = reduced * inverse
    square = turn * turn
    return polynomial(COS_TURN, square), -turn * polynomial(SIN_TURN, square)


def slot_choice(waves_ref, held, first, slots):
    width = waves_ref.shape[1]
    owners = slots // ROWS
    row = lax.broadcasted_iota(jnp.int32, (slots, width), 0)
    lane = lax.broadcasted_iota(jnp.int32, (slots, width), 1)
    place = row & (ROWS - 1)
    owner = (row >> 3) + first
    owner = jnp.where(owner >= owners, owner - owners, owner)
    chosen = (owner * held + place == lane) & (place < held)
    waves = jnp.broadcast_to(waves_ref[...].astype(jnp.float32) + 1.0, (slots, width))
    column = jnp.sum(jnp.where(chosen, waves, 0.0), axis=1, keepdims=True)
    mode = lax.broadcasted_iota(jnp.int32, (slots, LANES), 1).astype(jnp.float32) + 1.0
    return jnp.where(mode == column, 1.0, 0.0)


def segments(start, length):
    done = 0
    while done < length:
        block, lane = divmod(start + done, LANES)
        size = min(length - done, LANES - lane)
        yield block, lane, done, size
        done += size


def turn(x, shift, axis):
    shift %= x.shape[axis]
    return pltpu.roll(x, shift, axis) if shift else x


def rest_home(c, held, rest):
    fit = LANES // rest
    return held + c // fit, (c % fit) * rest


def rest_choices(choice, held, rest):
    owners = choice.shape[0] // ROWS
    grouped = choice.reshape(owners, ROWS, LANES)
    sublane = lax.broadcasted_iota(jnp.int32, (1, ROWS, LANES), 1)
    fit = LANES // rest
    out = []
    for group in range(min(fit, held)):
        total = jnp.zeros_like(grouped)
        for c in range(group, held, fit):
            row, _ = rest_home(c, held, rest)
            total = jnp.where(sublane == row, turn(grouped, row - c, 1), total)
        out.append(total.reshape(choice.shape))
    return out


def fill_tables(table_ref, width, least):
    candidates, _, padded = table_ref.shape
    blocks = padded // LANES
    sublane = lax.broadcasted_iota(jnp.int32, (ROWS, LANES), 0)
    lane = lax.broadcasted_iota(jnp.int32, (ROWS, LANES), 1)
    strides = (ROWS * (sublane * LANES + lane)).astype(jnp.float32)
    steps = [(sublane * (lane + b * LANES)).astype(jnp.float32) for b in range(blocks)]
    for i in range(candidates):
        count = jnp.full((1, LANES), (least + 4 * i).astype(jnp.float32))
        inverse = 1.0 / count
        stride_cos, stride_sin = cos_minus_sin(strides, count, inverse)
        for b in range(blocks):
            turn_cos, turn_sin = stride_cos[b : b + 1], stride_sin[b : b + 1]
            twice = turn_cos + turn_cos
            cosine, sine = cos_minus_sin(steps[b], count, inverse)
            cosines = [cosine, cosine * turn_cos - sine * turn_sin]
            sines = [sine, sine * turn_cos + cosine * turn_sin]
            while len(cosines) * ROWS < width:
                cosines.append(twice * cosines[-1] - cosines[-2])
                sines.append(twice * sines[-1] - sines[-2])
            at = pl.ds(b * LANES, LANES)
            for part, values in enumerate((cosines, sines)):
                rows = pl.ds(part * width, width)
                table_ref[i, rows, at] = jnp.concatenate(values, axis=0).astype(jnp.bfloat16)


def fill_turned(turned_ref, least):
    candidates, points, _ = turned_ref.shape
    sublane = lax.broadcasted_iota(jnp.int32, (ROWS, LANES), 0)
    lane = lax.broadcasted_iota(jnp.int32, (ROWS, LANES), 1)
    strides = (ROWS * lane).astype(jnp.float32)
    for i in range(candidates):
        count = jnp.full((1, LANES), (least + 4 * i).astype(jnp.float32))
        inverse = 1.0 / count
        turn_cos, turn_sin = cos_minus_sin(strides, count, inverse)
        twice = turn_cos + turn_cos
        for start in range(0, points, LANES):
            rows = min(LANES, points - start)
            steps = ((sublane + start) * lane).astype(jnp.float32)
            cosine, sine = cos_minus_sin(steps, count, inverse)
            cosines = [cosine, cosine * turn_cos - sine * turn_sin]
            sines = [sine, sine * turn_cos + cosine * turn_sin]
            while len(cosines) * ROWS < rows:
                cosines.append(twice * cosines[-1] - cosines[-2])
                sines.append(twice * sines[-1] - sines[-2])
            for part, values in enumerate((cosines, sines)):
                at = pl.ds(start, rows), pl.ds(part * LANES, LANES)
                turned_ref[i, at[0], at[1]] = jnp.concatenate(values, axis=0).astype(jnp.bfloat16)


def least_count(pairs):
    return 4 * pairs * lax.axis_index("lat") + 16


def candidate_of(count, j, least):
    return j + jnp.clip((count - least - 4 * j) >> 2, 0, 1)


def analysis_kernel(
    held, fields, first,
    counts_hbm, weights_hbm, waves_hbm, stiffness_hbm, basis_hbm, grid_hbm,
    coef_ref, table_ref, choice_ref, basis_ref, across_ref, wave_ref, stiffness_ref, limit_ref,
    counts, weights, waves, levels, values, given, widened, turned_ref, arrived, grid_arrived,
):
    owners, blocks = coef_ref.shape[:2]
    pairs = limit_ref.shape[0]
    slots = owners * ROWS
    width = basis_ref.shape[2]
    points = grid_hbm.shape[1]
    rows = grid_hbm.shape[0] // pairs
    rest = pairs * rows - blocks * LANES
    small = [
        pltpu.make_async_copy(source, target, arrived.at[k])
        for k, (source, target) in enumerate(
            [(counts_hbm, counts), (waves_hbm, waves), (weights_hbm, weights), (stiffness_hbm, levels)]
        )
    ]
    latitudes = [pl.ds(j * rows, rows) for j in range(pairs)]
    fields_in = [pltpu.make_async_copy(grid_hbm, values, grid_arrived)]
    basis_in = pltpu.make_async_copy(basis_hbm, given, arrived.at[len(small)])
    for copy in (*fields_in, *small, basis_in):
        copy.start()
    least = least_count(pairs)
    fill_turned(turned_ref, least)
    fill_tables(table_ref, width, least)
    small[1].wait()
    choice = slot_choice(waves, held, first, slots)
    choices = [choice] + (rest_choices(choice, held, rest) if rest else [])
    choices = [each.astype(jnp.bfloat16) for each in choices]
    for k, each in enumerate(choices):
        choice_ref[k * slots : (k + 1) * slots, :] = each
    lane = lax.broadcasted_iota(jnp.int32, (1, LANES), 1)
    for copy in (small[0], *small[2:], *fields_in):
        copy.wait()
    padding = jnp.zeros((1, LANES - width), jnp.float32)
    own_waves = jnp.concatenate([waves[...].astype(jnp.float32), padding], axis=1)
    own_waves = pltpu.roll(own_waves, (LANES - lax.axis_index("lat") * held) % LANES, 1)
    for c in range(held):
        wave_ref[c : c + 1, :] = jnp.broadcast_to(own_waves[:, c : c + 1], (1, LANES))
    all_levels = levels.shape[1]
    own = jnp.concatenate([levels[...], jnp.zeros((1, LANES - all_levels), jnp.float32)], axis=1)
    own = pltpu.roll(own, (LANES - lax.axis_index("lev") * fields) % LANES, 1)
    own = jnp.where(lane < fields, own, 0.0)
    stiffness = own
    for copy in range(1, 4):
        stiffness = stiffness + turn(own, copy * fields, 1)
    stiffness_ref[...] = stiffness
    position = lax.broadcasted_iota(jnp.int32, (1, points), 1)
    mode = lax.broadcasted_iota(jnp.int32, (1, 2 * LANES), 1) & (LANES - 1)
    pieces = []
    for j in range(pairs):
        limit_ref[j : j + 1, :] = jnp.full((1, LANES), counts[j].astype(jnp.float32))
        inside = jnp.where(position < counts[j], 1.0, 0.0).astype(jnp.bfloat16)
        product = jnp.dot(
            values[latitudes[j], :] * inside,
            turned_ref[candidate_of(counts[j], j, least)],
            preferred_element_type=jnp.float32,
        )
        scale = jnp.full((1, 1), weights[j]) / jnp.full((1, 1), counts[j].astype(jnp.float32))
        scale = jnp.where(2 * mode < counts[j], scale, 0.0)
        pieces.append((product * scale).astype(jnp.bfloat16))
    basis_in.wait()
    widened[...] = given[...].astype(jnp.float32)
    for c in range(held):
        ordered = []
        for j in range(pairs):
            strip = widened[c, pl.ds(j, owners, stride=pairs), :]
            ordered.append(turn(strip, -first, 0))
        ordered = jnp.concatenate(ordered, axis=0)
        basis_ref[c] = ordered.astype(jnp.bfloat16)
        across_ref[c] = ordered.T.astype(jnp.bfloat16)
    whole = jnp.concatenate(pieces, axis=0)
    parts = [whole[:, part * LANES : (part + 1) * LANES] for part in range(2)]
    for block in range(blocks):
        taken = [choices[0]]
        modes = [[part[block * LANES : (block + 1) * LANES] for part in parts]]
        if rest and block == blocks - 1:
            for group, each in enumerate(choices[1:]):
                taken.append(each)
                above = jnp.zeros((group * rest, LANES), jnp.bfloat16)
                below = jnp.zeros((LANES - (group + 1) * rest, LANES), jnp.bfloat16)
                modes.append(
                    [
                        jnp.concatenate(
                            [x for x in (above, part[blocks * LANES :], below) if x.shape[0]], axis=0
                        )
                        for part in parts
                    ]
                )
        placed = lax.dot_general(
            jnp.concatenate(taken, axis=1),
            jnp.concatenate([jnp.concatenate(both, axis=0) for both in modes], axis=1),
            (((1,), (1,)), ((), ())),
            preferred_element_type=jnp.float32,
        )
        for part in range(2):
            strip = placed[:, part * LANES : (part + 1) * LANES]
            coef_ref[:, block, part] = strip.reshape(owners, ROWS, LANES).astype(jnp.bfloat16)


def legendre_kernel(
    held, fields, wave_ref, stiffness_ref, basis_ref, across_ref, recv_ref, send_ref, fan_in, fan_out
):
    owners, blocks = recv_ref.shape[:2]
    latitudes, width = basis_ref.shape[1:]
    pairs = latitudes // owners
    rows = 2 * fields
    rest = pairs * rows - blocks * LANES
    for block in range(blocks):
        for part in range(2):
            plane = recv_ref[:, block, part].astype(jnp.float32).reshape(owners * ROWS, LANES)
            fan_in[block * 2 + part] = plane

    def chunk_rows(block, part, row):
        return block * 2 + part, pl.ds(row, owners, stride=ROWS), slice(None)

    def home(c, block, lane):
        if block == blocks:
            row, start = rest_home(c, held, rest)
            return row, block - 1, start + lane
        return c, block, lane

    lane_at = lax.broadcasted_iota(jnp.int32, (1, LANES), 1)
    south = ((lane_at >= fields) & (lane_at < 2 * fields)) | (lane_at >= 3 * fields)
    offset = lax.broadcasted_iota(jnp.int32, (width, 1), 0)
    parity = jnp.where((offset & 1) == 0, 1.0, -1.0)
    offset = offset.astype(jnp.float32)
    empty = jnp.zeros((owners, LANES), jnp.float32)
    folded = {}
    for c in range(held):
        wave = wave_ref[c : c + 1, :]
        degree = offset + wave
        basis = basis_ref[c]
        strips = []
        for j in range(pairs):
            strip = empty
            for part in range(2):
                for block, lane, place, size in segments(j * rows, rows):
                    row, block, lane = home(c, block, lane)
                    source = fan_in[chunk_rows(block, part, row)]
                    target = part * rows + place
                    here = (lane_at >= target) & (lane_at < target + size)
                    strip = jnp.where(here, turn(source, target - lane, 1), strip)
            strips.append(strip.astype(jnp.bfloat16))
        spectra = jnp.dot(
            across_ref[c], jnp.concatenate(strips, axis=0), preferred_element_type=jnp.float32
        )
        factor = 1.0 / (1.0 + stiffness_ref[...] * degree * (degree + 1.0))
        damping = jnp.where(degree < float(width), factor, 0.0)
        other = jnp.where(south, turn(spectra, fields, 1), turn(spectra, -fields, 1))
        scaled = ((spectra + parity * other) * damping).astype(jnp.bfloat16)
        returned = jnp.dot(basis, scaled, preferred_element_type=jnp.float32)
        returned = returned * jnp.where(wave == 0.0, 1.0, 2.0)
        for part in range(2):
            built = {}
            for j in range(pairs):
                strip = returned[j * owners : (j + 1) * owners]
                for block, lane, place, size in segments(j * rows, rows):
                    row, block, lane = home(c, block, lane)
                    key = (block, part, row)
                    here = (lane_at >= lane) & (lane_at < lane + size)
                    moved = turn(strip, lane - part * rows - place, 1)
                    held_in = folded if row >= held else built
                    held_in[key] = jnp.where(here, moved, held_in.get(key, empty))
            for key, value in built.items():
                fan_out[chunk_rows(*key)] = value
    for block in range(blocks):
        for part in range(2):
            for row in range(held, ROWS):
                key = (block, part, row)
                fan_out[chunk_rows(*key)] = folded.get(key, empty)
    for block in range(blocks):
        for part in range(2):
            plane = fan_out[block * 2 + part].reshape(owners, ROWS, LANES)
            send_ref[:, block, part] = plane.astype(jnp.bfloat16)


def synthesis_kernel(
    held, limit_ref, choice_ref, recv_ref, table_ref, grid_hbm, values, left
):
    owners, blocks = recv_ref.shape[:2]
    pairs = limit_ref.shape[0]
    slots = owners * ROWS
    width = table_ref.shape[1] // 2
    points = grid_hbm.shape[1]
    rows = grid_hbm.shape[0] // pairs
    rest = pairs * rows - blocks * LANES
    least = least_count(pairs)
    operands = []
    for part in range(2):
        turned = []
        for block in range(blocks):
            plane = recv_ref[:, block, part].astype(jnp.float32).reshape(slots, LANES)
            turned.append(plane.T.astype(jnp.bfloat16))
        found = [
            jnp.dot(
                jnp.concatenate(turned, axis=0),
                choice_ref[:slots, :],
                preferred_element_type=jnp.float32,
            )
        ]
        if rest:
            groups = choice_ref.shape[0] // slots - 1
            folded = [turned[-1][group * rest : (group + 1) * rest] for group in range(groups)]
            found.append(
                jnp.dot(
                    jnp.concatenate(folded, axis=1),
                    choice_ref[slots:, :],
                    preferred_element_type=jnp.float32,
                )
            )
        operands.append(jnp.concatenate(found, axis=0))
    position = lax.broadcasted_iota(jnp.int32, (1, points), 1).astype(jnp.float32)
    mode = lax.broadcasted_iota(jnp.int32, (1, LANES), 1).astype(jnp.float32)
    copies = []
    for j in range(pairs):
        end = limit_ref[j : j + 1, :]
        at = pl.ds(j * rows, rows)
        candidate = candidate_of(jnp.max(end).astype(jnp.int32), j, least)
        product = None
        for part in range(2):
            operand = operands[part][j * rows : (j + 1) * rows]
            operand = jnp.where(2.0 * mode < end, operand, 0.0).astype(jnp.bfloat16)
            term = jnp.dot(
                operand[:, :width],
                table_ref[candidate, part * width : (part + 1) * width, :],
                preferred_element_type=jnp.float32,
            )
            product = term if product is None else product + term
        kept = jnp.where(position < end[:, :1], product[:, :points], 0.0)
        values[at, :] = kept.astype(jnp.bfloat16)
        copies.append(pltpu.make_async_copy(values.at[at, :], grid_hbm.at[at, :], left.at[j]))
        copies[-1].start()
    for copy in copies:
        copy.wait()


def on_device(mesh, grid, point_counts, waves, legendre, weights, stiffness):
    pairs, _, fields, points = grid.shape
    width = waves.shape[0]
    owners = mesh.shape["lat"]
    held = width // owners
    slots = owners * ROWS
    rows = 2 * fields
    padded = -(-points // LANES) * LANES
    blocks = pairs * rows // LANES
    rest = pairs * rows % LANES
    choices = 1 + (min(LANES // rest, held) if rest else 0)
    first = 11 * owners // 16
    groups = [[(place + first) % owners for place in range(owners)]]
    vmem = pl.BlockSpec(memory_space=pltpu.VMEM)
    hbm = pl.BlockSpec(memory_space=pltpu.HBM)
    limits = pltpu.CompilerParams(vmem_limit_bytes=KERNEL_BYTES)
    exchanged = jax.ShapeDtypeStruct((owners, blocks, 2, ROWS, LANES), jnp.bfloat16)
    coefficients, tables, choice, basis, across, wave_rows, levels, ends = pl.pallas_call(
        functools.partial(analysis_kernel, held, fields, first),
        out_shape=(
            exchanged,
            jax.ShapeDtypeStruct((pairs + 1, 2 * width, padded), jnp.bfloat16),
            jax.ShapeDtypeStruct((choices * slots, LANES), jnp.bfloat16),
            jax.ShapeDtypeStruct(legendre.shape, jnp.bfloat16),
            jax.ShapeDtypeStruct((held, legendre.shape[2], legendre.shape[1]), jnp.bfloat16),
            jax.ShapeDtypeStruct((held, LANES), jnp.float32),
            jax.ShapeDtypeStruct((1, LANES), jnp.float32),
            jax.ShapeDtypeStruct((pairs, LANES), jnp.float32),
        ),
        in_specs=[hbm] * 6,
        out_specs=(vmem,) * 8,
        scratch_shapes=[
            pltpu.SMEM((pairs,), jnp.int32),
            pltpu.SMEM((pairs,), jnp.float32),
            pltpu.VMEM((1, width), jnp.int32),
            pltpu.VMEM((1, stiffness.shape[0]), jnp.float32),
            pltpu.VMEM((pairs * rows, points), jnp.bfloat16),
            pltpu.VMEM(legendre.shape, jnp.bfloat16),
            pltpu.VMEM(legendre.shape, jnp.float32),
            pltpu.VMEM((pairs + 1, points, 2 * LANES), jnp.bfloat16),
            pltpu.SemaphoreType.DMA((5,)),
            pltpu.SemaphoreType.DMA,
        ],
        compiler_params=limits,
        name="analysis",
    )(
        *(
            pltpu.with_memory_space_constraint(array, pltpu.HBM)
            for array in (
                point_counts, weights, waves.reshape(1, width), stiffness.reshape(1, -1), legendre,
                grid.reshape(pairs * rows, points),
            )
        )
    )

    def exchange(array):
        return lax.all_to_all(
            array, "lat", split_axis=0, concat_axis=0, axis_index_groups=groups, tiled=True
        )

    synthesised = pl.pallas_call(
        functools.partial(legendre_kernel, held, fields),
        out_shape=exchanged,
        in_specs=[vmem] * 5,
        out_specs=vmem,
        scratch_shapes=[
            pltpu.VMEM((blocks * 2, slots, LANES), jnp.float32),
            pltpu.VMEM((blocks * 2, slots, LANES), jnp.float32),
        ],
        compiler_params=limits,
        name="legendre",
    )(wave_rows, levels, basis, across, exchange(coefficients))
    result = pl.pallas_call(
        functools.partial(synthesis_kernel, held),
        out_shape=jax.ShapeDtypeStruct((pairs * rows, points), jnp.bfloat16),
        in_specs=[vmem] * 4,
        out_specs=hbm,
        scratch_shapes=[
            pltpu.VMEM((pairs * rows, points), jnp.bfloat16),
            pltpu.SemaphoreType.DMA((pairs,)),
        ],
        compiler_params=limits,
        name="synthesis",
    )(ends, choice, exchange(synthesised), tables)
    return result.reshape(grid.shape)


def fourier_tables(count, wavenumbers, quarter_max):
    quarter = count // 4
    step_angle = TWO_PI / quarter.astype(jnp.float32)
    coarse_count = (quarter_max + FINE_STEPS - 1) // FINE_STEPS
    coarse_pos = FINE_STEPS * jnp.arange(coarse_count, dtype=jnp.int32)
    fine_pos = jnp.arange(FINE_STEPS, dtype=jnp.int32)
    coarse_angle = (coarse_pos[:, None] * wavenumbers[None, :] % quarter).astype(
        jnp.float32
    ) * step_angle
    fine_angle = (fine_pos[:, None] * wavenumbers[None, :] % quarter).astype(
        jnp.float32
    ) * step_angle
    coarse_cos = jnp.cos(coarse_angle)[:, None, :]
    coarse_sin = jnp.sin(coarse_angle)[:, None, :]
    fine_cos = jnp.cos(fine_angle)[None, :, :]
    fine_sin = jnp.sin(fine_angle)[None, :, :]
    full_cos = (coarse_cos * fine_cos - coarse_sin * fine_sin).reshape(
        coarse_count * FINE_STEPS, -1
    )[:quarter_max]
    full_sin = (coarse_sin * fine_cos + coarse_cos * fine_sin).reshape(
        coarse_count * FINE_STEPS, -1
    )[:quarter_max]
    positions = jnp.arange(quarter_max, dtype=jnp.int32)
    inside = (positions < quarter)[:, None]
    cosine = jnp.where(inside, full_cos, 0.0)
    sine = jnp.where(inside, full_sin, 0.0)
    matrix = jnp.concatenate([cosine, sine], axis=1).astype(jnp.bfloat16)
    offsets = jnp.arange(4, dtype=jnp.int32)
    twist = offsets[:, None] * wavenumbers[None, :] % count
    theta = twist.astype(jnp.float32) * (TWO_PI / count.astype(jnp.float32))
    return (matrix, jnp.cos(theta), jnp.sin(theta))


def helmholtz(spectra, wavenumbers, offsets, stiffness_local, width):
    full_shape = spectra.shape
    quartered = spectra.reshape(full_shape[:-2] + (full_shape[-2] // 4, 2, 2, full_shape[-1]))
    parity = (1 - 2 * (offsets % 2)).astype(jnp.float32)
    combined = quartered[..., 0, :] + parity * quartered[..., 1, :]
    degrees = (wavenumbers + offsets).astype(jnp.float32)
    inside_band = offsets < width - wavenumbers
    factor = 1.0 / (
        1.0 + stiffness_local[:, None] * degrees[..., None, :] * (degrees[..., None, :] + 1.0)
    )
    damping = jnp.where(inside_band[..., None, :], factor, 0.0)
    scaled = (combined * damping[..., :, None, :]).astype(jnp.bfloat16)
    flipped = scaled * parity.astype(jnp.bfloat16)
    return jnp.stack([scaled, flipped], axis=-2).reshape(full_shape)


def spectral(received, wavenumbers, basis, stiffness_local):
    width = basis.shape[2]
    spectra = jnp.einsum("jcr,cjl->crl", received, basis, preferred_element_type=jnp.float32)
    offsets = jnp.arange(width, dtype=jnp.int32)
    operand = helmholtz(spectra, wavenumbers[:, None], offsets, stiffness_local, width)
    returned = jnp.einsum("crl,cjl->jcr", operand, basis, preferred_element_type=jnp.float32)
    return returned.astype(jnp.bfloat16)


def on_device_blocked(grid, point_counts, waves, legendre, weights, stiffness):
    pairs, _, fields, points = grid.shape
    quarter_max = points // 4
    width = waves.shape[0]
    held_slots = legendre.shape[0]
    lat_index = lax.axis_index("lat")
    lev_index = lax.axis_index("lev")

    def analyse(pieces):
        latitude, count, weight = pieces
        matrix, twist_cos, twist_sin = fourier_tables(count, waves, quarter_max)
        values = latitude.reshape(2, fields, quarter_max, 4)
        partial_value = jnp.einsum(
            "hfab,at->hfbt", values, matrix, preferred_element_type=jnp.float32
        )
        cos_part = partial_value[..., :width]
        sin_part = partial_value[..., width:]
        real = jnp.sum(twist_cos * cos_part - twist_sin * sin_part, axis=2)
        imag = -jnp.sum(twist_sin * cos_part + twist_cos * sin_part, axis=2)
        factor = jnp.where(2 * waves < count, weight / count.astype(jnp.float32), 0.0)
        stacked = jnp.stack([real * factor, imag * factor], axis=0)
        packed = jnp.transpose(stacked, (3, 2, 0, 1)).reshape(width, 4 * fields)
        return (packed.astype(jnp.bfloat16), matrix, twist_cos, twist_sin)

    coefficients, matrices, twist_cos, twist_sin = lax.map(analyse, (grid, point_counts, weights))
    received = lax.all_to_all(coefficients, "lat", split_axis=1, concat_axis=0, tiled=True)
    owned = lax.dynamic_slice_in_dim(waves, lat_index * held_slots, held_slots)
    own_stiffness = lax.dynamic_slice_in_dim(stiffness, lev_index * fields, fields)
    synthesised = spectral(received, owned, legendre, own_stiffness)
    returned = lax.all_to_all(synthesised, "lat", split_axis=0, concat_axis=1, tiled=True)

    def synthesise(pieces):
        packed, matrix, turn_cos, turn_sin, count = pieces
        values = packed.astype(jnp.float32).reshape(width, fields, 2, 2)
        real = values[:, :, 0, :]
        imag = values[:, :, 1, :]
        factor = jnp.where(2 * waves < count, jnp.where(waves == 0, 1.0, 2.0), 0.0)[:, None, None]
        cosines = turn_cos[:, :, None, None]
        sines = turn_sin[:, :, None, None]
        turned_real = factor * (real * cosines - imag * sines)
        turned_imag = factor * (real * sines + imag * cosines)
        operand = jnp.concatenate([turned_real, -turned_imag], axis=1)
        upper = operand.astype(jnp.bfloat16)
        lower = (operand - upper.astype(jnp.float32)).astype(jnp.bfloat16)
        result = jnp.einsum("bmfh,am->hfab", upper, matrix, preferred_element_type=jnp.float32)
        result = result + jnp.einsum(
            "bmfh,am->hfab", lower, matrix, preferred_element_type=jnp.float32
        )
        return result.reshape(2, fields, points).astype(jnp.bfloat16)

    return lax.map(synthesise, (returned, matrices, twist_cos, twist_sin, point_counts))


def fits_on_chip(mesh, grid, waves, stiffness):
    owners = mesh.shape["lat"]
    pairs, fields = grid.shape[0] // owners, grid.shape[2] // mesh.shape["lev"]
    width, points = waves.shape[0], grid.shape[3]
    held = width // owners
    lanes = 2 * pairs * fields
    rest = lanes % LANES
    return (
        width % owners == 0
        and width % (2 * ROWS) == 0
        and width <= LANES
        and 4 * (pairs + 1) * LANES * points <= TABLE_BUDGET
        and points <= ROWS * LANES
        and points % (2 * ROWS) == 0
        and held <= ROWS
        and lanes >= LANES
        and (rest == 0 or rest % (2 * ROWS) == 0)
        and (rest == 0 or held <= (ROWS - held) * (LANES // rest))
        and 4 * fields <= LANES
        and fields % ROWS == 0
        and owners % (2 * ROWS) == 0
        and stiffness.shape[0] <= LANES
    )


def solution(mesh):
    in_specs = (P("lat", None, "lev", None), P("lat"), P(), P("lat", None, None), P("lat"), P())
    out_specs = P("lat", None, "lev", None)

    def program(grid, point_counts, waves, legendre, weights, stiffness):
        fits = fits_on_chip(mesh, grid, waves, stiffness)
        body = functools.partial(on_device, mesh) if fits else on_device_blocked
        return jax.shard_map(
            body, mesh=mesh, in_specs=in_specs, out_specs=out_specs, check_vma=False
        )(grid, point_counts, waves, legendre, weights, stiffness)

    return program
```

```python
import functools
import math

import jax
import jax.numpy as jnp
from jax import lax
from jax.experimental import pallas as pl
from jax.experimental.pallas import tpu as pltpu
from jax.sharding import PartitionSpec as P

TWO_PI = 2.0 * math.pi
FINE_STEPS = 32
LANES = 128
ROWS = 8
TABLE_BUDGET = 4 << 20
KERNEL_BYTES = 8 << 20

COS_TURN = (
    0.9999999998781397, -19.739208740145937, 64.9393888386778, -85.45665201444898,
    60.24205245141228, -26.404165331517056, 7.79855301354287, -1.4511773940976733,
)
SIN_TURN = (
    6.2831853022485955, -41.341700317335295, 81.60512671223316, -76.70292598092092,
    42.02516399730493, -14.896874459689428, 3.233831551278599,
)


def polynomial(coefficients, u):
    total = coefficients[-1] * u + coefficients[-2]
    for value in coefficients[-3::-1]:
        total = total * u + value
    return total


def cos_minus_sin(steps, count, inverse):
    reduced = steps - jnp.floor(steps * inverse + 0.5) * count
    turn = reduced * inverse
    square = turn * turn
    return polynomial(COS_TURN, square), -turn * polynomial(SIN_TURN, square)


def slot_choice(waves_ref, held, first, slots):
    width = waves_ref.shape[1]
    owners = slots // ROWS
    row = lax.broadcasted_iota(jnp.int32, (slots, width), 0)
    lane = lax.broadcasted_iota(jnp.int32, (slots, width), 1)
    place = row & (ROWS - 1)
    owner = (row >> 3) + first
    owner = jnp.where(owner >= owners, owner - owners, owner)
    chosen = (owner * held + place == lane) & (place < held)
    waves = jnp.broadcast_to(waves_ref[...].astype(jnp.float32) + 1.0, (slots, width))
    column = jnp.sum(jnp.where(chosen, waves, 0.0), axis=1, keepdims=True)
    mode = lax.broadcasted_iota(jnp.int32, (slots, LANES), 1).astype(jnp.float32) + 1.0
    return jnp.where(mode == column, 1.0, 0.0)


def segments(start, length):
    done = 0
    while done < length:
        block, lane = divmod(start + done, LANES)
        size = min(length - done, LANES - lane)
        yield block, lane, done, size
        done += size


def turn(x, shift, axis):
    shift %= x.shape[axis]
    return pltpu.roll(x, shift, axis) if shift else x


def rest_home(c, held, rest):
    fit = LANES // rest
    return held + c // fit, (c % fit) * rest


def rest_choices(choice, held, rest):
    owners = choice.shape[0] // ROWS
    grouped = choice.reshape(owners, ROWS, LANES)
    sublane = lax.broadcasted_iota(jnp.int32, (1, ROWS, LANES), 1)
    fit = LANES // rest
    out = []
    for group in range(min(fit, held)):
        total = jnp.zeros_like(grouped)
        for c in range(group, held, fit):
            row, _ = rest_home(c, held, rest)
            total = jnp.where(sublane == row, turn(grouped, row - c, 1), total)
        out.append(total.reshape(choice.shape))
    return out


def fill_tables(table_ref, width, least):
    candidates, _, padded = table_ref.shape
    blocks = padded // LANES
    sublane = lax.broadcasted_iota(jnp.int32, (ROWS, LANES), 0)
    lane = lax.broadcasted_iota(jnp.int32, (ROWS, LANES), 1)
    strides = (ROWS * (sublane * LANES + lane)).astype(jnp.float32)
    steps = [(sublane * (lane + b * LANES)).astype(jnp.float32) for b in range(blocks)]
    for i in range(candidates):
        count = jnp.full((1, LANES), (least + 4 * i).astype(jnp.float32))
        inverse = 1.0 / count
        stride_cos, stride_sin = cos_minus_sin(strides, count, inverse)
        for b in range(blocks):
            turn_cos, turn_sin = stride_cos[b : b + 1], stride_sin[b : b + 1]
            twice = turn_cos + turn_cos
            cosine, sine = cos_minus_sin(steps[b], count, inverse)
            cosines = [cosine, cosine * turn_cos - sine * turn_sin]
            sines = [sine, sine * turn_cos + cosine * turn_sin]
            while len(cosines) * ROWS < width:
                cosines.append(twice * cosines[-1] - cosines[-2])
                sines.append(twice * sines[-1] - sines[-2])
            at = pl.ds(b * LANES, LANES)
            for part, values in enumerate((cosines, sines)):
                rows = pl.ds(part * width, width)
                table_ref[i, rows, at] = jnp.concatenate(values, axis=0).astype(jnp.bfloat16)


def fill_turned(turned_ref, least):
    candidates, points, _ = turned_ref.shape
    sublane = lax.broadcasted_iota(jnp.int32, (ROWS, LANES), 0)
    lane = lax.broadcasted_iota(jnp.int32, (ROWS, LANES), 1)
    strides = (ROWS * lane).astype(jnp.float32)
    for i in range(candidates):
        count = jnp.full((1, LANES), (least + 4 * i).astype(jnp.float32))
        inverse = 1.0 / count
        turn_cos, turn_sin = cos_minus_sin(strides, count, inverse)
        twice = turn_cos + turn_cos
        for start in range(0, points, LANES):
            rows = min(LANES, points - start)
            steps = ((sublane + start) * lane).astype(jnp.float32)
            cosine, sine = cos_minus_sin(steps, count, inverse)
            cosines = [cosine, cosine * turn_cos - sine * turn_sin]
            sines = [sine, sine * turn_cos + cosine * turn_sin]
            while len(cosines) * ROWS < rows:
                cosines.append(twice * cosines[-1] - cosines[-2])
                sines.append(twice * sines[-1] - sines[-2])
            for part, values in enumerate((cosines, sines)):
                at = pl.ds(start, rows), pl.ds(part * LANES, LANES)
                turned_ref[i, at[0], at[1]] = jnp.concatenate(values, axis=0).astype(jnp.bfloat16)


def least_count(pairs):
    return 4 * pairs * lax.axis_index("lat") + 16


def candidate_of(count, j, least):
    return j + jnp.clip((count - least - 4 * j) >> 2, 0, 1)


def analysis_kernel(
    held, fields, first,
    counts_hbm, weights_hbm, waves_hbm, stiffness_hbm, basis_hbm, grid_hbm,
    coef_ref, table_ref, choice_ref, basis_ref, across_ref, wave_ref, damping_ref, limit_ref,
    counts, weights, waves, levels, values, given, widened, turned_ref, arrived, grid_arrived,
):
    owners, blocks = coef_ref.shape[:2]
    pairs = limit_ref.shape[0]
    slots = owners * ROWS
    width = basis_ref.shape[2]
    points = grid_hbm.shape[1]
    rows = grid_hbm.shape[0] // pairs
    rest = pairs * rows - blocks * LANES
    small = [
        pltpu.make_async_copy(source, target, arrived.at[k])
        for k, (source, target) in enumerate(
            [(counts_hbm, counts), (waves_hbm, waves), (weights_hbm, weights), (stiffness_hbm, levels)]
        )
    ]
    latitudes = [pl.ds(j * rows, rows) for j in range(pairs)]
    fields_in = [pltpu.make_async_copy(grid_hbm, values, grid_arrived)]
    basis_in = pltpu.make_async_copy(basis_hbm, given, arrived.at[len(small)])
    for copy in (*fields_in, *small, basis_in):
        copy.start()
    least = least_count(pairs)
    fill_turned(turned_ref, least)
    fill_tables(table_ref, width, least)
    small[1].wait()
    choice = slot_choice(waves, held, first, slots)
    choices = [choice] + (rest_choices(choice, held, rest) if rest else [])
    choices = [each.astype(jnp.bfloat16) for each in choices]
    for k, each in enumerate(choices):
        choice_ref[k * slots : (k + 1) * slots, :] = each
    lane = lax.broadcasted_iota(jnp.int32, (1, LANES), 1)
    for copy in (small[0], *small[2:], *fields_in):
        copy.wait()
    padding = jnp.zeros((1, LANES - width), jnp.float32)
    own_waves = jnp.concatenate([waves[...].astype(jnp.float32), padding], axis=1)
    own_waves = pltpu.roll(own_waves, (LANES - lax.axis_index("lat") * held) % LANES, 1)
    for c in range(held):
        wave_ref[c : c + 1, :] = jnp.broadcast_to(own_waves[:, c : c + 1], (1, LANES))
    all_levels = levels.shape[1]
    own = jnp.concatenate([levels[...], jnp.zeros((1, LANES - all_levels), jnp.float32)], axis=1)
    own = pltpu.roll(own, (LANES - lax.axis_index("lev") * fields) % LANES, 1)
    own = jnp.where(lane < fields, own, 0.0)
    stiffness = own
    for copy in range(1, 4):
        stiffness = stiffness + turn(own, copy * fields, 1)
    degree_step = lax.broadcasted_iota(jnp.int32, (width, 1), 0).astype(jnp.float32)
    for c in range(held):
        degree = degree_step + own_waves[:, c : c + 1]
        factor = 1.0 / (1.0 + stiffness * degree * (degree + 1.0))
        damping_ref[c] = jnp.where(degree < float(width), factor, 0.0)
    position = lax.broadcasted_iota(jnp.int32, (1, points), 1)
    mode = lax.broadcasted_iota(jnp.int32, (1, 2 * LANES), 1) & (LANES - 1)
    pieces = []
    for j in range(pairs):
        limit_ref[j : j + 1, :] = jnp.full((1, LANES), counts[j].astype(jnp.float32))
        inside = jnp.where(position < counts[j], 1.0, 0.0).astype(jnp.bfloat16)
        product = jnp.dot(
            values[latitudes[j], :] * inside,
            turned_ref[candidate_of(counts[j], j, least)],
            preferred_element_type=jnp.float32,
        )
        scale = jnp.full((1, 1), weights[j]) / jnp.full((1, 1), counts[j].astype(jnp.float32))
        scale = jnp.where(2 * mode < counts[j], scale, 0.0)
        pieces.append((product * scale).astype(jnp.bfloat16))
    basis_in.wait()
    widened[...] = given[...].astype(jnp.float32)
    for c in range(held):
        ordered = []
        for j in range(pairs):
            strip = widened[c, pl.ds(j, owners, stride=pairs), :]
            ordered.append(turn(strip, -first, 0))
        ordered = jnp.concatenate(ordered, axis=0)
        basis_ref[c] = ordered.astype(jnp.bfloat16)
        across_ref[c] = ordered.T.astype(jnp.bfloat16)
    whole = jnp.concatenate(pieces, axis=0)
    parts = [whole[:, part * LANES : (part + 1) * LANES] for part in range(2)]
    for block in range(blocks):
        taken = [choices[0]]
        modes = [[part[block * LANES : (block + 1) * LANES] for part in parts]]
        if rest and block == blocks - 1:
            for group, each in enumerate(choices[1:]):
                taken.append(each)
                above = jnp.zeros((group * rest, LANES), jnp.bfloat16)
                below = jnp.zeros((LANES - (group + 1) * rest, LANES), jnp.bfloat16)
                modes.append(
                    [
                        jnp.concatenate(
                            [x for x in (above, part[blocks * LANES :], below) if x.shape[0]], axis=0
                        )
                        for part in parts
                    ]
                )
        placed = lax.dot_general(
            jnp.concatenate(taken, axis=1),
            jnp.concatenate([jnp.concatenate(both, axis=0) for both in modes], axis=1),
            (((1,), (1,)), ((), ())),
            preferred_element_type=jnp.float32,
        )
        for part in range(2):
            strip = placed[:, part * LANES : (part + 1) * LANES]
            coef_ref[:, block, part] = strip.reshape(owners, ROWS, LANES).astype(jnp.bfloat16)


def legendre_kernel(
    held, fields, wave_ref, damping_ref, basis_ref, across_ref, recv_ref, send_ref, fan_in, fan_out
):
    owners, blocks = recv_ref.shape[:2]
    latitudes, width = basis_ref.shape[1:]
    pairs = latitudes // owners
    rows = 2 * fields
    rest = pairs * rows - blocks * LANES
    for block in range(blocks):
        for part in range(2):
            plane = recv_ref[:, block, part].astype(jnp.float32).reshape(owners * ROWS, LANES)
            fan_in[block * 2 + part] = plane

    def chunk_rows(block, part, row):
        return block * 2 + part, pl.ds(row, owners, stride=ROWS), slice(None)

    def home(c, block, lane):
        if block == blocks:
            row, start = rest_home(c, held, rest)
            return row, block - 1, start + lane
        return c, block, lane

    lane_at = lax.broadcasted_iota(jnp.int32, (1, LANES), 1)
    south = ((lane_at >= fields) & (lane_at < 2 * fields)) | (lane_at >= 3 * fields)
    offset = lax.broadcasted_iota(jnp.int32, (width, 1), 0)
    parity = jnp.where((offset & 1) == 0, 1.0, -1.0)
    empty = jnp.zeros((owners, LANES), jnp.float32)
    folded = {}
    for c in range(held):
        wave = wave_ref[c : c + 1, :]
        basis = basis_ref[c]
        strips = []
        for j in range(pairs):
            strip = empty
            for part in range(2):
                for block, lane, place, size in segments(j * rows, rows):
                    row, block, lane = home(c, block, lane)
                    source = fan_in[chunk_rows(block, part, row)]
                    target = part * rows + place
                    here = (lane_at >= target) & (lane_at < target + size)
                    strip = jnp.where(here, turn(source, target - lane, 1), strip)
            strips.append(strip.astype(jnp.bfloat16))
        spectra = jnp.dot(
            across_ref[c], jnp.concatenate(strips, axis=0), preferred_element_type=jnp.float32
        )
        other = jnp.where(south, turn(spectra, fields, 1), turn(spectra, -fields, 1))
        scaled = ((spectra + parity * other) * damping_ref[c]).astype(jnp.bfloat16)
        returned = jnp.dot(basis, scaled, preferred_element_type=jnp.float32)
        returned = returned * jnp.where(wave == 0.0, 1.0, 2.0)
        for part in range(2):
            built = {}
            for j in range(pairs):
                strip = returned[j * owners : (j + 1) * owners]
                for block, lane, place, size in segments(j * rows, rows):
                    row, block, lane = home(c, block, lane)
                    key = (block, part, row)
                    here = (lane_at >= lane) & (lane_at < lane + size)
                    moved = turn(strip, lane - part * rows - place, 1)
                    held_in = folded if row >= held else built
                    held_in[key] = jnp.where(here, moved, held_in.get(key, empty))
            for key, value in built.items():
                fan_out[chunk_rows(*key)] = value
    for block in range(blocks):
        for part in range(2):
            for row in range(held, ROWS):
                key = (block, part, row)
                fan_out[chunk_rows(*key)] = folded.get(key, empty)
    for block in range(blocks):
        for part in range(2):
            plane = fan_out[block * 2 + part].reshape(owners, ROWS, LANES)
            send_ref[:, block, part] = plane.astype(jnp.bfloat16)


def synthesis_kernel(
    held, limit_ref, choice_ref, recv_ref, table_ref, grid_hbm, values, left
):
    owners, blocks = recv_ref.shape[:2]
    pairs = limit_ref.shape[0]
    slots = owners * ROWS
    width = table_ref.shape[1] // 2
    points = grid_hbm.shape[1]
    rows = grid_hbm.shape[0] // pairs
    rest = pairs * rows - blocks * LANES
    least = least_count(pairs)
    operands = []
    for part in range(2):
        turned = []
        for block in range(blocks):
            plane = recv_ref[:, block, part].astype(jnp.float32).reshape(slots, LANES)
            turned.append(plane.T.astype(jnp.bfloat16))
        found = [
            jnp.dot(
                jnp.concatenate(turned, axis=0),
                choice_ref[:slots, :],
                preferred_element_type=jnp.float32,
            )
        ]
        if rest:
            groups = choice_ref.shape[0] // slots - 1
            folded = [turned[-1][group * rest : (group + 1) * rest] for group in range(groups)]
            found.append(
                jnp.dot(
                    jnp.concatenate(folded, axis=1),
                    choice_ref[slots:, :],
                    preferred_element_type=jnp.float32,
                )
            )
        operands.append(jnp.concatenate(found, axis=0))
    position = lax.broadcasted_iota(jnp.int32, (1, points), 1).astype(jnp.float32)
    mode = lax.broadcasted_iota(jnp.int32, (1, LANES), 1).astype(jnp.float32)
    copies = []
    for j in range(pairs):
        end = limit_ref[j : j + 1, :]
        at = pl.ds(j * rows, rows)
        candidate = candidate_of(jnp.max(end).astype(jnp.int32), j, least)
        product = None
        for part in range(2):
            operand = operands[part][j * rows : (j + 1) * rows]
            operand = jnp.where(2.0 * mode < end, operand, 0.0).astype(jnp.bfloat16)
            term = jnp.dot(
                operand[:, :width],
                table_ref[candidate, part * width : (part + 1) * width, :],
                preferred_element_type=jnp.float32,
            )
            product = term if product is None else product + term
        kept = jnp.where(position < end[:, :1], product[:, :points], 0.0)
        values[at, :] = kept.astype(jnp.bfloat16)
        copies.append(pltpu.make_async_copy(values.at[at, :], grid_hbm.at[at, :], left.at[j]))
        copies[-1].start()
    for copy in copies:
        copy.wait()


def on_device(mesh, grid, point_counts, waves, legendre, weights, stiffness):
    pairs, _, fields, points = grid.shape
    width = waves.shape[0]
    owners = mesh.shape["lat"]
    held = width // owners
    slots = owners * ROWS
    rows = 2 * fields
    padded = -(-points // LANES) * LANES
    blocks = pairs * rows // LANES
    rest = pairs * rows % LANES
    choices = 1 + (min(LANES // rest, held) if rest else 0)
    first = 11 * owners // 16
    groups = [[(place + first) % owners for place in range(owners)]]
    vmem = pl.BlockSpec(memory_space=pltpu.VMEM)
    hbm = pl.BlockSpec(memory_space=pltpu.HBM)
    limits = pltpu.CompilerParams(vmem_limit_bytes=KERNEL_BYTES)
    exchanged = jax.ShapeDtypeStruct((owners, blocks, 2, ROWS, LANES), jnp.bfloat16)
    coefficients, tables, choice, basis, across, wave_rows, damping, ends = pl.pallas_call(
        functools.partial(analysis_kernel, held, fields, first),
        out_shape=(
            exchanged,
            jax.ShapeDtypeStruct((pairs + 1, 2 * width, padded), jnp.bfloat16),
            jax.ShapeDtypeStruct((choices * slots, LANES), jnp.bfloat16),
            jax.ShapeDtypeStruct(legendre.shape, jnp.bfloat16),
            jax.ShapeDtypeStruct((held, legendre.shape[2], legendre.shape[1]), jnp.bfloat16),
            jax.ShapeDtypeStruct((held, LANES), jnp.float32),
            jax.ShapeDtypeStruct((held, width, LANES), jnp.float32),
            jax.ShapeDtypeStruct((pairs, LANES), jnp.float32),
        ),
        in_specs=[hbm] * 6,
        out_specs=(vmem,) * 8,
        scratch_shapes=[
            pltpu.SMEM((pairs,), jnp.int32),
            pltpu.SMEM((pairs,), jnp.float32),
            pltpu.VMEM((1, width), jnp.int32),
            pltpu.VMEM((1, stiffness.shape[0]), jnp.float32),
            pltpu.VMEM((pairs * rows, points), jnp.bfloat16),
            pltpu.VMEM(legendre.shape, jnp.bfloat16),
            pltpu.VMEM(legendre.shape, jnp.float32),
            pltpu.VMEM((pairs + 1, points, 2 * LANES), jnp.bfloat16),
            pltpu.SemaphoreType.DMA((5,)),
            pltpu.SemaphoreType.DMA,
        ],
        compiler_params=limits,
        name="analysis",
    )(
        *(
            pltpu.with_memory_space_constraint(array, pltpu.HBM)
            for array in (
                point_counts, weights, waves.reshape(1, width), stiffness.reshape(1, -1), legendre,
                grid.reshape(pairs * rows, points),
            )
        )
    )

    def exchange(array):
        return lax.all_to_all(
            array, "lat", split_axis=0, concat_axis=0, axis_index_groups=groups, tiled=True
        )

    synthesised = pl.pallas_call(
        functools.partial(legendre_kernel, held, fields),
        out_shape=exchanged,
        in_specs=[vmem] * 5,
        out_specs=vmem,
        scratch_shapes=[
            pltpu.VMEM((blocks * 2, slots, LANES), jnp.float32),
            pltpu.VMEM((blocks * 2, slots, LANES), jnp.float32),
        ],
        compiler_params=limits,
        name="legendre",
    )(wave_rows, damping, basis, across, exchange(coefficients))
    result = pl.pallas_call(
        functools.partial(synthesis_kernel, held),
        out_shape=jax.ShapeDtypeStruct((pairs * rows, points), jnp.bfloat16),
        in_specs=[vmem] * 4,
        out_specs=hbm,
        scratch_shapes=[
            pltpu.VMEM((pairs * rows, points), jnp.bfloat16),
            pltpu.SemaphoreType.DMA((pairs,)),
        ],
        compiler_params=limits,
        name="synthesis",
    )(ends, choice, exchange(synthesised), tables)
    return result.reshape(grid.shape)


def fourier_tables(count, wavenumbers, quarter_max):
    quarter = count // 4
    step_angle = TWO_PI / quarter.astype(jnp.float32)
    coarse_count = (quarter_max + FINE_STEPS - 1) // FINE_STEPS
    coarse_pos = FINE_STEPS * jnp.arange(coarse_count, dtype=jnp.int32)
    fine_pos = jnp.arange(FINE_STEPS, dtype=jnp.int32)
    coarse_angle = (coarse_pos[:, None] * wavenumbers[None, :] % quarter).astype(
        jnp.float32
    ) * step_angle
    fine_angle = (fine_pos[:, None] * wavenumbers[None, :] % quarter).astype(
        jnp.float32
    ) * step_angle
    coarse_cos = jnp.cos(coarse_angle)[:, None, :]
    coarse_sin = jnp.sin(coarse_angle)[:, None, :]
    fine_cos = jnp.cos(fine_angle)[None, :, :]
    fine_sin = jnp.sin(fine_angle)[None, :, :]
    full_cos = (coarse_cos * fine_cos - coarse_sin * fine_sin).reshape(
        coarse_count * FINE_STEPS, -1
    )[:quarter_max]
    full_sin = (coarse_sin * fine_cos + coarse_cos * fine_sin).reshape(
        coarse_count * FINE_STEPS, -1
    )[:quarter_max]
    positions = jnp.arange(quarter_max, dtype=jnp.int32)
    inside = (positions < quarter)[:, None]
    cosine = jnp.where(inside, full_cos, 0.0)
    sine = jnp.where(inside, full_sin, 0.0)
    matrix = jnp.concatenate([cosine, sine], axis=1).astype(jnp.bfloat16)
    offsets = jnp.arange(4, dtype=jnp.int32)
    twist = offsets[:, None] * wavenumbers[None, :] % count
    theta = twist.astype(jnp.float32) * (TWO_PI / count.astype(jnp.float32))
    return (matrix, jnp.cos(theta), jnp.sin(theta))


def helmholtz(spectra, wavenumbers, offsets, stiffness_local, width):
    full_shape = spectra.shape
    quartered = spectra.reshape(full_shape[:-2] + (full_shape[-2] // 4, 2, 2, full_shape[-1]))
    parity = (1 - 2 * (offsets % 2)).astype(jnp.float32)
    combined = quartered[..., 0, :] + parity * quartered[..., 1, :]
    degrees = (wavenumbers + offsets).astype(jnp.float32)
    inside_band = offsets < width - wavenumbers
    factor = 1.0 / (
        1.0 + stiffness_local[:, None] * degrees[..., None, :] * (degrees[..., None, :] + 1.0)
    )
    damping = jnp.where(inside_band[..., None, :], factor, 0.0)
    scaled = (combined * damping[..., :, None, :]).astype(jnp.bfloat16)
    flipped = scaled * parity.astype(jnp.bfloat16)
    return jnp.stack([scaled, flipped], axis=-2).reshape(full_shape)


def spectral(received, wavenumbers, basis, stiffness_local):
    width = basis.shape[2]
    spectra = jnp.einsum("jcr,cjl->crl", received, basis, preferred_element_type=jnp.float32)
    offsets = jnp.arange(width, dtype=jnp.int32)
    operand = helmholtz(spectra, wavenumbers[:, None], offsets, stiffness_local, width)
    returned = jnp.einsum("crl,cjl->jcr", operand, basis, preferred_element_type=jnp.float32)
    return returned.astype(jnp.bfloat16)


def on_device_blocked(grid, point_counts, waves, legendre, weights, stiffness):
    pairs, _, fields, points = grid.shape
    quarter_max = points // 4
    width = waves.shape[0]
    held_slots = legendre.shape[0]
    lat_index = lax.axis_index("lat")
    lev_index = lax.axis_index("lev")

    def analyse(pieces):
        latitude, count, weight = pieces
        matrix, twist_cos, twist_sin = fourier_tables(count, waves, quarter_max)
        values = latitude.reshape(2, fields, quarter_max, 4)
        partial_value = jnp.einsum(
            "hfab,at->hfbt", values, matrix, preferred_element_type=jnp.float32
        )
        cos_part = partial_value[..., :width]
        sin_part = partial_value[..., width:]
        real = jnp.sum(twist_cos * cos_part - twist_sin * sin_part, axis=2)
        imag = -jnp.sum(twist_sin * cos_part + twist_cos * sin_part, axis=2)
        factor = jnp.where(2 * waves < count, weight / count.astype(jnp.float32), 0.0)
        stacked = jnp.stack([real * factor, imag * factor], axis=0)
        packed = jnp.transpose(stacked, (3, 2, 0, 1)).reshape(width, 4 * fields)
        return (packed.astype(jnp.bfloat16), matrix, twist_cos, twist_sin)

    coefficients, matrices, twist_cos, twist_sin = lax.map(analyse, (grid, point_counts, weights))
    received = lax.all_to_all(coefficients, "lat", split_axis=1, concat_axis=0, tiled=True)
    owned = lax.dynamic_slice_in_dim(waves, lat_index * held_slots, held_slots)
    own_stiffness = lax.dynamic_slice_in_dim(stiffness, lev_index * fields, fields)
    synthesised = spectral(received, owned, legendre, own_stiffness)
    returned = lax.all_to_all(synthesised, "lat", split_axis=0, concat_axis=1, tiled=True)

    def synthesise(pieces):
        packed, matrix, turn_cos, turn_sin, count = pieces
        values = packed.astype(jnp.float32).reshape(width, fields, 2, 2)
        real = values[:, :, 0, :]
        imag = values[:, :, 1, :]
        factor = jnp.where(2 * waves < count, jnp.where(waves == 0, 1.0, 2.0), 0.0)[:, None, None]
        cosines = turn_cos[:, :, None, None]
        sines = turn_sin[:, :, None, None]
        turned_real = factor * (real * cosines - imag * sines)
        turned_imag = factor * (real * sines + imag * cosines)
        operand = jnp.concatenate([turned_real, -turned_imag], axis=1)
        upper = operand.astype(jnp.bfloat16)
        lower = (operand - upper.astype(jnp.float32)).astype(jnp.bfloat16)
        result = jnp.einsum("bmfh,am->hfab", upper, matrix, preferred_element_type=jnp.float32)
        result = result + jnp.einsum(
            "bmfh,am->hfab", lower, matrix, preferred_element_type=jnp.float32
        )
        return result.reshape(2, fields, points).astype(jnp.bfloat16)

    return lax.map(synthesise, (returned, matrices, twist_cos, twist_sin, point_counts))


def fits_on_chip(mesh, grid, waves, stiffness):
    owners = mesh.shape["lat"]
    pairs, fields = grid.shape[0] // owners, grid.shape[2] // mesh.shape["lev"]
    width, points = waves.shape[0], grid.shape[3]
    held = width // owners
    lanes = 2 * pairs * fields
    rest = lanes % LANES
    return (
        width % owners == 0
        and width % (2 * ROWS) == 0
        and width <= LANES
        and 4 * (pairs + 1) * LANES * points <= TABLE_BUDGET
        and points <= ROWS * LANES
        and points % (2 * ROWS) == 0
        and held <= ROWS
        and lanes >= LANES
        and (rest == 0 or rest % (2 * ROWS) == 0)
        and (rest == 0 or held <= (ROWS - held) * (LANES // rest))
        and 4 * fields <= LANES
        and fields % ROWS == 0
        and owners % (2 * ROWS) == 0
        and stiffness.shape[0] <= LANES
    )


def solution(mesh):
    in_specs = (P("lat", None, "lev", None), P("lat"), P(), P("lat", None, None), P("lat"), P())
    out_specs = P("lat", None, "lev", None)

    def program(grid, point_counts, waves, legendre, weights, stiffness):
        fits = fits_on_chip(mesh, grid, waves, stiffness)
        body = functools.partial(on_device, mesh) if fits else on_device_blocked
        return jax.shard_map(
            body, mesh=mesh, in_specs=in_specs, out_specs=out_specs, check_vma=False
        )(grid, point_counts, waves, legendre, weights, stiffness)

    return program
```
